32 devices in a mesh: screen: 2 (over x), pool: 8 (over z, y), dap: 2 (over core).
Axes of the slice: x: 2, y: 2, z: 4, core: 2. Of those that a mesh axis runs over, the one named last changes fastest.
Arguments:
- pair_rep: bfloat16 [352, 16, 16, 128], P(('screen', 'pool'), 'dap'), parts along dimension 0, may hold values from -6 to 6
- alignment: bfloat16 [352, 16, 16, 256], P(('screen', 'pool'), None, 'dap'), parts along dimension 0, may hold values from -6 to 6
- lengths: int32 [352], P('screen'), parts along dimension 0, may hold values from 8 to 16, as said below
- chain_breaks: int32 [352], P('screen'), parts along dimension 0, may hold values from 1 to 15, as said below
- shifts: int32 [44], P('screen'), parts along dimension 0, may hold values from 0 to 7, as said below
- alignment_proj: bfloat16 [256, 64], replicated, may hold values from -0.375 to 0.375
- outer_proj: bfloat16 [1024, 128], replicated, may hold values from -0.75 to 0.75
- chain_bias: bfloat16 [2, 128], replicated, may hold values from -4 to 4
- outgoing_ab: bfloat16 [128, 512], replicated, may hold values from -0.5 to 0.5
- outgoing_gate: bfloat16 [128, 128], replicated, may hold values from -0.5 to 0.5
- outgoing_proj: bfloat16 [128, 128], replicated, may hold values from -0.5 to 0.5
- incoming_ab: bfloat16 [128, 512], replicated, may hold values from -0.5 to 0.5
- incoming_gate: bfloat16 [128, 128], replicated, may hold values from -0.5 to 0.5
- incoming_proj: bfloat16 [128, 128], replicated, may hold values from -0.5 to 0.5
Outputs:
- pair_out: bfloat16 [352, 16, 16, 128], P(('screen', 'pool'), 'dap'), parts along dimension 0
The draws below stay inside these ranges and needn't reach their ends.
There are 2 independent parts, one for each index of `screen`. The reference program is written for one: setup_inputs(seed, part) draws one part's arguments, and reference() takes and returns one part's arrays. A program takes and returns all parts, laid end to end along the dimension named above; an argument that names none is the same for every part. Nothing has to cross between parts.
Inputs may be any that keep to these rules, and one draw needn't show every extreme that they name: The complex in slot s of group g goes to group (g + shifts[s]) mod 8 and keeps slot s. No value occurs more than 6 times in shifts, and one value occurs exactly 6 times. `lengths`: at least one complex has exactly 16 residues. The bait chain is residues 0 to chain_breaks - 1, the candidate chain the rest up to the complex's length.
All inputs are finite; a program needn't handle non-finite values.
Results may differ from the reference program's by a relative error of at most 0.0066.
Values may be sent and summed in bfloat16 or wider, within the bound.
No kernel may reach another device: no remote copies, remote signals or barrier semaphores. Data moves between devices by JAX's collectives and lax.ppermute only.
A program may use at most 128 MiB of HBM per device.

```python
import jax
import jax.numpy as jnp
from jax import lax

CZ = 128
CM = 256
CO = 32
CT = 128
NS = 16
LMAX = 16
SLOTS = 22
GROUPS = 8
COMPLEXES = 176
CAP = 6


def residue_layout(key):
    base = jax.random.fold_in(key, 21)
    first_key, second_key, third_key = jax.random.split(base, 3)
    places = jnp.arange(COMPLEXES, dtype=jnp.int32)
    lengths = jax.random.randint(first_key, (COMPLEXES,), LMAX // 2, LMAX + 1, dtype=jnp.int32)
    longest = jax.random.randint(second_key, (), 0, COMPLEXES, dtype=jnp.int32)
    lengths = jnp.where(places == longest, LMAX, lengths).astype(jnp.int32)
    breaks = 1 + jax.random.randint(third_key, (COMPLEXES,), 0, lengths - 1, dtype=jnp.int32)
    return (lengths, breaks.astype(jnp.int32))


def draw_lengths(key, part):
    return residue_layout(key)[0]


def draw_chain_breaks(key, part):
    return residue_layout(key)[1]


def draw_shifts(key, part):
    favour_key = jax.random.fold_in(key, 11)
    score_key = jax.random.fold_in(key, 12)
    order_key = jax.random.fold_in(key, 13)
    entries = GROUPS * CAP
    offsets = jnp.repeat(jnp.arange(GROUPS, dtype=jnp.int32), CAP)
    favoured = jax.random.randint(favour_key, (), 0, GROUPS, dtype=jnp.int32)
    counter = jnp.arange(entries, dtype=jnp.int32)
    scores = jax.random.randint(score_key, (entries,), 0, 1 << 20, dtype=jnp.int32) * entries + counter
    scores = jnp.where(offsets == favoured, -1 - counter, scores)
    ordering = jnp.argsort(scores)
    chosen = offsets[ordering][:SLOTS]
    return jax.random.permutation(order_key, chosen).astype(jnp.int32)


def level_of(key, shape, pieces, least, high):
    def one(dim, shards_of):
        heights = jax.random.uniform(jax.random.fold_in(jax.random.fold_in(key, 6), dim), (shards_of,), jnp.float32, least / len(pieces), high / len(pieces))
        return jnp.repeat(jnp.exp(heights), shape[dim] // shards_of).reshape((-1,) + (1,) * (len(shape) - dim - 1))

    loudness = one(*pieces[0])
    for cut in pieces[1:]:
        loudness = loudness * one(*cut)
    return loudness


def centred(own_key, extent, scale, bound, shards=(), held_as=jnp.bfloat16):
    array = jax.random.normal(own_key, extent, jnp.float32) * scale
    if len(shards) > 0:
        array = level_of(own_key, extent, shards, -0.22, 0.18) * array
    return jnp.clip(array, min=-bound, max=bound).astype(held_as)


def setup_inputs(seed: int = 0, part: int = 0) -> dict:
    arg_keys = jax.random.split(jax.random.key(seed), 15)
    part_splits = jax.random.split(jax.random.fold_in(arg_keys[14], part), 15)
    return {
        "pair_rep": centred(part_splits[0], (COMPLEXES, LMAX, LMAX, CZ), 1.0, 6.0, ((0, 8), (1, 2))),
        "alignment": centred(part_splits[1], (COMPLEXES, NS, LMAX, CM), 1.0, 6.0, ((0, 8), (2, 2))),
        "lengths": draw_lengths(jax.random.fold_in(jax.random.fold_in(arg_keys[14], part), 71), part),
        "chain_breaks": draw_chain_breaks(jax.random.fold_in(jax.random.fold_in(arg_keys[14], part), 71), part),
        "shifts": draw_shifts(jax.random.fold_in(jax.random.fold_in(arg_keys[14], part), 71), part),
        "alignment_proj": centred(arg_keys[5], (CM, 2 * CO), CM ** -0.5, 0.375),
        "outer_proj": centred(arg_keys[6], (CO * CO, CZ), (CO * CO // NS) ** -0.5, 0.75),
        "chain_bias": centred(arg_keys[7], (2, CZ), 1.0, 4.0),
        "outgoing_ab": centred(arg_keys[8], (CZ, 4 * CT), CZ ** -0.5, 0.5),
        "outgoing_gate": centred(arg_keys[9], (CZ, CZ), CZ ** -0.5, 0.5),
        "outgoing_proj": centred(arg_keys[10], (CT, CZ), CT ** -0.5, 0.5),
        "incoming_ab": centred(arg_keys[11], (CZ, 4 * CT), CZ ** -0.5, 0.5),
        "incoming_gate": centred(arg_keys[12], (CZ, CZ), CZ ** -0.5, 0.5),
        "incoming_proj": centred(arg_keys[13], (CT, CZ), CT ** -0.5, 0.5),
    }


EPSILON = 1e-05

def layer_normalize(values):
    values = values.astype(jnp.float32)
    center = lax.optimization_barrier(jnp.mean(values, axis=-1, keepdims=True))
    spread = lax.optimization_barrier(jnp.mean(jnp.square(values - center), axis=-1, keepdims=True))
    return (values - center) * lax.rsqrt(spread + EPSILON)

def triangle(stream, pair_mask, weight_ab, weight_gate, weight_proj):
    normalized_rows = layer_normalize(stream).astype(jnp.bfloat16)
    project = jnp.dot(normalized_rows, weight_ab, preferred_element_type=jnp.float32)
    hidden_width = weight_proj.shape[0]
    left_side = jax.nn.sigmoid(project[..., hidden_width:2 * hidden_width]) * project[..., :hidden_width]
    left_side = (left_side * pair_mask[..., None]).astype(jnp.bfloat16)
    right_side = jax.nn.sigmoid(project[..., 3 * hidden_width:]) * project[..., 2 * hidden_width:3 * hidden_width]
    right_side = (right_side * pair_mask[..., None]).astype(jnp.bfloat16)
    product = jnp.einsum('ikc,jkc->ijc', left_side.astype(jnp.float32), right_side.astype(jnp.float32))
    normed_product = layer_normalize(product).astype(jnp.bfloat16)
    gating = jax.nn.sigmoid(jnp.dot(normalized_rows, weight_gate, preferred_element_type=jnp.float32))
    return gating * jnp.dot(normed_product, weight_proj, preferred_element_type=jnp.float32)

def single_complex(pairwise_block, alignment_block, sequence_length, chain_stop_index, weight_params):
    alignment_proj, outer_proj, chain_bias, outgoing_ab, outgoing_gate, outgoing_proj, incoming_ab, incoming_gate, incoming_proj = weight_params
    places = jnp.arange(LMAX, dtype=jnp.int32)
    residue_mask = (places < sequence_length).astype(jnp.float32)
    pair_mask = residue_mask[:, None] * residue_mask[None, :]
    normalized_rows = layer_normalize(alignment_block).astype(jnp.bfloat16)
    project = jnp.dot(normalized_rows, alignment_proj, preferred_element_type=jnp.float32)
    project = (project * residue_mask[None, :, None]).astype(jnp.bfloat16)
    inner_width = alignment_proj.shape[1] // 2
    left_side = project[..., :inner_width].astype(jnp.float32)
    right_side = project[..., inner_width:].astype(jnp.float32)
    products = jnp.einsum('sic,sjd->ijcd', left_side, right_side) / NS
    products = products.reshape(LMAX, LMAX, inner_width * inner_width).astype(jnp.bfloat16)
    update = jnp.dot(products, outer_proj, preferred_element_type=jnp.float32)
    first_chain = places < chain_stop_index
    same_chain = first_chain[:, None] == first_chain[None, :]
    chain_term = jnp.where(same_chain[..., None], chain_bias[0].astype(jnp.float32), chain_bias[1].astype(jnp.float32))
    stream = pairwise_block.astype(jnp.float32) + update + chain_term
    stream = (stream + triangle(stream, pair_mask, outgoing_ab, outgoing_gate, outgoing_proj)).astype(jnp.bfloat16)
    flipped = jnp.transpose(stream, (1, 0, 2)).astype(jnp.float32)
    flipped = flipped + triangle(flipped, pair_mask, incoming_ab, incoming_gate, incoming_proj)
    flipped = (flipped * pair_mask[..., None]).astype(jnp.bfloat16)
    return jnp.transpose(flipped, (1, 0, 2))

def reference(pair_rep, alignment, lengths, chain_breaks, shifts, alignment_proj, outer_proj, chain_bias, outgoing_ab, outgoing_gate, outgoing_proj, incoming_ab, incoming_gate, incoming_proj):
    weight_params = (alignment_proj, outer_proj, chain_bias, outgoing_ab, outgoing_gate, outgoing_proj, incoming_ab, incoming_gate, incoming_proj)

    def build(target):
        slot_number = (target % SLOTS).astype(jnp.int32)
        dest_group = (target // SLOTS).astype(jnp.int32)
        home_index = ((dest_group - shifts[slot_number]) % GROUPS * SLOTS + slot_number).astype(jnp.int32)
        return single_complex(pair_rep[home_index], alignment[home_index], lengths[home_index], chain_breaks[home_index], weight_params)
    return lax.map(build, jnp.arange(COMPLEXES, dtype=jnp.int32))
```

```python
import functools

import jax
import jax.numpy as jnp
from jax import lax
from jax.experimental import pallas as pl
from jax.experimental.pallas import tpu as pltpu
from jax.sharding import PartitionSpec as P

EPSILON = 1e-05
F32 = jnp.float32
BF16 = jnp.bfloat16


def dot(left, right):
    return jnp.dot(left, right, preferred_element_type=F32)


def sigmoid(values):
    return 0.5 * jnp.tanh(0.5 * values) + 0.5


def normalize(values):
    center = jnp.mean(values, axis=-1, keepdims=True)
    values = values - center
    spread = jnp.mean(values * values, axis=-1, keepdims=True)
    return (values * lax.rsqrt(spread + EPSILON)).astype(BF16)


def update_kernel(
    half_ref,
    lengths_ref,
    breaks_ref,
    own_pair,
    other_pair,
    own_alignment,
    other_alignment,
    w_project,
    w_spread,
    w_outer,
    bias,
    out_w,
    out_proj,
    in_w,
    in_proj,
    keep_ref,
    send_ref,
    side,
    rights,
    spread,
    stacked,
    outer,
    stream,
    first,
    second,
):
    count, rows, full, width = own_pair.shape
    depth = own_alignment.shape[1]
    pairs = full * full
    inner = rights.shape[-1] // depth
    half = half_ref[0]

    lane = lax.broadcasted_iota(jnp.int32, (1, 128), 1)
    groups = [(lane // inner) == q for q in range(4)]

    def project(step, carry):
        length = lengths_ref[step]
        for place, ref in ((half, own_alignment), (1 - half, other_alignment)):
            values = ref[step].astype(F32).reshape(depth * rows, ref.shape[-1])
            values = dot(normalize(values), w_project[...])
            residue = (
                lax.broadcasted_iota(jnp.int32, (depth, rows, 1), 1) + place * rows
            ).reshape(depth * rows, 1)
            values = jnp.where(residue < length, values, 0.0).astype(BF16).astype(F32)
            left = values[:, :128] * (1.0 / depth)
            side[step, place] = left
            right = values[:, 128:].reshape(depth, rows, 128)
            for group in range(depth // 4):
                piece = right[4 * group]
                for q in range(1, 4):
                    piece = jnp.where(groups[q], right[4 * group + q], piece)
                rights[step, pl.ds(pl.multiple_of(place * rows, rows), rows), 128 * group : 128 * group + 128] = piece
        return carry

    lax.fori_loop(0, count, project, 0)

    flat = rights[...].reshape(count * full, rights.shape[-1]).astype(BF16)
    spread[...] = dot(flat, w_spread[...]).astype(BF16).reshape(spread.shape)
    stacked[...] = jnp.zeros_like(stacked)

    row = lax.broadcasted_iota(jnp.int32, (pairs, 1), 0)
    row_i = row // full
    row_j = row % full

    def complex_step(step, carry):
        length = lengths_ref[step]
        stop = breaks_ref[step]
        for i in range(full):
            left = side[step, i // rows, pl.ds(i % rows, depth, stride=rows), :]
            for q in range(4):
                stacked[16 * q : 16 * q + 16, 128 * i : 128 * i + 128] = jnp.where(
                    groups[q], left, 0.0
                ).astype(BF16)
        right = spread[step]
        right = jnp.concatenate([right[:, 128 * g : 128 * g + 128] for g in range(8)], axis=0)
        for i in range(0, full, 2):
            product = dot(right, stacked[:, 128 * i : 128 * i + 256]).astype(BF16)
            for g in range(8):
                outer[16 * i : 16 * i + 16, 128 * g : 128 * g + 128] = product[16 * g : 16 * g + 16, :128]
                outer[16 * i + 16 : 16 * i + 32, 128 * g : 128 * g + 128] = product[16 * g : 16 * g + 16, 128:]
        stream[pl.ds(pl.multiple_of(half * rows * full, rows * full), rows * full), :] = (
            own_pair[step].astype(F32).reshape(rows * full, width)
        )
        stream[pl.ds(pl.multiple_of((1 - half) * rows * full, rows * full), rows * full), :] = (
            other_pair[step].astype(F32).reshape(rows * full, width)
        )
        same = (row_i < stop) == (row_j < stop)
        inside = ((row_i < length) & (row_j < length)).astype(F32)
        z1 = stream[...] + dot(outer[...], w_outer[...])
        z1 = z1 + jnp.where(same, bias[0:1].astype(F32), bias[1:2].astype(F32))

        def sides(values, weight):
            x = normalize(values)
            projected = dot(x, weight[...])
            a = sigmoid(projected[:, 128:256]) * projected[:, :128] * inside
            b = sigmoid(projected[:, 384:512]) * projected[:, 256:384] * inside
            gate = sigmoid(projected[:, 512:])
            return a.astype(BF16).astype(F32), b.astype(BF16).astype(F32), gate

        def contract(rows_of, columns):
            parts = []
            for i in range(full):
                total = None
                for k in range(full):
                    term = rows_of(i, k) * columns[k]
                    total = term if total is None else total + term
                parts.append(total)
            return jnp.concatenate(parts, axis=0)

        a, b, gate = sides(z1, out_w)
        first[...] = a
        second[...] = b
        columns = [second[pl.ds(k, full, stride=full), :] for k in range(full)]
        t = contract(lambda i, k: first[pl.ds(full * i + k, 1), :], columns)
        z2 = (z1 + gate * dot(normalize(t), out_proj[...])).astype(BF16).astype(F32)
        a, b, gate = sides(z2, in_w)
        second[...] = b
        columns = [a[full * k : full * k + full] for k in range(full)]
        t = contract(lambda i, k: second[pl.ds(full * k + i, 1), :], columns)
        stream[...] = (z2 + gate * dot(normalize(t), in_proj[...])) * inside
        keep_ref[step] = (
            stream[pl.ds(pl.multiple_of(half * rows * full, rows * full), rows * full), :]
            .reshape(rows, full, width)
            .astype(BF16)
        )
        send_ref[step] = (
            stream[pl.ds(pl.multiple_of((1 - half) * rows * full, rows * full), rows * full), :]
            .reshape(rows, full, width)
            .astype(BF16)
        )
        return carry

    lax.fori_loop(0, count, complex_step, 0)


def update(half, lengths, breaks, own_pair, other_pair, own_alignment, other_alignment, weights):
    (
        alignment_proj,
        outer_proj,
        chain_bias,
        outgoing_ab,
        outgoing_gate,
        outgoing_proj,
        incoming_ab,
        incoming_gate,
        incoming_proj,
    ) = weights
    count, rows, full, width = own_pair.shape
    depth = own_alignment.shape[1]
    inner = alignment_proj.shape[1] // 2
    pieces = 128 // inner
    sets = inner // pieces
    w_project = jnp.concatenate(
        [alignment_proj[:, :inner]] * pieces + [alignment_proj[:, inner:]] * pieces, axis=1
    )
    source = lax.broadcasted_iota(jnp.int32, (depth * inner, sets * 128), 0)
    target = lax.broadcasted_iota(jnp.int32, (depth * inner, sets * 128), 1)
    r, c2 = source // inner, source % inner
    w_spread = (target == (c2 // pieces) * 128 + (c2 % pieces) * depth + r).astype(BF16)
    w_outer = (
        outer_proj.reshape(inner, inner, width).transpose(1, 0, 2).reshape(inner * inner, width)
    )
    out_w = jnp.concatenate([outgoing_ab, outgoing_gate], axis=1)
    in_w = jnp.concatenate([incoming_ab, incoming_gate], axis=1)
    smem = pl.BlockSpec(memory_space=pltpu.SMEM)
    vmem = pl.BlockSpec(memory_space=pltpu.VMEM)
    shape = jax.ShapeDtypeStruct(own_pair.shape, BF16)
    pairs = full * full
    return pl.pallas_call(
        update_kernel,
        out_shape=(shape, shape),
        in_specs=[smem] * 3 + [vmem] * 12,
        out_specs=(vmem, vmem),
        scratch_shapes=[
            pltpu.VMEM((count, 2, depth * rows, 128), F32),
            pltpu.VMEM((count, full, depth * inner), F32),
            pltpu.VMEM((count, full, sets * 128), BF16),
            pltpu.VMEM((128, full * 128), BF16),
            pltpu.VMEM((pairs, inner * inner), BF16),
            pltpu.VMEM((pairs, width), F32),
            pltpu.VMEM((pairs, width), F32),
            pltpu.VMEM((pairs, width), F32),
        ],
        name="pair_update",
    )(
        half,
        lengths,
        breaks,
        own_pair,
        other_pair,
        own_alignment,
        other_alignment,
        w_project,
        w_spread,
        w_outer,
        chain_bias,
        out_w,
        outgoing_proj,
        in_w,
        incoming_proj,
    )


def pack_slots(blocks, positions, buffer_slots):
    slot_index = jnp.arange(positions.shape[0], dtype=jnp.int32)
    matches = positions[None, :] == jnp.arange(buffer_slots, dtype=jnp.int32)[:, None]
    source = jnp.sum(jnp.where(matches, slot_index[None, :], 0), axis=1)
    return jnp.take(blocks, source, axis=0)


def body(pair_rep, alignment, lengths, chain_breaks, shifts, *weights):
    group_count = lax.axis_size("pool")
    my_group = lax.axis_index("pool")
    half = lax.axis_index("dap")
    slot_count = pair_rep.shape[0]
    count = slot_count // 2
    capacity = max(2, (2 * slot_count + group_count - 1) // group_count)
    buffer_slots = group_count * capacity
    swap = [(0, 1), (1, 0)]
    mine = half * count
    theirs = (1 - half) * count
    other_pair = lax.ppermute(lax.dynamic_slice_in_dim(pair_rep, theirs, count), "dap", swap)
    other_alignment = lax.ppermute(lax.dynamic_slice_in_dim(alignment, theirs, count), "dap", swap)
    home = my_group * slot_count + mine
    keep, send = update(
        half.reshape(1).astype(jnp.int32),
        lax.dynamic_slice_in_dim(lengths, home, count),
        lax.dynamic_slice_in_dim(chain_breaks, home, count),
        lax.dynamic_slice_in_dim(pair_rep, mine, count),
        other_pair,
        lax.dynamic_slice_in_dim(alignment, mine, count),
        other_alignment,
        weights,
    )
    received = lax.ppermute(send, "dap", swap)
    result = jnp.concatenate([keep, received], axis=0)

    slot_index = jnp.arange(slot_count, dtype=jnp.int32)
    earlier = (shifts[None, :] == shifts[:, None]) & (slot_index[None, :] < slot_index[:, None])
    slot_rank = jnp.sum(earlier.astype(jnp.int32), axis=1)
    send_at = (my_group + shifts) % group_count * capacity + slot_rank
    send_at = jnp.where(half == 0, send_at, jnp.roll(send_at, count))
    receive_position = (my_group - shifts) % group_count * capacity + slot_rank
    outgoing = pack_slots(result, send_at, buffer_slots)
    received_blocks = lax.all_to_all(outgoing, "pool", split_axis=0, concat_axis=0, tiled=True)
    return jnp.take(received_blocks, receive_position, axis=0)


def solution(mesh):
    return jax.shard_map(
        body,
        mesh=mesh,
        in_specs=(
            P(("screen", "pool"), "dap", None, None),
            P(("screen", "pool"), None, "dap", None),
            P("screen"),
            P("screen"),
            P("screen"),
        )
        + (P(),) * 9,
        out_specs=P(("screen", "pool"), "dap", None, None),
        check_vma=False,
    )
```

```python
import functools

import jax
import jax.numpy as jnp
import numpy as np
from jax import lax
from jax.experimental import pallas as pl
from jax.experimental.pallas import tpu as pltpu
from jax.sharding import PartitionSpec as P

EPSILON = 1e-05
F32 = jnp.float32
BF16 = jnp.bfloat16
LANES = 128


def dot(left, right):
    return jnp.dot(left, right, preferred_element_type=F32)


def normalize(values, scale):
    width = values.shape[-1]
    values = values - jnp.sum(values, axis=-1, keepdims=True) * (1.0 / width)
    spread = jnp.sum(values * values, axis=-1, keepdims=True)
    return (values * (lax.rsqrt(spread + width * EPSILON) * scale)).astype(BF16)


def lane_groups(inner):
    group = lax.broadcasted_iota(jnp.int32, (1, LANES), 1) // inner
    return [group == q for q in range(LANES // inner)]


def project_kernel(send, place_ref, lengths_ref, *refs):
    if send:
        alignment, pair, w_align, w_spread, out_ref, pair_out, rows_in, side, rights, sems = refs
    else:
        alignment, w_align, w_spread, out_ref, rows_in, side, rights, sems = refs
    count, depth, rows, width = rows_in.shape
    inner = rights.shape[-1] // depth
    pieces = LANES // inner
    half = place_ref[0]
    start = place_ref[1] if send else place_ref[2]
    home = place_ref[3]
    copy = pltpu.make_async_copy(alignment.at[pl.ds(start, count)], rows_in, sems.at[0])
    copy.start()
    if send:
        pair_copy = pltpu.make_async_copy(pair.at[pl.ds(start, count)], pair_out, sems.at[1])
        pair_copy.start()
    groups = lane_groups(inner)
    source = lax.broadcasted_iota(jnp.int32, (2 * inner, 2 * LANES), 0)
    target = lax.broadcasted_iota(jnp.int32, (2 * inner, 2 * LANES), 1)
    repeat = (source == (target // LANES) * inner + target % inner).astype(BF16)
    w_project = dot(w_align[...], repeat).astype(BF16)
    copy.wait()

    def step(index, carry):
        length = lengths_ref[home + start + index]
        values = rows_in[index].astype(F32).reshape(depth * rows, width)
        values = dot(normalize(values, width**0.5), w_project)
        residue = lax.broadcasted_iota(jnp.int32, (rows, 1), 0) + half * rows
        mask = jnp.where(residue < length, 1.0, 0.0)
        values = values.reshape(depth, rows, 2 * LANES) * mask
        side[...] = values[:, :, :LANES].reshape(depth * rows, LANES) * (1.0 / depth)
        tiles = []
        for tile in range(rows // pieces):
            piece = side[pl.ds(tile * pieces, depth, stride=rows), :]
            for q in range(1, pieces):
                piece = jnp.where(groups[q], side[pl.ds(tile * pieces + q, depth, stride=rows), :], piece)
            tiles.append(piece)
        out_ref[index, :depth] = jnp.concatenate(tiles, axis=1).astype(BF16)
        for tile in range(depth // pieces):
            piece = values[tile * pieces, :, LANES:]
            for q in range(1, pieces):
                piece = jnp.where(groups[q], values[tile * pieces + q, :, LANES:], piece)
            rights[index, :, LANES * tile : LANES * tile + LANES] = piece
        return carry

    lax.fori_loop(0, count, step, 0, unroll=False)
    flat = rights[...].reshape(count * rows, depth * inner).astype(BF16)
    spread = dot(flat, w_spread[...]).reshape(count, rows, depth * inner)
    parts = out_ref.shape[-1]
    for part in range(depth * inner // parts):
        out_ref[:, depth + part * rows : depth + part * rows + rows] = spread[
            :, :, part * parts : part * parts + parts
        ].astype(BF16)
    if send:
        pair_copy.wait()


def project(send, place, lengths, alignment, pair, w_align, w_spread):
    slots, depth, rows, width = alignment.shape
    count = slots // 2
    inner = w_align.shape[1] // 2
    smem = pl.BlockSpec(memory_space=pltpu.SMEM)
    vmem = pl.BlockSpec(memory_space=pltpu.VMEM)
    anywhere = pl.BlockSpec(memory_space=pl.ANY)
    out = jax.ShapeDtypeStruct((count, 2 * depth, rows * inner), BF16)
    pair_out = jax.ShapeDtypeStruct((count,) + pair.shape[1:], BF16)
    return pl.pallas_call(
        functools.partial(project_kernel, send),
        out_shape=(out, pair_out) if send else out,
        in_specs=[smem, smem, anywhere] + [anywhere] * send + [vmem, vmem],
        out_specs=(vmem, vmem) if send else vmem,
        scratch_shapes=[
            pltpu.VMEM((count, depth, rows, width), BF16),
            pltpu.VMEM((depth * rows, LANES), F32),
            pltpu.VMEM((count, rows, depth * inner), F32),
            pltpu.SemaphoreType.DMA((2,)),
        ],
        cost_estimate=pl.CostEstimate(flops=10**9, bytes_accessed=2 * 10**6, transcendentals=0),
        name="project_send" if send else "project_own",
    )(*((place, lengths, alignment) + ((pair,) if send else ()) + (w_align, w_spread)))


def update_kernel(
    place_ref,
    lengths_ref,
    breaks_ref,
    own_sides,
    other_sides,
    pair,
    other_pair,
    w_outer,
    bias,
    out_ab,
    out_gate,
    out_proj,
    in_ab,
    in_gate,
    in_proj,
    keep_ref,
    send_ref,
    own_pair,
    stacked,
    outer,
    updates,
    first,
    second,
    sem,
):
    count, rows, full, width = own_pair.shape
    depth = own_sides.shape[1] // 2
    inner = own_sides.shape[2] // rows
    pieces = LANES // inner
    sets = inner // pieces
    hidden = out_proj.shape[0]
    half = place_ref[0]
    start = place_ref[2]
    home = place_ref[3] + start
    copy = pltpu.make_async_copy(pair.at[pl.ds(start, count)], own_pair, sem.at[0])
    copy.start()
    low_is_own = half == 0
    groups = lane_groups(inner)
    zero = jnp.zeros((), BF16)
    stacked[...] = jnp.zeros_like(stacked)
    place_j = lax.broadcasted_iota(jnp.int32, (full, 1), 0)

    def outer_update(step):
        own, other = own_sides[step], other_sides[step]
        low = jnp.where(low_is_own, own, other)
        high = jnp.where(low_is_own, other, own)
        for tile in range(full // pieces):
            source = low if tile < rows // pieces else high
            at = tile % (rows // pieces) * LANES
            left = source[:depth, at : at + LANES]
            turned = [left] + [pltpu.roll(left, inner * turn, 1) for turn in range(1, pieces)]
            for p in range(pieces):
                column = (tile * pieces + p) * LANES
                for q in range(pieces):
                    stacked[depth * q : depth * q + depth, column : column + LANES] = jnp.where(
                        groups[q], turned[(q - p) % pieces], zero
                    )
        lanes = own_sides.shape[2]
        right = jnp.concatenate(
            [
                jnp.concatenate([low[depth + rows * part : depth + rows * part + rows] for part in range(depth // rows)], axis=1),
                jnp.concatenate([high[depth + rows * part : depth + rows * part + rows] for part in range(depth // rows)], axis=1),
            ],
            axis=0,
        )
        per = LANES // (pieces * depth)
        tiles = []
        for c2 in range(sets):
            tile = right[:, c2 // per * LANES : c2 // per * LANES + LANES]
            turn = c2 % per * pieces * depth
            tiles.append(pltpu.roll(tile, LANES - turn, 1) if turn else tile)
        right = jnp.concatenate(tiles, axis=0)
        for i in range(0, full, 2):
            product = dot(right, stacked[:, LANES * i : LANES * i + 2 * LANES]).astype(BF16)
            for k in range(2):
                for g in range(sets):
                    outer[full * (i + k) : full * (i + k) + full, LANES * g : LANES * g + LANES] = product[
                        full * g : full * g + full, LANES * k : LANES * k + LANES
                    ]
        updates[...] = dot(outer[...], w_outer[...])

    def finish(step):
        length = lengths_ref[home + step]
        stop = breaks_ref[home + step]
        own, other = own_pair[step], other_pair[step]
        low = jnp.where(low_is_own, own, other).reshape(rows * full, width)
        high = jnp.where(low_is_own, other, own).reshape(rows * full, width)
        within, across = bias[0:1].astype(F32), bias[1:2].astype(F32)
        head = place_j < stop
        terms = (jnp.where(head, within, across), jnp.where(head, across, within))
        chain = jnp.concatenate([jnp.where(i < stop, terms[0], terms[1]) for i in range(full)], axis=0)
        column = jnp.where(place_j < length, 1.0, 0.0)
        inside = jnp.concatenate([jnp.where(i < length, column, 0.0) for i in range(full)], axis=0)
        z1 = jnp.concatenate([low, high], axis=0).astype(F32) + updates[...] + chain
        unit = 0.5 * width**0.5
        within_unit = inside * unit

        def sides(values, w_ab, w_gate):
            x = normalize(values, within_unit)
            projected = dot(x, w_ab[...])
            a = (jnp.tanh(projected[:, hidden : 2 * hidden]) + 1.0) * projected[:, :hidden]
            b = (jnp.tanh(projected[:, 3 * hidden :]) + 1.0) * projected[:, 2 * hidden : 3 * hidden]
            gate = jnp.tanh(dot(x, w_gate[...])) + 1.0
            return a, b, gate

        def contract(row_of, columns):
            parts = []
            for i in range(full):
                terms = [row_of(i, k) * columns[k] for k in range(full)]
                while len(terms) > 1:
                    terms = [terms[n] + terms[n + 1] for n in range(0, len(terms), 2)]
                parts.append(terms[0])
            return jnp.concatenate(parts, axis=0)

        a, b, gate = sides(z1, out_ab, out_gate)
        first[...] = a
        second[...] = b
        columns = [second[pl.ds(k, full, stride=full), :] for k in range(full)]
        t = contract(lambda i, k: first[pl.ds(full * i + k, 1), :], columns)
        z2 = (z1 + gate * dot(normalize(t, unit), out_proj[...])).astype(BF16).astype(F32)
        a, b, gate = sides(z2, in_ab, in_gate)
        second[...] = b
        columns = [a[full * k : full * k + full] for k in range(full)]
        t = contract(lambda i, k: second[pl.ds(full * k + i, 1), :], columns)
        y3 = ((z2 + gate * dot(normalize(t, unit), in_proj[...])) * inside).astype(BF16)
        low = y3[: rows * full].reshape(rows, full, width)
        high = y3[rows * full :].reshape(rows, full, width)
        keep_ref[step] = jnp.where(low_is_own, low, high)
        send_ref[step] = jnp.where(low_is_own, high, low)

    outer_update(0)
    copy.wait()

    def both(step, carry):
        finish(step)
        outer_update(jnp.minimum(step + 1, count - 1))
        return carry

    lax.fori_loop(0, count, both, 0)


def update(place, lengths, breaks, own_sides, other_sides, pair, other_pair, weights):
    outer_proj, chain_bias, out_ab, out_gate, out_proj, in_ab, in_gate, in_proj = weights
    count, rows, full, width = other_pair.shape
    depth = own_sides.shape[1] // 2
    inner = own_sides.shape[2] // rows
    smem = pl.BlockSpec(memory_space=pltpu.SMEM)
    vmem = pl.BlockSpec(memory_space=pltpu.VMEM)
    anywhere = pl.BlockSpec(memory_space=pl.ANY)
    shape = jax.ShapeDtypeStruct(other_pair.shape, BF16)
    pairs = full * full
    return pl.pallas_call(
        update_kernel,
        out_shape=(shape, shape),
        in_specs=[smem] * 3 + [vmem] * 2 + [anywhere] + [vmem] * 9,
        out_specs=(vmem, vmem),
        scratch_shapes=[
            pltpu.VMEM(other_pair.shape, BF16),
            pltpu.VMEM((LANES, full * LANES), BF16),
            pltpu.VMEM((pairs, inner * inner), BF16),
            pltpu.VMEM((pairs, width), F32),
            pltpu.VMEM((pairs, width), F32),
            pltpu.VMEM((pairs, width), F32),
            pltpu.SemaphoreType.DMA((1,)),
        ],
        name="pair_update",
    )(
        place,
        lengths,
        breaks,
        own_sides,
        other_sides,
        pair,
        other_pair,
        outer_proj,
        chain_bias,
        out_ab,
        out_gate,
        out_proj,
        in_ab,
        in_gate,
        in_proj,
    )


def spread_matrix(depth, inner):
    pieces = LANES // inner
    r, c2 = np.divmod(np.arange(depth * inner), inner)
    matrix = np.zeros((depth * inner, depth * inner), np.float32)
    matrix[np.arange(depth * inner), (c2 // pieces) * pieces * depth + (c2 % pieces) * depth + r] = 1.0
    return jnp.asarray(matrix, BF16)


def pack_slots(blocks, positions, buffer_slots):
    slot_index = jnp.arange(positions.shape[0], dtype=jnp.int32)
    matches = positions[None, :] == jnp.arange(buffer_slots, dtype=jnp.int32)[:, None]
    source = jnp.sum(jnp.where(matches, slot_index[None, :], 0), axis=1)
    return jnp.take(blocks, source, axis=0)


def body(pair_rep, alignment, lengths, chain_breaks, shifts, *weights):
    group_count = lax.axis_size("pool")
    my_group = lax.axis_index("pool")
    half = lax.axis_index("dap")
    slot_count = pair_rep.shape[0]
    count = slot_count // 2
    capacity = max(2, (2 * slot_count + group_count - 1) // group_count)
    buffer_slots = group_count * capacity
    swap = [(0, 1), (1, 0)]
    mine = half * count
    theirs = (1 - half) * count
    home = my_group * slot_count
    place = jnp.stack([half, theirs, mine, home]).astype(jnp.int32)
    alignment_proj, outer_proj = weights[:2]
    inner = alignment_proj.shape[1] // 2
    w_spread = spread_matrix(alignment.shape[1], inner)
    w_outer = (
        outer_proj.reshape(inner, inner, -1).transpose(1, 0, 2).reshape(outer_proj.shape)
    )
    send_sides, send_pair = project(True, place, lengths, alignment, pair_rep, alignment_proj, w_spread)
    other_sides = lax.ppermute(send_sides, "dap", swap)
    other_pair = lax.ppermute(send_pair, "dap", swap)
    own_sides = project(False, place, lengths, alignment, pair_rep, alignment_proj, w_spread)
    keep, send = update(
        place, lengths, chain_breaks, own_sides, other_sides, pair_rep, other_pair, (w_outer,) + weights[2:]
    )
    received = lax.ppermute(send, "dap", swap)
    result = jnp.concatenate([keep, received], axis=0)

    slot_index = jnp.arange(slot_count, dtype=jnp.int32)
    earlier = (shifts[None, :] == shifts[:, None]) & (slot_index[None, :] < slot_index[:, None])
    slot_rank = jnp.sum(earlier.astype(jnp.int32), axis=1)
    send_at = (my_group + shifts) % group_count * capacity + slot_rank
    send_at = jnp.where(half == 0, send_at, jnp.roll(send_at, count))
    receive_position = (my_group - shifts) % group_count * capacity + slot_rank
    outgoing = pack_slots(result, send_at, buffer_slots)
    received_blocks = lax.all_to_all(outgoing, "pool", split_axis=0, concat_axis=0, tiled=True)
    return jnp.take(received_blocks, receive_position, axis=0)


def solution(mesh):
    return jax.shard_map(
        body,
        mesh=mesh,
        in_specs=(
            P(("screen", "pool"), "dap", None, None),
            P(("screen", "pool"), None, "dap", None),
            P("screen"),
            P("screen"),
            P("screen"),
        )
        + (P(),) * 9,
        out_specs=P(("screen", "pool"), "dap", None, None),
        check_vma=False,
    )
```

```python
import functools

import jax
import jax.numpy as jnp
import numpy as np
from jax import lax
from jax.experimental import pallas as pl
from jax.experimental.pallas import tpu as pltpu
from jax.sharding import PartitionSpec as P

EPSILON = 1e-05
F32 = jnp.float32
BF16 = jnp.bfloat16
LANES = 128
VMEM_LIMIT = 24 * 2**20


def dot(left, right):
    return jnp.dot(left, right, preferred_element_type=F32)


def normalize(values, scale):
    width = values.shape[-1]
    values = values - jnp.sum(values, axis=-1, keepdims=True) * (1.0 / width)
    spread = jnp.sum(values * values, axis=-1, keepdims=True)
    return (values * (lax.rsqrt(spread + width * EPSILON) * scale)).astype(BF16)


def lane_groups(inner):
    group = lax.broadcasted_iota(jnp.int32, (1, LANES), 1) // inner
    return [group == q for q in range(LANES // inner)]


def project_kernel(
    place_ref, lengths_ref, alignment, w_align, w_spread, own_ref, send_ref, side, rights
):
    slots, depth, rows, width = alignment.shape
    count = slots // 2
    inner = rights.shape[-1] // depth
    pieces = LANES // inner
    half, theirs, mine, home = place_ref[0], place_ref[1], place_ref[2], place_ref[3]
    groups = lane_groups(inner)
    source = lax.broadcasted_iota(jnp.int32, (2 * inner, 2 * LANES), 0)
    target = lax.broadcasted_iota(jnp.int32, (2 * inner, 2 * LANES), 1)
    repeat = (source == (target // LANES) * inner + target % inner).astype(BF16)
    w_project = lax.dot_general(
        w_align[...], repeat, (((0,), (0,)), ((), ())), preferred_element_type=F32
    ).astype(BF16)
    residue = lax.broadcasted_iota(jnp.int32, (rows, 1), 0) + half * rows

    def one(index, start, which, out_ref):
        length = lengths_ref[home + start + index]
        values = alignment[start + index].astype(F32).reshape(depth * rows, width)
        values = dot(normalize(values, width**0.5), w_project)
        values = values.reshape(depth, rows, 2 * LANES) * jnp.where(residue < length, 1.0, 0.0)
        side[which] = values[:, :, :LANES].reshape(depth * rows, LANES) * (1.0 / depth)
        tiles = []
        for tile in range(rows // pieces):
            piece = side[which, pl.ds(tile * pieces, depth, stride=rows), :]
            for q in range(1, pieces):
                other = side[which, pl.ds(tile * pieces + q, depth, stride=rows), :]
                piece = jnp.where(groups[q], other, piece)
            tiles.append(piece)
        out_ref[index, :depth] = jnp.concatenate(tiles, axis=1).astype(BF16)
        for tile in range(depth // pieces):
            piece = values[tile * pieces, :, LANES:]
            for q in range(1, pieces):
                piece = jnp.where(groups[q], values[tile * pieces + q, :, LANES:], piece)
            rights[which, index, :, LANES * tile : LANES * tile + LANES] = piece

    def step(index, carry):
        one(index, mine, 0, own_ref)
        one(index, theirs, 1, send_ref)
        return carry

    lax.fori_loop(0, count, step, 0)
    flat = rights[...].reshape(slots * rows, depth * inner).astype(BF16)
    spread = dot(flat, w_spread[...]).reshape(2, count, rows, depth * inner).astype(BF16)
    parts = own_ref.shape[-1]
    for which, out_ref in enumerate((own_ref, send_ref)):
        for part in range(depth * inner // parts):
            out_ref[:, depth + part * rows : depth + part * rows + rows] = spread[
                which, :, :, part * parts : part * parts + parts
            ]


def project(place, lengths, alignment, w_align, w_spread):
    slots, depth, rows, width = alignment.shape
    count = slots // 2
    inner = w_align.shape[0] // 2
    smem = pl.BlockSpec(memory_space=pltpu.SMEM)
    vmem = pl.BlockSpec(memory_space=pltpu.VMEM)
    out = jax.ShapeDtypeStruct((count, 2 * depth, rows * inner), BF16)
    return pl.pallas_call(
        project_kernel,
        out_shape=(out, out),
        in_specs=[smem, smem, vmem, vmem, vmem],
        out_specs=(vmem, vmem),
        scratch_shapes=[
            pltpu.VMEM((2, depth * rows, LANES), F32),
            pltpu.VMEM((2, count, rows, depth * inner), F32),
        ],
        compiler_params=pltpu.CompilerParams(vmem_limit_bytes=VMEM_LIMIT),
        cost_estimate=pl.CostEstimate(flops=2 * 10**9, bytes_accessed=4 * 10**6, transcendentals=0),
        name="project",
    )(place, lengths, alignment, w_align, w_spread)


def update_kernel(
    place_ref,
    lengths_ref,
    breaks_ref,
    own_sides,
    other_sides,
    pair,
    other_pair,
    w_outer,
    bias,
    out_ab,
    out_gate,
    out_proj,
    in_ab,
    in_gate,
    in_proj,
    keep_ref,
    send_ref,
    stacked,
    outer,
    updates,
    first,
    second,
):
    count, rows, full, width = keep_ref.shape
    depth = own_sides.shape[1] // 2
    inner = own_sides.shape[2] // rows
    pieces = LANES // inner
    sets = inner // pieces
    hidden = out_proj.shape[0]
    half = place_ref[0]
    start = place_ref[2]
    home = place_ref[3] + start
    low_is_own = half == 0
    groups = lane_groups(inner)
    zero = jnp.zeros((), BF16)
    stacked[...] = jnp.zeros_like(stacked)
    place_j = lax.broadcasted_iota(jnp.int32, (full, 1), 0)

    def outer_update(step):
        own, other = own_sides[step], other_sides[step]
        low = jnp.where(low_is_own, own, other)
        high = jnp.where(low_is_own, other, own)
        for tile in range(full // pieces):
            source = low if tile < rows // pieces else high
            at = tile % (rows // pieces) * LANES
            left = source[:depth, at : at + LANES]
            turned = [left] + [pltpu.roll(left, inner * turn, 1) for turn in range(1, pieces)]
            for p in range(pieces):
                column = (tile * pieces + p) * LANES
                for q in range(pieces):
                    stacked[depth * q : depth * q + depth, column : column + LANES] = jnp.where(
                        groups[q], turned[(q - p) % pieces], zero
                    )
        lanes = own_sides.shape[2]
        right = jnp.concatenate(
            [
                jnp.concatenate([low[depth + rows * part : depth + rows * part + rows] for part in range(depth // rows)], axis=1),
                jnp.concatenate([high[depth + rows * part : depth + rows * part + rows] for part in range(depth // rows)], axis=1),
            ],
            axis=0,
        )
        per = LANES // (pieces * depth)
        tiles = []
        for c2 in range(sets):
            tile = right[:, c2 // per * LANES : c2 // per * LANES + LANES]
            turn = c2 % per * pieces * depth
            tiles.append(pltpu.roll(tile, LANES - turn, 1) if turn else tile)
        right = jnp.concatenate(tiles, axis=0)
        for i in range(0, full, 2):
            product = dot(right, stacked[:, LANES * i : LANES * i + 2 * LANES]).astype(BF16)
            for k in range(2):
                for g in range(sets):
                    outer[full * (i + k) : full * (i + k) + full, LANES * g : LANES * g + LANES] = product[
                        full * g : full * g + full, LANES * k : LANES * k + LANES
                    ]
        updates[...] = dot(outer[...], w_outer[...])

    def finish(step):
        length = lengths_ref[home + step]
        stop = breaks_ref[home + step]
        own, other = pair[start + step], other_pair[start + step]
        low = jnp.where(low_is_own, own, other).reshape(rows * full, width)
        high = jnp.where(low_is_own, other, own).reshape(rows * full, width)
        within, across = bias[0:1].astype(F32), bias[1:2].astype(F32)
        head = place_j < stop
        terms = (jnp.where(head, within, across), jnp.where(head, across, within))
        chain = jnp.concatenate([jnp.where(i < stop, terms[0], terms[1]) for i in range(full)], axis=0)
        column = jnp.where(place_j < length, 1.0, 0.0)
        inside = jnp.concatenate([jnp.where(i < length, column, 0.0) for i in range(full)], axis=0)
        z1 = jnp.concatenate([low, high], axis=0).astype(F32) + updates[...] + chain
        unit = 0.5 * width**0.5
        within_unit = inside * unit

        def sides(values, w_ab, w_gate):
            x = normalize(values, within_unit)
            projected = dot(x, w_ab[...])
            a = (jnp.tanh(projected[:, hidden : 2 * hidden]) + 1.0) * projected[:, :hidden]
            b = (jnp.tanh(projected[:, 3 * hidden :]) + 1.0) * projected[:, 2 * hidden : 3 * hidden]
            gate = jnp.tanh(dot(x, w_gate[...])) + 1.0
            return a, b, gate

        def contract(row_of, columns):
            parts = []
            for i in range(full):
                terms = [row_of(i, k) * columns[k] for k in range(full)]
                while len(terms) > 1:
                    terms = [terms[n] + terms[n + 1] for n in range(0, len(terms), 2)]
                parts.append(terms[0])
            return jnp.concatenate(parts, axis=0)

        a, b, gate = sides(z1, out_ab, out_gate)
        first[...] = a
        second[...] = b
        columns = [second[pl.ds(k, full, stride=full), :] for k in range(full)]
        t = contract(lambda i, k: first[pl.ds(full * i + k, 1), :], columns)
        z2 = (z1 + gate * dot(normalize(t, unit), out_proj[...])).astype(BF16).astype(F32)
        a, b, gate = sides(z2, in_ab, in_gate)
        second[...] = b
        columns = [a[full * k : full * k + full] for k in range(full)]
        t = contract(lambda i, k: second[pl.ds(full * k + i, 1), :], columns)
        y3 = ((z2 + gate * dot(normalize(t, unit), in_proj[...])) * inside).astype(BF16)
        low = y3[: rows * full].reshape(rows, full, width)
        high = y3[rows * full :].reshape(rows, full, width)
        keep_ref[step] = jnp.where(low_is_own, low, high)
        send_ref[step] = jnp.where(low_is_own, high, low)

    outer_update(0)

    def both(step, carry):
        finish(step)
        outer_update(jnp.minimum(step + 1, count - 1))
        return carry

    lax.fori_loop(0, count, both, 0)


def update(place, lengths, breaks, own_sides, other_sides, pair, other_pair, weights):
    outer_proj, chain_bias, out_ab, out_gate, out_proj, in_ab, in_gate, in_proj = weights
    count, depth = own_sides.shape[0], own_sides.shape[1] // 2
    rows, full, width = pair.shape[1:]
    inner = own_sides.shape[2] // rows
    smem = pl.BlockSpec(memory_space=pltpu.SMEM)
    vmem = pl.BlockSpec(memory_space=pltpu.VMEM)
    shape = jax.ShapeDtypeStruct((count,) + pair.shape[1:], BF16)
    pairs = full * full
    return pl.pallas_call(
        update_kernel,
        out_shape=(shape, shape),
        in_specs=[smem] * 3 + [vmem] * 12,
        out_specs=(vmem, vmem),
        scratch_shapes=[
            pltpu.VMEM((LANES, full * LANES), BF16),
            pltpu.VMEM((pairs, inner * inner), BF16),
            pltpu.VMEM((pairs, width), F32),
            pltpu.VMEM((pairs, width), F32),
            pltpu.VMEM((pairs, width), F32),
        ],
        compiler_params=pltpu.CompilerParams(vmem_limit_bytes=VMEM_LIMIT),
        cost_estimate=pl.CostEstimate(flops=10**10, bytes_accessed=4 * 10**6, transcendentals=0),
        name="pair_update",
    )(
        place,
        lengths,
        breaks,
        own_sides,
        other_sides,
        pair,
        other_pair,
        outer_proj,
        chain_bias,
        out_ab,
        out_gate,
        out_proj,
        in_ab,
        in_gate,
        in_proj,
    )


def spread_matrix(depth, inner):
    pieces = LANES // inner
    r, c2 = np.divmod(np.arange(depth * inner), inner)
    matrix = np.zeros((depth * inner, depth * inner), np.float32)
    matrix[np.arange(depth * inner), (c2 // pieces) * pieces * depth + (c2 % pieces) * depth + r] = 1.0
    return jnp.asarray(matrix, BF16)


def build_tables(shifts_ref, table, counts, capacity):
    slots, groups = shifts_ref.shape[0], counts.shape[0]
    for v in range(groups):
        counts[v] = 0

    def step(slot, carry):
        v = shifts_ref[slot]
        rank = counts[v]
        table[v * capacity + rank] = slot
        counts[v] = rank + 1
        return carry

    lax.fori_loop(0, slots, step, 0)


def list_large(counts, large, low):
    for k in range(large.shape[0]):
        large[k] = 0
    found = jnp.int32(0)
    for v in range(1, counts.shape[0]):
        many = counts[v] > low

        @pl.when(many)
        def _(found=found, v=v):
            large[found] = v

        found = found + many.astype(jnp.int32)
    return found


def pair_index(first, second, groups):
    both = groups + (first - 1) * (2 * groups - 2 - first) // 2 + second - first - 1
    return jnp.where(second > 0, both, first)


def pack_kernel(low, capacity, half_ref, shifts_ref, keep, other, *refs):
    table, counts, large = refs[-3:]
    groups = counts.shape[0]
    branch = refs[-4]
    outs = refs[:-4]
    statics, rests = outs[: groups - 1], outs[groups - 1 :]
    count = keep.shape[0]
    slots = shifts_ref.shape[0]
    base = half_ref[0] * count
    build_tables(shifts_ref, table, counts, capacity)
    found = list_large(counts, large, low)
    branches = branch.shape[0] - 1
    for n in range(branches):
        second = large[2 * n + 1] if 2 * n + 1 < large.shape[0] else 0
        branch[n] = pair_index(large[2 * n], second, groups)
    branch[branches] = found

    def fetch(v, rank):
        slot = jnp.where(rank < counts[v], table[v * capacity + rank], 0)
        at = slot - base
        mine = (at >= 0) & (at < count)
        near = keep[jnp.clip(at, 0, count - 1)]
        far = other[jnp.clip(slot - (count - base), 0, count - 1)]
        return jnp.where(mine, near, far)

    for v in range(1, groups):
        for rank in range(low):
            statics[v - 1][rank] = fetch(v, rank)
    for k, rest in enumerate(rests):
        @pl.when(k < found)
        def _(k=k, rest=rest):
            v = large[k]
            for rank in range(low, capacity):
                rest[rank - low] = fetch(v, rank)


def unpack_kernel(low, capacity, half_ref, shifts_ref, keep, other, *refs):
    table, counts, large = refs[-3:]
    groups = counts.shape[0]
    out = refs[-4]
    statics, rests = refs[: groups - 1], refs[groups - 1 : -4]
    count = keep.shape[0]
    base = half_ref[0] * count
    build_tables(shifts_ref, table, counts, capacity)
    found = list_large(counts, large, low)

    def step(rank, carry):
        slot = table[rank]
        at = slot - base
        mine = (at >= 0) & (at < count)
        near = keep[jnp.clip(at, 0, count - 1)]
        far = other[jnp.clip(slot - (count - base), 0, count - 1)]
        out[slot] = jnp.where(mine, near, far)
        return carry

    lax.fori_loop(0, counts[0], step, 0)
    for v in range(1, groups):
        for rank in range(low):
            @pl.when(rank < counts[v])
            def _(v=v, rank=rank):
                out[table[v * capacity + rank]] = statics[v - 1][rank]
    for k, rest in enumerate(rests):
        for rank in range(low, capacity):
            @pl.when((k < found) & (rank < counts[large[k]]))
            def _(k=k, rank=rank, rest=rest):
                out[table[large[k] * capacity + rank]] = rest[rank - low]


def exchange(half, shifts, keep, other, group_count, capacity):
    slots = shifts.shape[0]
    low = capacity // 2
    most = min(slots // (low + 1), group_count - 1)
    most += most % 2
    block = keep.shape[1:]
    smem = pl.BlockSpec(memory_space=pltpu.SMEM)
    vmem = pl.BlockSpec(memory_space=pltpu.VMEM)
    tables = [
        pltpu.SMEM((group_count * capacity,), jnp.int32),
        pltpu.SMEM((group_count,), jnp.int32),
        pltpu.SMEM((most,), jnp.int32),
    ]
    params = pltpu.CompilerParams(vmem_limit_bytes=VMEM_LIMIT)
    low_shape = jax.ShapeDtypeStruct((low,) + block, BF16)
    high_shape = jax.ShapeDtypeStruct((capacity - low,) + block, BF16)
    packed = pl.pallas_call(
        functools.partial(pack_kernel, low, capacity),
        out_shape=[low_shape] * (group_count - 1)
        + [high_shape] * most
        + [jax.ShapeDtypeStruct((most // 2 + 1,), jnp.int32)],
        in_specs=[smem, smem, vmem, vmem],
        out_specs=[vmem] * (group_count - 1 + most) + [smem],
        scratch_shapes=tables,
        compiler_params=params,
        name="pack",
    )(half, shifts, keep, other)
    statics = packed[: group_count - 1]
    rests = packed[group_count - 1 : -1]
    branch = packed[-1]

    def move(block, v):
        return lax.ppermute(block, "pool", [(g, (g + v) % group_count) for g in range(group_count)])

    arrived = [move(block, v + 1) for v, block in enumerate(statics)]
    choices = [()] + [(v,) for v in range(1, group_count)]
    choices += [(v, w) for v in range(1, group_count) for w in range(v + 1, group_count)]

    def choice(shift_pair):
        def run(first, second):
            if len(shift_pair) > 0:
                first = move(first, shift_pair[0])
            if len(shift_pair) > 1:
                second = move(second, shift_pair[1])
            return first, second

        return run

    def pair_move(n, first, second):
        return lax.switch(branch[n], [choice(shift_pair) for shift_pair in choices], first, second)

    late = list(pair_move(0, rests[0], rests[1]))
    if most > 2:
        def more(*blocks):
            moved = []
            for n in range(0, len(blocks), 2):
                moved += pair_move(n // 2 + 1, blocks[n], blocks[n + 1])
            return tuple(moved)

        late += lax.cond(branch[most // 2] > 2, more, lambda *blocks: blocks, *rests[2:])
    return pl.pallas_call(
        functools.partial(unpack_kernel, low, capacity),
        out_shape=jax.ShapeDtypeStruct((slots,) + block, BF16),
        in_specs=[smem, smem] + [vmem] * (2 + group_count - 1 + most),
        out_specs=vmem,
        scratch_shapes=tables,
        compiler_params=params,
        name="unpack",
    )(half, shifts, keep, other, *arrived, *late)


def exchange_padded(half, shifts, keep, other, group_count, capacity):
    slots = shifts.shape[0]
    count = slots // 2
    my_group = lax.axis_index("pool")
    blocks = jnp.where(
        half == 0, jnp.concatenate([keep, other], axis=0), jnp.concatenate([other, keep], axis=0)
    )
    slot = jnp.arange(slots, dtype=jnp.int32)
    earlier = (shifts[None, :] == shifts[:, None]) & (slot[None, :] < slot[:, None])
    rank = jnp.sum(earlier.astype(jnp.int32), axis=1)
    send_at = (my_group + shifts) % group_count * capacity + rank
    receive_at = (my_group - shifts) % group_count * capacity + rank
    place = jnp.arange(group_count * capacity, dtype=jnp.int32)
    source = jnp.sum(jnp.where(send_at[None, :] == place[:, None], slot[None, :], 0), axis=1)
    received = lax.all_to_all(
        jnp.take(blocks, source, axis=0), "pool", split_axis=0, concat_axis=0, tiled=True
    )
    return jnp.take(received, receive_at, axis=0)


def body(pair_rep, alignment, lengths, chain_breaks, shifts, *weights):
    group_count = lax.axis_size("pool")
    slot_count = pair_rep.shape[0]
    count = slot_count // 2
    capacity = max(2, (2 * slot_count + group_count - 1) // group_count)
    half = lax.axis_index("dap").astype(jnp.int32)
    swap = [(0, 1), (1, 0)]
    place = jnp.stack([half, (1 - half) * count, half * count, lax.axis_index("pool") * slot_count])
    place = place.astype(jnp.int32)
    alignment_proj, outer_proj = weights[:2]
    inner = alignment_proj.shape[1] // 2
    w_spread = spread_matrix(alignment.shape[1], inner)
    w_outer = (
        outer_proj.reshape(inner, inner, -1).transpose(1, 0, 2).reshape(outer_proj.shape)
    )
    other_pair = lax.ppermute(pair_rep, "dap", swap)
    own_sides, send_sides = project(place, lengths, alignment, alignment_proj.T, w_spread)
    other_sides = lax.ppermute(send_sides, "dap", swap)
    keep, send = update(
        place, lengths, chain_breaks, own_sides, other_sides, pair_rep, other_pair, (w_outer,) + weights[2:]
    )
    other = lax.ppermute(send, "dap", swap)
    move = exchange if group_count <= 8 else exchange_padded
    return move(half.reshape(1), shifts, keep, other, group_count, capacity)


def solution(mesh):
    return jax.shard_map(
        body,
        mesh=mesh,
        in_specs=(
            P(("screen", "pool"), "dap", None, None),
            P(("screen", "pool"), None, "dap", None),
            P("screen"),
            P("screen"),
            P("screen"),
        )
        + (P(),) * 9,
        out_specs=P(("screen", "pool"), "dap", None, None),
        check_vma=False,
    )
```

```python
import functools
import itertools

import jax
import jax.numpy as jnp
import numpy as np
from jax import lax
from jax.experimental import pallas as pl
from jax.experimental.pallas import tpu as pltpu
from jax.sharding import PartitionSpec as P

EPSILON = 1e-05
F32 = jnp.float32
BF16 = jnp.bfloat16
LANES = 128
AT_ONCE = 3
VMEM_LIMIT = 24 * 2**20
WAYS = 4
PROJECT_WAYS = 2
OUTER_AFTER = 2
BLOCK = 4
OUTER_TILES = 4


def dot(left, right):
    return jnp.dot(left, right, preferred_element_type=F32)


def normalize_steps(values, scale, ones):
    width = values.shape[-1]
    values = values - jnp.sum(values, axis=-1, keepdims=True) * (1.0 / width)
    yield
    spread = dot((values * values).astype(BF16), ones[...])
    yield
    return (values * (lax.rsqrt(spread + width * EPSILON) * scale)).astype(BF16)


def interleave(streams):
    running = list(streams)
    while running:
        for stream in list(running):
            if next(stream, running) is running:
                running.remove(stream)


def lane_groups(inner):
    group = lax.broadcasted_iota(jnp.int32, (1, LANES), 1) // inner
    return [group == q for q in range(LANES // inner)]


def project_kernel(
    place_ref,
    lengths_in,
    alignment_in,
    w_align_in,
    w_spread_in,
    own_ref,
    send_ref,
    lengths_ref,
    alignment,
    w_align,
    w_spread,
    side,
    rights,
    sems,
):
    slots, depth, rows, width = alignment.shape
    count = slots // 2
    inner = rights.shape[-1] // depth
    pieces = LANES // inner
    half, theirs, mine, home = place_ref[0], place_ref[1], place_ref[2], place_ref[3]
    copies = [
        pltpu.make_async_copy(source, target, sems.at[n])
        for n, (source, target) in enumerate(
            ((w_align_in, w_align), (lengths_in, lengths_ref), (alignment_in, alignment), (w_spread_in, w_spread))
        )
    ]
    for copy in copies:
        copy.start()
    groups = lane_groups(inner)
    source = lax.broadcasted_iota(jnp.int32, (2 * inner, 2 * LANES), 0)
    target = lax.broadcasted_iota(jnp.int32, (2 * inner, 2 * LANES), 1)
    repeat = (source == (target // LANES) * inner + target % inner).astype(BF16)
    copies[0].wait()
    w_project = lax.dot_general(
        w_align[...], repeat, (((0,), (0,)), ((), ())), preferred_element_type=F32
    ).astype(BF16)
    residue = lax.broadcasted_iota(jnp.int32, (rows, 1), 0) + half * rows
    copies[1].wait()
    copies[2].wait()

    def one(index, start, which, way, out_ref):
        length = lengths_ref[home + start + index]
        values = alignment[start + index].astype(F32).reshape(depth * rows, width)
        values = values - jnp.sum(values, axis=-1, keepdims=True) * (1.0 / width)
        yield
        spread = jnp.sum(values * values, axis=-1, keepdims=True) * (1.0 / width)
        yield
        values = dot((values * lax.rsqrt(spread + EPSILON)).astype(BF16), w_project)
        yield
        values = values.reshape(depth, rows, 2 * LANES) * jnp.where(residue < length, 1.0, 0.0)
        side[way] = values[:, :, :LANES].reshape(depth * rows, LANES) * (1.0 / depth)
        tiles = []
        for tile in range(rows // pieces):
            piece = side[way, pl.ds(tile * pieces, depth, stride=rows), :]
            for q in range(1, pieces):
                other = side[way, pl.ds(tile * pieces + q, depth, stride=rows), :]
                piece = jnp.where(groups[q], other, piece)
            tiles.append(piece)
        out_ref[index, :depth] = jnp.concatenate(tiles, axis=1).astype(BF16)
        for tile in range(depth // pieces):
            piece = values[tile * pieces, :, LANES:]
            for q in range(1, pieces):
                piece = jnp.where(groups[q], values[tile * pieces + q, :, LANES:], piece)
            rights[which, index, :, LANES * tile : LANES * tile + LANES] = piece

    ways = side.shape[0] // 2

    def step(round_, carry):
        streams = []
        for way in range(ways):
            index = jnp.minimum(round_ * ways + way, count - 1)
            streams.append(one(index, mine, 0, 2 * way, own_ref))
            streams.append(one(index, theirs, 1, 2 * way + 1, send_ref))
        interleave(streams)
        return carry

    lax.fori_loop(0, (count + ways - 1) // ways, step, 0)
    copies[3].wait()
    flat = rights[...].reshape(slots * rows, depth * inner).astype(BF16)
    spread = dot(flat, w_spread[...]).reshape(2, count, rows, depth * inner).astype(BF16)
    parts = own_ref.shape[-1]
    for which, out_ref in enumerate((own_ref, send_ref)):
        for part in range(depth * inner // parts):
            out_ref[:, depth + part * rows : depth + part * rows + rows] = spread[
                which, :, :, part * parts : part * parts + parts
            ]


def project(place, lengths, alignment, w_align, w_spread):
    slots, depth, rows, width = alignment.shape
    count = slots // 2
    inner = w_align.shape[0] // 2
    smem = pl.BlockSpec(memory_space=pltpu.SMEM)
    vmem = pl.BlockSpec(memory_space=pltpu.VMEM)
    hbm = pl.BlockSpec(memory_space=pltpu.HBM)
    out = jax.ShapeDtypeStruct((count, 2 * depth, rows * inner), BF16)
    return pl.pallas_call(
        project_kernel,
        out_shape=(out, out),
        in_specs=[smem, hbm, hbm, hbm, hbm],
        out_specs=(vmem, vmem),
        scratch_shapes=[
            pltpu.SMEM(lengths.shape, jnp.int32),
            pltpu.VMEM(alignment.shape, BF16),
            pltpu.VMEM(w_align.shape, BF16),
            pltpu.VMEM(w_spread.shape, BF16),
            pltpu.VMEM((2 * PROJECT_WAYS, depth * rows, LANES), F32),
            pltpu.VMEM((2, count, rows, depth * inner), F32),
            pltpu.SemaphoreType.DMA((4,)),
        ],
        compiler_params=pltpu.CompilerParams(vmem_limit_bytes=VMEM_LIMIT),
        cost_estimate=pl.CostEstimate(flops=2 * 10**9, bytes_accessed=4 * 10**6, transcendentals=0),
        name="project",
    )(place, lengths, alignment, w_align, w_spread)


def update_kernel(
    place_ref,
    lengths_ref,
    breaks_ref,
    own_sides,
    other_sides,
    pair,
    other_pair,
    w_outer,
    bias,
    out_ab,
    out_gate,
    out_proj,
    in_ab,
    in_gate,
    in_proj,
    keep_ref,
    send_ref,
    ones,
    updates_refs,
    stream_refs,
    gates_refs,
    sides_refs,
):
    count, rows, full, width = keep_ref.shape
    depth = own_sides.shape[1] // 2
    inner = own_sides.shape[2] // rows
    pieces = LANES // inner
    sets = inner // pieces
    hidden = out_proj.shape[0]
    half = place_ref[0]
    start = place_ref[2]
    home = place_ref[3] + start
    low_is_own = half == 0
    groups = lane_groups(inner)
    zero = jnp.zeros((), BF16)
    place_j = lax.broadcasted_iota(jnp.int32, (full, 1), 0)
    ones[...] = jnp.ones_like(ones)
    unit = 0.5 * width**0.5
    pairs = full * full
    ways = updates_refs.shape[0]
    within, across = bias[0:1].astype(F32), bias[1:2].astype(F32)

    def clamp(index):
        return jnp.minimum(index, count - 1)

    def outer_update(way, step):
        own, other = own_sides[step], other_sides[step]
        low = jnp.where(low_is_own, own, other)
        high = jnp.where(low_is_own, other, own)
        right = jnp.concatenate(
            [
                jnp.concatenate(
                    [side[depth + rows * part : depth + rows * part + rows] for part in range(depth // rows)],
                    axis=1,
                )
                for side in (low, high)
            ],
            axis=0,
        )
        per = LANES // (pieces * depth)
        tiles = []
        for c2 in range(sets):
            tile = right[:, c2 // per * LANES : c2 // per * LANES + LANES]
            turn = c2 % per * pieces * depth
            tiles.append(pltpu.roll(tile, LANES - turn, 1) if turn else tile)
        right = jnp.concatenate(tiles, axis=0)
        yield
        tail = jnp.zeros((LANES - pieces * depth, 2 * LANES), BF16)
        lefts = rows // pieces
        parts = []
        for tile in range(full // pieces):
            source = low if tile < lefts else high
            at = tile % lefts * LANES
            left = source[:depth, at : at + LANES]
            turned = [left] + [pltpu.roll(left, inner * turn, 1) for turn in range(1, pieces)]
            for first_p in range(0, pieces, 2):
                column = [
                    jnp.concatenate(
                        [jnp.where(groups[q], turned[(q - p) % pieces], zero) for q in range(pieces)], axis=0
                    )
                    for p in (first_p, first_p + 1)
                ]
                stacked = jnp.concatenate([jnp.concatenate(column, axis=1), tail], axis=0)
                product = dot(right, stacked).astype(BF16)
                for k in range(2):
                    parts.append(
                        jnp.concatenate(
                            [
                                product[full * g : full * g + full, LANES * k : LANES * k + LANES]
                                for g in range(sets)
                            ],
                            axis=1,
                        )
                    )
                yield
            if (tile + 1) % OUTER_TILES == 0:
                span = len(parts) * full
                start_row = (tile + 1) * pieces * full - span
                updates_refs[way, start_row : start_row + span] = dot(
                    jnp.concatenate(parts, axis=0), w_outer[...]
                )
                parts = []
                yield

    def row_masks(length):
        column = jnp.where(place_j < length, 1.0, 0.0)
        return jnp.concatenate([jnp.where(i < length, column, 0.0) for i in range(full)], axis=0)

    def sides(values, inside, w_ab, w_gate, way, first):
        x = yield from normalize_steps(values, inside * unit, ones)
        yield
        for n in range(2):
            projected = dot(x, w_ab[:, 2 * hidden * n : 2 * hidden * n + 2 * hidden])
            sides_refs[way, first + n] = (jnp.tanh(projected[:, hidden:]) + 1.0) * projected[:, :hidden]
            yield
        gates_refs[way] = jnp.tanh(dot(x, w_gate[...])) + 1.0

    def contract(row_of, column_of):
        parts = []
        for first in range(0, full, BLOCK):
            totals = [None] * BLOCK
            for k in range(full):
                column = column_of(k)
                for i in range(BLOCK):
                    term = row_of(first + i, k) * column
                    totals[i] = term if totals[i] is None else totals[i] + term
            parts += totals
            yield
        return jnp.concatenate(parts, axis=0)

    def begin(step, way):
        stop = breaks_ref[home + step]
        head = place_j < stop
        terms = (jnp.where(head, within, across), jnp.where(head, across, within))
        chain = jnp.concatenate([jnp.where(i < stop, terms[0], terms[1]) for i in range(full)], axis=0)
        own, other = pair[start + step], other_pair[start + step]
        block = jnp.concatenate(
            [jnp.where(low_is_own, own, other), jnp.where(low_is_own, other, own)], axis=0
        )
        z1 = block.reshape(pairs, width).astype(F32) + updates_refs[way] + chain
        stream_refs[way] = z1
        yield
        yield from sides(z1, row_masks(lengths_ref[home + step]), out_ab, out_gate, way, 0)

    def middle(step, way):
        t = yield from contract(
            lambda i, k: sides_refs[way, 0, pl.ds(full * i + k, 1), :],
            lambda k: sides_refs[way, 1, pl.ds(k, full, stride=full), :],
        )
        u = yield from normalize_steps(t, unit, ones)
        yield
        z2 = stream_refs[way] + gates_refs[way] * dot(u, out_proj[...])
        z2 = z2.astype(BF16).astype(F32)
        stream_refs[way] = z2
        yield
        yield from sides(z2, row_masks(lengths_ref[home + step]), in_ab, in_gate, way, 2)

    def last(step, way):
        t = yield from contract(
            lambda i, k: sides_refs[way, 3, pl.ds(full * k + i, 1), :],
            lambda k: sides_refs[way, 2, full * k : full * k + full],
        )
        u = yield from normalize_steps(t, unit, ones)
        yield
        y3 = stream_refs[way] + gates_refs[way] * dot(u, in_proj[...])
        y3 = (y3 * row_masks(lengths_ref[home + step])).astype(BF16)
        low = y3[: rows * full].reshape(rows, full, width)
        high = y3[rows * full :].reshape(rows, full, width)
        keep_ref[step] = jnp.where(low_is_own, low, high)
        send_ref[step] = jnp.where(low_is_own, high, low)

    def whole(step, way):
        yield from begin(step, way)
        yield
        yield from middle(step, way)
        yield
        yield from last(step, way)

    def later(streams, ticks):
        for _ in range(ticks):
            yield
        for stream in streams:
            yield from stream

    def both(round_, carry):
        steps = [clamp(round_ * ways + way) for way in range(ways)]
        ahead = [clamp(round_ * ways + ways + way) for way in range(ways)]
        outers = [outer_update(way, step) for way, step in enumerate(ahead)]
        streams = [whole(step, way) for way, step in enumerate(steps)]
        interleave(streams + [later(outers, OUTER_AFTER)])
        return carry

    interleave([outer_update(way, clamp(way)) for way in range(ways)])
    lax.fori_loop(0, (count + ways - 1) // ways, both, 0)


def update(place, lengths, breaks, own_sides, other_sides, pair, other_pair, weights):
    outer_proj, chain_bias, out_ab, out_gate, out_proj, in_ab, in_gate, in_proj = weights
    count, depth = own_sides.shape[0], own_sides.shape[1] // 2
    rows, full, width = pair.shape[1:]
    inner = own_sides.shape[2] // rows
    smem = pl.BlockSpec(memory_space=pltpu.SMEM)
    vmem = pl.BlockSpec(memory_space=pltpu.VMEM)
    shape = jax.ShapeDtypeStruct((count,) + pair.shape[1:], BF16)
    pairs, hidden = full * full, out_proj.shape[0]
    return pl.pallas_call(
        update_kernel,
        out_shape=(shape, shape),
        in_specs=[smem] * 3 + [vmem] * 12,
        out_specs=(vmem, vmem),
        scratch_shapes=[
            pltpu.VMEM((width, width), BF16),
            pltpu.VMEM((WAYS, pairs, width), F32),
            pltpu.VMEM((WAYS, pairs, width), F32),
            pltpu.VMEM((WAYS, pairs, width), F32),
            pltpu.VMEM((WAYS, 4, pairs, hidden), F32),
        ],
        compiler_params=pltpu.CompilerParams(vmem_limit_bytes=VMEM_LIMIT),
        cost_estimate=pl.CostEstimate(flops=10**10, bytes_accessed=4 * 10**6, transcendentals=0),
        name="pair_update",
    )(
        place,
        lengths,
        breaks,
        own_sides,
        other_sides,
        pair,
        other_pair,
        outer_proj,
        chain_bias,
        out_ab,
        out_gate,
        out_proj,
        in_ab,
        in_gate,
        in_proj,
    )


def spread_matrix(depth, inner):
    pieces = LANES // inner
    r, c2 = np.divmod(np.arange(depth * inner), inner)
    matrix = np.zeros((depth * inner, depth * inner), np.float32)
    matrix[np.arange(depth * inner), (c2 // pieces) * pieces * depth + (c2 % pieces) * depth + r] = 1.0
    return jnp.asarray(matrix, BF16)


def build_tables(shifts_ref, table, counts, capacity):
    slots, groups = shifts_ref.shape[0], counts.shape[0]
    for v in range(groups):
        counts[v] = 0

    def step(slot, carry):
        v = shifts_ref[slot]
        rank = counts[v]
        table[v * capacity + rank] = slot
        counts[v] = rank + 1
        return carry

    lax.fori_loop(0, slots, step, 0)


def list_large(counts, large, low):
    for k in range(large.shape[0]):
        large[k] = 0
    found = jnp.int32(0)
    for v in range(1, counts.shape[0]):
        many = counts[v] > low

        @pl.when(many)
        def _(found=found, v=v):
            large[found] = v

        found = found + many.astype(jnp.int32)
    return found


def subsets(groups, most):
    return [c for n in range(most + 1) for c in itertools.combinations(range(1, groups), n)]


def pack_kernel(low, capacity, half_ref, shifts_ref, keep, other, *refs):
    table, counts, large = refs[-3:]
    groups = counts.shape[0]
    branch = refs[-4]
    outs = refs[:-4]
    statics, rests = outs[: groups - 1], outs[groups - 1 :]
    count = keep.shape[0]
    slots = shifts_ref.shape[0]
    base = half_ref[0] * count
    build_tables(shifts_ref, table, counts, capacity)
    found = list_large(counts, large, low)
    taken = [large[k] for k in range(min(AT_ONCE, large.shape[0]))]
    index = jnp.int32(0)
    for n, subset in enumerate(subsets(groups, AT_ONCE)):
        same = functools.reduce(
            jnp.logical_and, [t == (subset[k] if k < len(subset) else 0) for k, t in enumerate(taken)]
        )
        index = jnp.where(same, n, index)
    branch[0] = index
    branch[1] = found
    for k in range(AT_ONCE, large.shape[0]):
        branch[2 + k - AT_ONCE] = large[k]

    def fetch(v, rank):
        slot = jnp.where(rank < counts[v], table[v * capacity + rank], 0)
        at = slot - base
        mine = (at >= 0) & (at < count)
        near = keep[jnp.clip(at, 0, count - 1)]
        far = other[jnp.clip(slot - (count - base), 0, count - 1)]
        return jnp.where(mine, near, far)

    for v in range(1, groups):
        for rank in range(low):
            statics[v - 1][rank] = fetch(v, rank)
    for k, rest in enumerate(rests):
        @pl.when(k < found)
        def _(k=k, rest=rest):
            v = large[k]
            for rank in range(low, capacity):
                rest[rank - low] = fetch(v, rank)


def unpack_kernel(low, capacity, half_ref, shifts_ref, keep, other, *refs):
    table, counts, large = refs[-3:]
    groups = counts.shape[0]
    out = refs[-4]
    statics, rests = refs[: groups - 1], refs[groups - 1 : -4]
    count = keep.shape[0]
    base = half_ref[0] * count
    build_tables(shifts_ref, table, counts, capacity)
    found = list_large(counts, large, low)

    def step(rank, carry):
        slot = table[rank]
        at = slot - base
        mine = (at >= 0) & (at < count)
        near = keep[jnp.clip(at, 0, count - 1)]
        far = other[jnp.clip(slot - (count - base), 0, count - 1)]
        out[slot] = jnp.where(mine, near, far)
        return carry

    lax.fori_loop(0, counts[0], step, 0)
    for v in range(1, groups):
        for rank in range(low):
            @pl.when(rank < counts[v])
            def _(v=v, rank=rank):
                out[table[v * capacity + rank]] = statics[v - 1][rank]
    for k, rest in enumerate(rests):
        for rank in range(low, capacity):
            @pl.when((k < found) & (rank < counts[large[k]]))
            def _(k=k, rank=rank, rest=rest):
                out[table[large[k] * capacity + rank]] = rest[rank - low]


def exchange(half, shifts, keep, other, group_count, capacity):
    slots = shifts.shape[0]
    low = capacity // 2
    most = min(slots // (low + 1), group_count - 1)
    most = max(most, AT_ONCE)
    block = keep.shape[1:]
    smem = pl.BlockSpec(memory_space=pltpu.SMEM)
    vmem = pl.BlockSpec(memory_space=pltpu.VMEM)
    tables = [
        pltpu.SMEM((group_count * capacity,), jnp.int32),
        pltpu.SMEM((group_count,), jnp.int32),
        pltpu.SMEM((most,), jnp.int32),
    ]
    params = pltpu.CompilerParams(vmem_limit_bytes=VMEM_LIMIT)
    low_shape = jax.ShapeDtypeStruct((low,) + block, BF16)
    high_shape = jax.ShapeDtypeStruct((capacity - low,) + block, BF16)
    packed = pl.pallas_call(
        functools.partial(pack_kernel, low, capacity),
        out_shape=[low_shape] * (group_count - 1)
        + [high_shape] * most
        + [jax.ShapeDtypeStruct((2 + most - AT_ONCE,), jnp.int32)],
        in_specs=[smem, smem, vmem, vmem],
        out_specs=[vmem] * (group_count - 1 + most) + [smem],
        scratch_shapes=tables,
        compiler_params=params,
        name="pack",
    )(half, shifts, keep, other)
    statics = packed[: group_count - 1]
    rests = packed[group_count - 1 : -1]
    branch = packed[-1]

    def move(block, v):
        return lax.ppermute(block, "pool", [(g, (g + v) % group_count) for g in range(group_count)])

    arrived = [move(block, v + 1) for v, block in enumerate(statics)]
    def choice(subset):
        def run(*blocks):
            moved = [move(block, v) for block, v in zip(blocks, subset)]
            return tuple(moved) + blocks[len(subset) :]

        return run

    late = list(
        lax.switch(
            branch[0], [choice(subset) for subset in subsets(group_count, AT_ONCE)], *rests[:AT_ONCE]
        )
    )
    if most > AT_ONCE:

        def more(*blocks):
            singles = [choice(subset) for subset in subsets(group_count, 1)]
            return tuple(lax.switch(branch[2 + k], singles, block)[0] for k, block in enumerate(blocks))

        late += lax.cond(branch[1] > AT_ONCE, more, lambda *blocks: blocks, *rests[AT_ONCE:])
    return pl.pallas_call(
        functools.partial(unpack_kernel, low, capacity),
        out_shape=jax.ShapeDtypeStruct((slots,) + block, BF16),
        in_specs=[smem, smem] + [vmem] * (2 + group_count - 1 + most),
        out_specs=vmem,
        scratch_shapes=tables,
        compiler_params=params,
        name="unpack",
    )(half, shifts, keep, other, *arrived, *late)


def exchange_padded(half, shifts, keep, other, group_count, capacity):
    slots = shifts.shape[0]
    count = slots // 2
    my_group = lax.axis_index("pool")
    blocks = jnp.where(
        half == 0, jnp.concatenate([keep, other], axis=0), jnp.concatenate([other, keep], axis=0)
    )
    slot = jnp.arange(slots, dtype=jnp.int32)
    earlier = (shifts[None, :] == shifts[:, None]) & (slot[None, :] < slot[:, None])
    rank = jnp.sum(earlier.astype(jnp.int32), axis=1)
    send_at = (my_group + shifts) % group_count * capacity + rank
    receive_at = (my_group - shifts) % group_count * capacity + rank
    place = jnp.arange(group_count * capacity, dtype=jnp.int32)
    source = jnp.sum(jnp.where(send_at[None, :] == place[:, None], slot[None, :], 0), axis=1)
    received = lax.all_to_all(
        jnp.take(blocks, source, axis=0), "pool", split_axis=0, concat_axis=0, tiled=True
    )
    return jnp.take(received, receive_at, axis=0)


def body(pair_rep, alignment, lengths, chain_breaks, shifts, *weights):
    group_count = lax.axis_size("pool")
    slot_count = pair_rep.shape[0]
    count = slot_count // 2
    capacity = max(2, (2 * slot_count + group_count - 1) // group_count)
    half = lax.axis_index("dap").astype(jnp.int32)
    swap = [(0, 1), (1, 0)]
    place = jnp.stack([half, (1 - half) * count, half * count, lax.axis_index("pool") * slot_count])
    place = place.astype(jnp.int32)
    alignment_proj, outer_proj = weights[:2]
    inner = alignment_proj.shape[1] // 2
    w_spread = spread_matrix(alignment.shape[1], inner)
    w_outer = (
        outer_proj.reshape(inner, inner, -1).transpose(1, 0, 2).reshape(outer_proj.shape)
    )
    other_pair = lax.ppermute(pair_rep, "dap", swap)
    own_sides, send_sides = project(place, lengths, alignment, alignment_proj.T, w_spread)
    other_sides = lax.ppermute(send_sides, "dap", swap)
    keep, send = update(
        place, lengths, chain_breaks, own_sides, other_sides, pair_rep, other_pair, (w_outer,) + weights[2:]
    )
    other = lax.ppermute(send, "dap", swap)
    move = exchange if group_count <= 8 else exchange_padded
    return move(half.reshape(1), shifts, keep, other, group_count, capacity)


def solution(mesh):
    return jax.shard_map(
        body,
        mesh=mesh,
        in_specs=(
            P(("screen", "pool"), "dap", None, None),
            P(("screen", "pool"), None, "dap", None),
            P("screen"),
            P("screen"),
            P("screen"),
        )
        + (P(),) * 9,
        out_specs=P(("screen", "pool"), "dap", None, None),
        check_vma=False,
    )
```

```python
import functools
import itertools

import jax
import jax.numpy as jnp
import numpy as np
from jax import lax
from jax.experimental import pallas as pl
from jax.experimental.pallas import tpu as pltpu
from jax.sharding import PartitionSpec as P

EPSILON = 1e-05
F32 = jnp.float32
BF16 = jnp.bfloat16
LANES = 128
AT_ONCE = 3
VMEM_LIMIT = 24 * 2**20
PROJECT_LIMIT = 64500000
WAYS = 4
PROJECT_WAYS = 3
OUTER_AFTER = 2
BLOCK = 4
OUTER_TILES = 4


def dot(left, right):
    return jnp.dot(left, right, preferred_element_type=F32)


def normalize_steps(values, scale, ones):
    width = values.shape[-1]
    values = values - jnp.sum(values, axis=-1, keepdims=True) * (1.0 / width)
    yield
    spread = dot((values * values).astype(BF16), ones[...])
    yield
    return (values * (lax.rsqrt(spread + width * EPSILON) * scale)).astype(BF16)


def interleave(streams):
    running = list(streams)
    while running:
        for stream in list(running):
            if next(stream, running) is running:
                running.remove(stream)


def lane_groups(inner):
    group = lax.broadcasted_iota(jnp.int32, (1, LANES), 1) // inner
    return [group == q for q in range(LANES // inner)]


def project_kernel(
    place_ref,
    lengths_in,
    alignment_in,
    w_align_in,
    w_spread_in,
    own_ref,
    send_ref,
    lengths_ref,
    alignment,
    w_align,
    w_spread,
    side,
    rights,
    sems,
):
    slots, depth, rows, width = alignment.shape
    count = slots // 2
    inner = rights.shape[-1] // depth
    pieces = LANES // inner
    half, theirs, mine, home = place_ref[0], place_ref[1], place_ref[2], place_ref[3]
    copies = [
        pltpu.make_async_copy(source, target, sems.at[n])
        for n, (source, target) in enumerate(
            ((w_align_in, w_align), (lengths_in, lengths_ref), (alignment_in, alignment), (w_spread_in, w_spread))
        )
    ]
    for copy in copies:
        copy.start()
    groups = lane_groups(inner)
    source = lax.broadcasted_iota(jnp.int32, (2 * inner, 2 * LANES), 0)
    target = lax.broadcasted_iota(jnp.int32, (2 * inner, 2 * LANES), 1)
    repeat = (source == (target // LANES) * inner + target % inner).astype(BF16)
    copies[0].wait()
    w_project = lax.dot_general(
        w_align[...], repeat, (((0,), (0,)), ((), ())), preferred_element_type=F32
    ).astype(BF16)
    residue = lax.broadcasted_iota(jnp.int32, (rows, 1), 0) + half * rows
    copies[1].wait()
    copies[2].wait()

    def one(index, start, which, way, out_ref):
        length = lengths_ref[home + start + index]
        values = alignment[start + index].astype(F32).reshape(depth * rows, width)
        values = values - jnp.sum(values, axis=-1, keepdims=True) * (1.0 / width)
        yield
        spread = jnp.sum(values * values, axis=-1, keepdims=True) * (1.0 / width)
        yield
        values = dot((values * lax.rsqrt(spread + EPSILON)).astype(BF16), w_project)
        yield
        values = values.reshape(depth, rows, 2 * LANES) * jnp.where(residue < length, 1.0, 0.0)
        side[way] = values[:, :, :LANES].reshape(depth * rows, LANES) * (1.0 / depth)
        tiles = []
        for tile in range(rows // pieces):
            piece = side[way, pl.ds(tile * pieces, depth, stride=rows), :]
            for q in range(1, pieces):
                other = side[way, pl.ds(tile * pieces + q, depth, stride=rows), :]
                piece = jnp.where(groups[q], other, piece)
            tiles.append(piece)
        out_ref[index, :depth] = jnp.concatenate(tiles, axis=1).astype(BF16)
        for tile in range(depth // pieces):
            piece = values[tile * pieces, :, LANES:]
            for q in range(1, pieces):
                piece = jnp.where(groups[q], values[tile * pieces + q, :, LANES:], piece)
            rights[which, index, :, LANES * tile : LANES * tile + LANES] = piece

    ways = side.shape[0] // 2

    def step(round_, carry):
        streams = []
        for way in range(ways):
            index = jnp.minimum(round_ * ways + way, count - 1)
            streams.append(one(index, mine, 0, 2 * way, own_ref))
            streams.append(one(index, theirs, 1, 2 * way + 1, send_ref))
        interleave(streams)
        return carry

    lax.fori_loop(0, (count + ways - 1) // ways, step, 0)
    copies[3].wait()
    flat = rights[...].reshape(slots * rows, depth * inner).astype(BF16)
    spread = dot(flat, w_spread[...]).reshape(2, count, rows, depth * inner).astype(BF16)
    parts = own_ref.shape[-1]
    for which, out_ref in enumerate((own_ref, send_ref)):
        for part in range(depth * inner // parts):
            out_ref[:, depth + part * rows : depth + part * rows + rows] = spread[
                which, :, :, part * parts : part * parts + parts
            ]


def project(place, lengths, alignment, w_align, w_spread):
    slots, depth, rows, width = alignment.shape
    count = slots // 2
    inner = w_align.shape[0] // 2
    smem = pl.BlockSpec(memory_space=pltpu.SMEM)
    vmem = pl.BlockSpec(memory_space=pltpu.VMEM)
    hbm = pl.BlockSpec(memory_space=pltpu.HBM)
    out = jax.ShapeDtypeStruct((count, 2 * depth, rows * inner), BF16)
    return pl.pallas_call(
        project_kernel,
        out_shape=(out, out),
        in_specs=[smem, hbm, hbm, hbm, hbm],
        out_specs=(vmem, vmem),
        scratch_shapes=[
            pltpu.SMEM(lengths.shape, jnp.int32),
            pltpu.VMEM(alignment.shape, BF16),
            pltpu.VMEM(w_align.shape, BF16),
            pltpu.VMEM(w_spread.shape, BF16),
            pltpu.VMEM((2 * PROJECT_WAYS, depth * rows, LANES), F32),
            pltpu.VMEM((2, count, rows, depth * inner), F32),
            pltpu.SemaphoreType.DMA((4,)),
        ],
        compiler_params=pltpu.CompilerParams(vmem_limit_bytes=PROJECT_LIMIT),
        cost_estimate=pl.CostEstimate(flops=2 * 10**9, bytes_accessed=4 * 10**6, transcendentals=0),
        name="project",
    )(place, lengths, alignment, w_align, w_spread)


def update_kernel(
    place_ref,
    lengths_ref,
    breaks_ref,
    own_sides,
    other_sides,
    pair,
    other_pair,
    w_outer,
    bias,
    out_ab,
    out_gate,
    out_proj,
    in_ab,
    in_gate,
    in_proj,
    keep_ref,
    send_ref,
    ones,
    updates_refs,
    stream_refs,
    gates_refs,
    sides_refs,
):
    count, rows, full, width = keep_ref.shape
    depth = own_sides.shape[1] // 2
    inner = own_sides.shape[2] // rows
    pieces = LANES // inner
    sets = inner // pieces
    hidden = out_proj.shape[0]
    half = place_ref[0]
    start = place_ref[2]
    home = place_ref[3] + start
    low_is_own = half == 0
    groups = lane_groups(inner)
    zero = jnp.zeros((), BF16)
    place_j = lax.broadcasted_iota(jnp.int32, (full, 1), 0)
    ones[...] = jnp.ones_like(ones)
    unit = 0.5 * width**0.5
    pairs = full * full
    ways = updates_refs.shape[0]
    within, across = bias[0:1].astype(F32), bias[1:2].astype(F32)

    def clamp(index):
        return jnp.minimum(index, count - 1)

    def outer_update(way, step):
        own, other = own_sides[step], other_sides[step]
        low = jnp.where(low_is_own, own, other)
        high = jnp.where(low_is_own, other, own)
        right = jnp.concatenate(
            [
                jnp.concatenate(
                    [side[depth + rows * part : depth + rows * part + rows] for part in range(depth // rows)],
                    axis=1,
                )
                for side in (low, high)
            ],
            axis=0,
        )
        per = LANES // (pieces * depth)
        tiles = []
        for c2 in range(sets):
            tile = right[:, c2 // per * LANES : c2 // per * LANES + LANES]
            turn = c2 % per * pieces * depth
            tiles.append(pltpu.roll(tile, LANES - turn, 1) if turn else tile)
        right = jnp.concatenate(tiles, axis=0)
        yield
        tail = jnp.zeros((LANES - pieces * depth, 2 * LANES), BF16)
        lefts = rows // pieces
        parts = []
        for tile in range(full // pieces):
            source = low if tile < lefts else high
            at = tile % lefts * LANES
            left = source[:depth, at : at + LANES]
            turned = [left] + [pltpu.roll(left, inner * turn, 1) for turn in range(1, pieces)]
            for first_p in range(0, pieces, 2):
                column = [
                    jnp.concatenate(
                        [jnp.where(groups[q], turned[(q - p) % pieces], zero) for q in range(pieces)], axis=0
                    )
                    for p in (first_p, first_p + 1)
                ]
                stacked = jnp.concatenate([jnp.concatenate(column, axis=1), tail], axis=0)
                product = dot(right, stacked).astype(BF16)
                for k in range(2):
                    parts.append(
                        jnp.concatenate(
                            [
                                product[full * g : full * g + full, LANES * k : LANES * k + LANES]
                                for g in range(sets)
                            ],
                            axis=1,
                        )
                    )
                yield
            if (tile + 1) % OUTER_TILES == 0:
                span = len(parts) * full
                start_row = (tile + 1) * pieces * full - span
                updates_refs[way, start_row : start_row + span] = dot(
                    jnp.concatenate(parts, axis=0), w_outer[...]
                )
                parts = []
                yield

    def row_masks(length):
        column = jnp.where(place_j < length, 1.0, 0.0)
        return jnp.concatenate([jnp.where(i < length, column, 0.0) for i in range(full)], axis=0)

    def sides(values, inside, w_ab, w_gate, way, first):
        x = yield from normalize_steps(values, inside * unit, ones)
        yield
        for n in range(2):
            projected = dot(x, w_ab[:, 2 * hidden * n : 2 * hidden * n + 2 * hidden])
            sides_refs[way, first + n] = (jnp.tanh(projected[:, hidden:]) + 1.0) * projected[:, :hidden]
            yield
        gates_refs[way] = jnp.tanh(dot(x, w_gate[...])) + 1.0

    def contract(row_of, column_of):
        parts = []
        for first in range(0, full, BLOCK):
            totals = [None] * BLOCK
            for k in range(full):
                column = column_of(k)
                for i in range(BLOCK):
                    term = row_of(first + i, k) * column
                    totals[i] = term if totals[i] is None else totals[i] + term
            parts += totals
            yield
        return jnp.concatenate(parts, axis=0)

    def begin(step, way):
        stop = breaks_ref[home + step]
        head = place_j < stop
        terms = (jnp.where(head, within, across), jnp.where(head, across, within))
        chain = jnp.concatenate([jnp.where(i < stop, terms[0], terms[1]) for i in range(full)], axis=0)
        own, other = pair[start + step], other_pair[start + step]
        block = jnp.concatenate(
            [jnp.where(low_is_own, own, other), jnp.where(low_is_own, other, own)], axis=0
        )
        z1 = block.reshape(pairs, width).astype(F32) + updates_refs[way] + chain
        stream_refs[way] = z1
        yield
        yield from sides(z1, row_masks(lengths_ref[home + step]), out_ab, out_gate, way, 0)

    def middle(step, way):
        t = yield from contract(
            lambda i, k: sides_refs[way, 0, pl.ds(full * i + k, 1), :],
            lambda k: sides_refs[way, 1, pl.ds(k, full, stride=full), :],
        )
        u = yield from normalize_steps(t, unit, ones)
        yield
        z2 = stream_refs[way] + gates_refs[way] * dot(u, out_proj[...])
        z2 = z2.astype(BF16).astype(F32)
        stream_refs[way] = z2
        yield
        yield from sides(z2, row_masks(lengths_ref[home + step]), in_ab, in_gate, way, 2)

    def last(step, way):
        t = yield from contract(
            lambda i, k: sides_refs[way, 3, pl.ds(full * k + i, 1), :],
            lambda k: sides_refs[way, 2, full * k : full * k + full],
        )
        u = yield from normalize_steps(t, unit, ones)
        yield
        y3 = stream_refs[way] + gates_refs[way] * dot(u, in_proj[...])
        y3 = (y3 * row_masks(lengths_ref[home + step])).astype(BF16)
        low = y3[: rows * full].reshape(rows, full, width)
        high = y3[rows * full :].reshape(rows, full, width)
        keep_ref[step] = jnp.where(low_is_own, low, high)
        send_ref[step] = jnp.where(low_is_own, high, low)

    def whole(step, way):
        yield from begin(step, way)
        yield
        yield from middle(step, way)
        yield
        yield from last(step, way)

    def later(streams, ticks):
        for _ in range(ticks):
            yield
        for stream in streams:
            yield from stream

    def both(round_, carry):
        steps = [clamp(round_ * ways + way) for way in range(ways)]
        ahead = [clamp(round_ * ways + ways + way) for way in range(ways)]
        outers = [outer_update(way, step) for way, step in enumerate(ahead)]
        streams = [whole(step, way) for way, step in enumerate(steps)]
        interleave(streams + [later(outers, OUTER_AFTER)])
        return carry

    interleave([outer_update(way, clamp(way)) for way in range(ways)])
    lax.fori_loop(0, (count + ways - 1) // ways, both, 0)


def update(place, lengths, breaks, own_sides, other_sides, pair, other_pair, weights):
    outer_proj, chain_bias, out_ab, out_gate, out_proj, in_ab, in_gate, in_proj = weights
    count, depth = own_sides.shape[0], own_sides.shape[1] // 2
    rows, full, width = pair.shape[1:]
    inner = own_sides.shape[2] // rows
    smem = pl.BlockSpec(memory_space=pltpu.SMEM)
    vmem = pl.BlockSpec(memory_space=pltpu.VMEM)
    shape = jax.ShapeDtypeStruct((count,) + pair.shape[1:], BF16)
    pairs, hidden = full * full, out_proj.shape[0]
    return pl.pallas_call(
        update_kernel,
        out_shape=(shape, shape),
        in_specs=[smem] * 3 + [vmem] * 12,
        out_specs=(vmem, vmem),
        scratch_shapes=[
            pltpu.VMEM((width, width), BF16),
            pltpu.VMEM((WAYS, pairs, width), F32),
            pltpu.VMEM((WAYS, pairs, width), F32),
            pltpu.VMEM((WAYS, pairs, width), F32),
            pltpu.VMEM((WAYS, 4, pairs, hidden), F32),
        ],
        compiler_params=pltpu.CompilerParams(vmem_limit_bytes=VMEM_LIMIT),
        cost_estimate=pl.CostEstimate(flops=10**10, bytes_accessed=4 * 10**6, transcendentals=0),
        name="pair_update",
    )(
        place,
        lengths,
        breaks,
        own_sides,
        other_sides,
        pair,
        other_pair,
        outer_proj,
        chain_bias,
        out_ab,
        out_gate,
        out_proj,
        in_ab,
        in_gate,
        in_proj,
    )


def spread_matrix(depth, inner):
    pieces = LANES // inner
    r, c2 = np.divmod(np.arange(depth * inner), inner)
    matrix = np.zeros((depth * inner, depth * inner), np.float32)
    matrix[np.arange(depth * inner), (c2 // pieces) * pieces * depth + (c2 % pieces) * depth + r] = 1.0
    return jnp.asarray(matrix, BF16)


def build_tables(shifts_ref, table, counts, capacity):
    slots, groups = shifts_ref.shape[0], counts.shape[0]
    for v in range(groups):
        counts[v] = 0

    def step(slot, carry):
        v = shifts_ref[slot]
        rank = counts[v]
        table[v * capacity + rank] = slot
        counts[v] = rank + 1
        return carry

    lax.fori_loop(0, slots, step, 0)


def list_large(counts, large, low):
    for k in range(large.shape[0]):
        large[k] = 0
    found = jnp.int32(0)
    for v in range(1, counts.shape[0]):
        many = counts[v] > low

        @pl.when(many)
        def _(found=found, v=v):
            large[found] = v

        found = found + many.astype(jnp.int32)
    return found


def subsets(groups, most):
    return [c for n in range(most + 1) for c in itertools.combinations(range(1, groups), n)]


def pack_kernel(low, capacity, half_ref, shifts_ref, keep, other, *refs):
    branch, table, counts, large, sem = refs[-5:]
    groups = counts.shape[0]
    outs = refs[:-5]
    statics, rests = outs[: groups - 1], outs[groups - 1 :]
    count = keep.shape[0]
    slots = shifts_ref.shape[0]
    base = half_ref[0] * count
    build_tables(shifts_ref, table, counts, capacity)
    found = list_large(counts, large, low)
    taken = [large[k] for k in range(min(AT_ONCE, large.shape[0]))]
    index = jnp.int32(0)
    for n, subset in enumerate(subsets(groups, AT_ONCE)):
        same = functools.reduce(
            jnp.logical_and, [t == (subset[k] if k < len(subset) else 0) for k, t in enumerate(taken)]
        )
        index = jnp.where(same, n, index)
    branch[0] = index
    branch[1] = found
    for k in range(AT_ONCE, large.shape[0]):
        branch[2 + k - AT_ONCE] = large[k]

    def send(v, rank, target, action):
        slot = table[v * capacity + rank]
        at = slot - base
        mine = (at >= 0) & (at < count)
        for chosen, source, index in (
            (mine, keep, at),
            (jnp.logical_not(mine), other, slot - (count - base)),
        ):

            @pl.when((rank < counts[v]) & chosen)
            def _(source=source, index=index):
                action(pltpu.make_async_copy(source.at[jnp.clip(index, 0, count - 1)], target, sem))

    def every(action):
        for v in range(1, groups):
            for rank in range(low):
                send(v, rank, statics[v - 1].at[rank], action)
        for k, rest in enumerate(rests):

            @pl.when(k < found)
            def _(k=k, rest=rest):
                for rank in range(low, capacity):
                    send(large[k], rank, rest.at[rank - low], action)

    every(lambda copy: copy.start())
    every(lambda copy: copy.wait())


def unpack_kernel(low, capacity, half_ref, shifts_ref, keep, other, *refs):
    out, table, counts, large, sem = refs[-5:]
    groups = counts.shape[0]
    statics, rests = refs[: groups - 1], refs[groups - 1 : -5]
    count = keep.shape[0]
    base = half_ref[0] * count
    build_tables(shifts_ref, table, counts, capacity)
    found = list_large(counts, large, low)

    def put(source, slot):
        pltpu.make_async_copy(source, out.at[slot], sem).start()

    for v in range(1, groups):
        for rank in range(low):

            @pl.when(rank < counts[v])
            def _(v=v, rank=rank):
                put(statics[v - 1].at[rank], table[v * capacity + rank])

    def step(rank, carry):
        slot = table[rank]
        at = slot - base
        mine = (at >= 0) & (at < count)

        @pl.when(mine)
        def _():
            put(keep.at[jnp.clip(at, 0, count - 1)], slot)

        @pl.when(jnp.logical_not(mine))
        def _():
            put(other.at[jnp.clip(slot - (count - base), 0, count - 1)], slot)

        return carry

    lax.fori_loop(0, counts[0], step, 0)
    for k, rest in enumerate(rests):
        for rank in range(low, capacity):

            @pl.when((k < found) & (rank < counts[large[k]]))
            def _(k=k, rank=rank, rest=rest):
                put(rest.at[rank - low], table[large[k] * capacity + rank])

    pltpu.make_async_copy(out, out, sem).wait()


def exchange(half, shifts, keep, other, group_count, capacity):
    slots = shifts.shape[0]
    low = capacity // 2
    most = min(slots // (low + 1), group_count - 1)
    most = max(most, AT_ONCE)
    block = keep.shape[1:]
    smem = pl.BlockSpec(memory_space=pltpu.SMEM)
    vmem = pl.BlockSpec(memory_space=pltpu.VMEM)
    anywhere = pl.BlockSpec(memory_space=pl.ANY)
    tables = [
        pltpu.SMEM((group_count * capacity,), jnp.int32),
        pltpu.SMEM((group_count,), jnp.int32),
        pltpu.SMEM((most,), jnp.int32),
        pltpu.SemaphoreType.DMA,
    ]
    params = pltpu.CompilerParams(vmem_limit_bytes=VMEM_LIMIT)
    low_shape = jax.ShapeDtypeStruct((low,) + block, BF16)
    high_shape = jax.ShapeDtypeStruct((capacity - low,) + block, BF16)
    packed = pl.pallas_call(
        functools.partial(pack_kernel, low, capacity),
        out_shape=[low_shape] * (group_count - 1)
        + [high_shape] * most
        + [jax.ShapeDtypeStruct((2 + most - AT_ONCE,), jnp.int32)],
        in_specs=[smem, smem, vmem, vmem],
        out_specs=[anywhere] * (group_count - 1 + most) + [smem],
        scratch_shapes=tables,
        compiler_params=params,
        name="pack",
    )(half, shifts, keep, other)
    statics = packed[: group_count - 1]
    rests = packed[group_count - 1 : -1]
    branch = packed[-1]

    def move(block, v):
        return lax.ppermute(block, "pool", [(g, (g + v) % group_count) for g in range(group_count)])

    order = sorted(range(1, group_count), key=lambda v: (abs(2 * v - group_count), v))
    arrived = {}
    for v in order:
        arrived[v] = move(statics[v - 1], v)
    arrived = [arrived[v] for v in range(1, group_count)]
    def choice(subset):
        def run(*blocks):
            moved = [move(block, v) for block, v in zip(blocks, subset)]
            return tuple(moved) + blocks[len(subset) :]

        return run

    late = list(
        lax.switch(
            branch[0], [choice(subset) for subset in subsets(group_count, AT_ONCE)], *rests[:AT_ONCE]
        )
    )
    if most > AT_ONCE:

        def more(*blocks):
            singles = [choice(subset) for subset in subsets(group_count, 1)]
            return tuple(lax.switch(branch[2 + k], singles, block)[0] for k, block in enumerate(blocks))

        late += lax.cond(branch[1] > AT_ONCE, more, lambda *blocks: blocks, *rests[AT_ONCE:])
    return pl.pallas_call(
        functools.partial(unpack_kernel, low, capacity),
        out_shape=jax.ShapeDtypeStruct((slots,) + block, BF16),
        in_specs=[smem, smem] + [vmem] * (2 + group_count - 1 + most),
        out_specs=anywhere,
        scratch_shapes=tables,
        compiler_params=params,
        name="unpack",
    )(half, shifts, keep, other, *arrived, *late)


def exchange_padded(half, shifts, keep, other, group_count, capacity):
    slots = shifts.shape[0]
    count = slots // 2
    my_group = lax.axis_index("pool")
    blocks = jnp.where(
        half == 0, jnp.concatenate([keep, other], axis=0), jnp.concatenate([other, keep], axis=0)
    )
    slot = jnp.arange(slots, dtype=jnp.int32)
    earlier = (shifts[None, :] == shifts[:, None]) & (slot[None, :] < slot[:, None])
    rank = jnp.sum(earlier.astype(jnp.int32), axis=1)
    send_at = (my_group + shifts) % group_count * capacity + rank
    receive_at = (my_group - shifts) % group_count * capacity + rank
    place = jnp.arange(group_count * capacity, dtype=jnp.int32)
    source = jnp.sum(jnp.where(send_at[None, :] == place[:, None], slot[None, :], 0), axis=1)
    received = lax.all_to_all(
        jnp.take(blocks, source, axis=0), "pool", split_axis=0, concat_axis=0, tiled=True
    )
    return jnp.take(received, receive_at, axis=0)


def body(pair_rep, alignment, lengths, chain_breaks, shifts, *weights):
    group_count = lax.axis_size("pool")
    slot_count = pair_rep.shape[0]
    count = slot_count // 2
    capacity = max(2, (2 * slot_count + group_count - 1) // group_count)
    half = lax.axis_index("dap").astype(jnp.int32)
    swap = [(0, 1), (1, 0)]
    place = jnp.stack([half, (1 - half) * count, half * count, lax.axis_index("pool") * slot_count])
    place = place.astype(jnp.int32)
    alignment_proj, outer_proj = weights[:2]
    inner = alignment_proj.shape[1] // 2
    w_spread = spread_matrix(alignment.shape[1], inner)
    w_outer = (
        outer_proj.reshape(inner, inner, -1).transpose(1, 0, 2).reshape(outer_proj.shape)
    )
    other_pair = lax.ppermute(pair_rep, "dap", swap)
    own_sides, send_sides = project(place, lengths, alignment, alignment_proj.T, w_spread)
    other_sides = lax.ppermute(send_sides, "dap", swap)
    keep, send = update(
        place, lengths, chain_breaks, own_sides, other_sides, pair_rep, other_pair, (w_outer,) + weights[2:]
    )
    other = lax.ppermute(send, "dap", swap)
    move = exchange if group_count <= 8 else exchange_padded
    return move(half.reshape(1), shifts, keep, other, group_count, capacity)


def solution(mesh):
    return jax.shard_map(
        body,
        mesh=mesh,
        in_specs=(
            P(("screen", "pool"), "dap", None, None),
            P(("screen", "pool"), None, "dap", None),
            P("screen"),
            P("screen"),
            P("screen"),
        )
        + (P(),) * 9,
        out_specs=P(("screen", "pool"), "dap", None, None),
        check_vma=False,
    )
```

```python
import functools
import itertools

import jax
import jax.numpy as jnp
import numpy as np
from jax import lax
from jax.experimental import pallas as pl
from jax.experimental.pallas import tpu as pltpu
from jax.sharding import PartitionSpec as P

EPSILON = 1e-05
F32 = jnp.float32
BF16 = jnp.bfloat16
LANES = 128
AT_ONCE = 3
VMEM_LIMIT = 24 * 2**20
PROJECT_LIMIT = 64500000
WAYS = 4
PROJECT_WAYS = 3
OUTER_AFTER = 2
BLOCK = 4
OUTER_TILES = 4


def dot(left, right):
    return jnp.dot(left, right, preferred_element_type=F32)


def normalize_steps(values, scale, ones):
    width = values.shape[-1]
    values = values - jnp.sum(values, axis=-1, keepdims=True) * (1.0 / width)
    yield
    spread = dot((values * values).astype(BF16), ones[...])
    yield
    return (values * (lax.rsqrt(spread + width * EPSILON) * scale)).astype(BF16)


def interleave(streams):
    running = list(streams)
    while running:
        for stream in list(running):
            if next(stream, running) is running:
                running.remove(stream)


def lane_groups(inner):
    group = lax.broadcasted_iota(jnp.int32, (1, LANES), 1) // inner
    return [group == q for q in range(LANES // inner)]


def project_kernel(
    place_ref,
    lengths_in,
    alignment_in,
    w_align_in,
    w_spread_in,
    own_ref,
    send_ref,
    lengths_ref,
    alignment,
    w_align,
    w_spread,
    side,
    rights,
    sems,
):
    slots, depth, rows, width = alignment.shape
    count = slots // 2
    inner = rights.shape[-1] // depth
    pieces = LANES // inner
    half, theirs, mine, home = place_ref[0], place_ref[1], place_ref[2], place_ref[3]
    copies = [
        pltpu.make_async_copy(source, target, sems.at[n])
        for n, (source, target) in enumerate(
            ((w_align_in, w_align), (lengths_in, lengths_ref), (alignment_in, alignment), (w_spread_in, w_spread))
        )
    ]
    for copy in copies:
        copy.start()
    groups = lane_groups(inner)
    source = lax.broadcasted_iota(jnp.int32, (2 * inner, 2 * LANES), 0)
    target = lax.broadcasted_iota(jnp.int32, (2 * inner, 2 * LANES), 1)
    repeat = (source == (target // LANES) * inner + target % inner).astype(BF16)
    copies[0].wait()
    w_project = lax.dot_general(
        w_align[...], repeat, (((0,), (0,)), ((), ())), preferred_element_type=F32
    ).astype(BF16)
    residue = lax.broadcasted_iota(jnp.int32, (rows, 1), 0) + half * rows
    copies[1].wait()
    copies[2].wait()

    def one(index, start, which, way, out_ref):
        length = lengths_ref[home + start + index]
        values = alignment[start + index].astype(F32).reshape(depth * rows, width)
        values = values - jnp.sum(values, axis=-1, keepdims=True) * (1.0 / width)
        yield
        spread = jnp.sum(values * values, axis=-1, keepdims=True) * (1.0 / width)
        yield
        values = dot((values * lax.rsqrt(spread + EPSILON)).astype(BF16), w_project)
        yield
        values = values.reshape(depth, rows, 2 * LANES) * jnp.where(residue < length, 1.0, 0.0)
        side[way] = values[:, :, :LANES].reshape(depth * rows, LANES) * (1.0 / depth)
        tiles = []
        for tile in range(rows // pieces):
            piece = side[way, pl.ds(tile * pieces, depth, stride=rows), :]
            for q in range(1, pieces):
                other = side[way, pl.ds(tile * pieces + q, depth, stride=rows), :]
                piece = jnp.where(groups[q], other, piece)
            tiles.append(piece)
        out_ref[index, :depth] = jnp.concatenate(tiles, axis=1).astype(BF16)
        for tile in range(depth // pieces):
            piece = values[tile * pieces, :, LANES:]
            for q in range(1, pieces):
                piece = jnp.where(groups[q], values[tile * pieces + q, :, LANES:], piece)
            rights[which, index, :, LANES * tile : LANES * tile + LANES] = piece

    ways = side.shape[0] // 2

    def step(round_, carry):
        streams = []
        for way in range(ways):
            index = jnp.minimum(round_ * ways + way, count - 1)
            streams.append(one(index, mine, 0, 2 * way, own_ref))
            streams.append(one(index, theirs, 1, 2 * way + 1, send_ref))
        interleave(streams)
        return carry

    lax.fori_loop(0, (count + ways - 1) // ways, step, 0)
    copies[3].wait()
    flat = rights[...].reshape(slots * rows, depth * inner).astype(BF16)
    spread = dot(flat, w_spread[...]).reshape(2, count, rows, depth * inner).astype(BF16)
    parts = own_ref.shape[-1]
    for which, out_ref in enumerate((own_ref, send_ref)):
        for part in range(depth * inner // parts):
            out_ref[:, depth + part * rows : depth + part * rows + rows] = spread[
                which, :, :, part * parts : part * parts + parts
            ]


def project(place, lengths, alignment, w_align, w_spread):
    slots, depth, rows, _ = alignment.shape
    count = slots // 2
    inner = w_align.shape[0] // 2
    smem = pl.BlockSpec(memory_space=pltpu.SMEM)
    vmem = pl.BlockSpec(memory_space=pltpu.VMEM)
    hbm = pl.BlockSpec(memory_space=pltpu.HBM)
    out_shape = (count, 2 * depth, rows * inner)
    return pl.pallas_call(
        project_kernel,
        out_shape=(pltpu.VMEM(out_shape, BF16), jax.ShapeDtypeStruct(out_shape, BF16)),
        in_specs=[smem, hbm, hbm, hbm, hbm],
        out_specs=(vmem, vmem),
        scratch_shapes=[
            pltpu.SMEM(lengths.shape, jnp.int32),
            pltpu.VMEM(alignment.shape, BF16),
            pltpu.VMEM(w_align.shape, BF16),
            pltpu.VMEM(w_spread.shape, BF16),
            pltpu.VMEM((2 * PROJECT_WAYS, depth * rows, LANES), F32),
            pltpu.VMEM((2, count, rows, depth * inner), F32),
            pltpu.SemaphoreType.DMA((4,)),
        ],
        compiler_params=pltpu.CompilerParams(vmem_limit_bytes=PROJECT_LIMIT),
        cost_estimate=pl.CostEstimate(flops=2 * 10**9, bytes_accessed=4 * 10**6, transcendentals=0),
        name="project",
    )(place, lengths, alignment, w_align, w_spread)


def update_kernel(
    place_ref,
    lengths_ref,
    breaks_ref,
    own_sides,
    other_sides,
    pair,
    other_pair,
    w_outer,
    bias,
    out_ab,
    out_gate,
    out_proj,
    in_ab,
    in_gate,
    in_proj,
    keep_ref,
    send_ref,
    ones,
    updates_refs,
    stream_refs,
    gates_refs,
    sides_refs,
):
    count, rows, full, width = keep_ref.shape
    depth = own_sides.shape[1] // 2
    inner = own_sides.shape[2] // rows
    pieces = LANES // inner
    sets = inner // pieces
    hidden = out_proj.shape[0]
    half = place_ref[0]
    start = place_ref[2]
    home = place_ref[3] + start
    low_is_own = half == 0
    groups = lane_groups(inner)
    zero = jnp.zeros((), BF16)
    place_j = lax.broadcasted_iota(jnp.int32, (full, 1), 0)
    ones[...] = jnp.ones_like(ones)
    unit = 0.5 * width**0.5
    pairs = full * full
    ways = updates_refs.shape[0]
    within, across = bias[0:1].astype(F32), bias[1:2].astype(F32)

    def clamp(index):
        return jnp.minimum(index, count - 1)

    def outer_update(way, step):
        own, other = own_sides[step], other_sides[step]
        low = jnp.where(low_is_own, own, other)
        high = jnp.where(low_is_own, other, own)
        right = jnp.concatenate(
            [
                jnp.concatenate(
                    [side[depth + rows * part : depth + rows * part + rows] for part in range(depth // rows)],
                    axis=1,
                )
                for side in (low, high)
            ],
            axis=0,
        )
        per = LANES // (pieces * depth)
        tiles = []
        for c2 in range(sets):
            tile = right[:, c2 // per * LANES : c2 // per * LANES + LANES]
            turn = c2 % per * pieces * depth
            tiles.append(pltpu.roll(tile, LANES - turn, 1) if turn else tile)
        right = jnp.concatenate(tiles, axis=0)
        yield
        tail = jnp.zeros((LANES - pieces * depth, 2 * LANES), BF16)
        lefts = rows // pieces
        parts = []
        for tile in range(full // pieces):
            source = low if tile < lefts else high
            at = tile % lefts * LANES
            left = source[:depth, at : at + LANES]
            turned = [left] + [pltpu.roll(left, inner * turn, 1) for turn in range(1, pieces)]
            for first_p in range(0, pieces, 2):
                column = [
                    jnp.concatenate(
                        [jnp.where(groups[q], turned[(q - p) % pieces], zero) for q in range(pieces)], axis=0
                    )
                    for p in (first_p, first_p + 1)
                ]
                stacked = jnp.concatenate([jnp.concatenate(column, axis=1), tail], axis=0)
                product = dot(right, stacked).astype(BF16)
                for k in range(2):
                    parts.append(
                        jnp.concatenate(
                            [
                                product[full * g : full * g + full, LANES * k : LANES * k + LANES]
                                for g in range(sets)
                            ],
                            axis=1,
                        )
                    )
                yield
            if (tile + 1) % OUTER_TILES == 0:
                span = len(parts) * full
                start_row = (tile + 1) * pieces * full - span
                updates_refs[way, start_row : start_row + span] = dot(
                    jnp.concatenate(parts, axis=0), w_outer[...]
                )
                parts = []
                yield

    def row_masks(length):
        column = jnp.where(place_j < length, 1.0, 0.0)
        return jnp.concatenate([jnp.where(i < length, column, 0.0) for i in range(full)], axis=0)

    def sides(values, inside, w_ab, w_gate, way, first):
        x = yield from normalize_steps(values, inside * unit, ones)
        yield
        for n in range(2):
            projected = dot(x, w_ab[:, 2 * hidden * n : 2 * hidden * n + 2 * hidden])
            sides_refs[way, first + n] = (jnp.tanh(projected[:, hidden:]) + 1.0) * projected[:, :hidden]
            yield
        gates_refs[way] = jnp.tanh(dot(x, w_gate[...])) + 1.0

    def contract(row_of, column_of):
        parts = []
        for first in range(0, full, BLOCK):
            totals = [None] * BLOCK
            for k in range(full):
                column = column_of(k)
                for i in range(BLOCK):
                    term = row_of(first + i, k) * column
                    totals[i] = term if totals[i] is None else totals[i] + term
            parts += totals
            yield
        return jnp.concatenate(parts, axis=0)

    def begin(step, way):
        stop = breaks_ref[home + step]
        head = place_j < stop
        terms = (jnp.where(head, within, across), jnp.where(head, across, within))
        chain = jnp.concatenate([jnp.where(i < stop, terms[0], terms[1]) for i in range(full)], axis=0)
        own, other = pair[start + step], other_pair[start + step]
        block = jnp.concatenate(
            [jnp.where(low_is_own, own, other), jnp.where(low_is_own, other, own)], axis=0
        )
        z1 = block.reshape(pairs, width).astype(F32) + updates_refs[way] + chain
        stream_refs[way] = z1
        yield
        yield from sides(z1, row_masks(lengths_ref[home + step]), out_ab, out_gate, way, 0)

    def middle(step, way):
        t = yield from contract(
            lambda i, k: sides_refs[way, 0, pl.ds(full * i + k, 1), :],
            lambda k: sides_refs[way, 1, pl.ds(k, full, stride=full), :],
        )
        u = yield from normalize_steps(t, unit, ones)
        yield
        z2 = stream_refs[way] + gates_refs[way] * dot(u, out_proj[...])
        z2 = z2.astype(BF16).astype(F32)
        stream_refs[way] = z2
        yield
        yield from sides(z2, row_masks(lengths_ref[home + step]), in_ab, in_gate, way, 2)

    def last(step, way):
        t = yield from contract(
            lambda i, k: sides_refs[way, 3, pl.ds(full * k + i, 1), :],
            lambda k: sides_refs[way, 2, full * k : full * k + full],
        )
        u = yield from normalize_steps(t, unit, ones)
        yield
        y3 = stream_refs[way] + gates_refs[way] * dot(u, in_proj[...])
        y3 = (y3 * row_masks(lengths_ref[home + step])).astype(BF16)
        low = y3[: rows * full].reshape(rows, full, width)
        high = y3[rows * full :].reshape(rows, full, width)
        keep_ref[step] = jnp.where(low_is_own, low, high)
        send_ref[step] = jnp.where(low_is_own, high, low)

    def whole(step, way):
        yield from begin(step, way)
        yield
        yield from middle(step, way)
        yield
        yield from last(step, way)

    def later(streams, ticks):
        for _ in range(ticks):
            yield
        for stream in streams:
            yield from stream

    def round_of(steps, ahead):
        streams = [whole(step, way) for way, step in enumerate(steps)]
        outers = [outer_update(way, step) for way, step in enumerate(ahead)]
        interleave(streams + [later(outers, OUTER_AFTER)])

    def both(round_, carry):
        base = round_ * ways
        round_of([base + way for way in range(ways)], [clamp(base + ways + way) for way in range(ways)])
        return carry

    rounds = (count + ways - 1) // ways
    interleave([outer_update(way, clamp(way)) for way in range(ways)])
    lax.fori_loop(0, rounds - 1, both, 0)
    round_of(list(range((rounds - 1) * ways, count)), [])


def update(place, lengths, breaks, own_sides, other_sides, pair, other_pair, weights):
    outer_proj, chain_bias, out_ab, out_gate, out_proj, in_ab, in_gate, in_proj = weights
    count = own_sides.shape[0]
    _, full, width = pair.shape[1:]
    smem = pl.BlockSpec(memory_space=pltpu.SMEM)
    vmem = pl.BlockSpec(memory_space=pltpu.VMEM)
    shape = jax.ShapeDtypeStruct((count,) + pair.shape[1:], BF16)
    pairs, hidden = full * full, out_proj.shape[0]
    return pl.pallas_call(
        update_kernel,
        out_shape=(shape, shape),
        in_specs=[smem] * 3 + [vmem] * 12,
        out_specs=(vmem, vmem),
        scratch_shapes=[
            pltpu.VMEM((width, width), BF16),
            pltpu.VMEM((WAYS, pairs, width), F32),
            pltpu.VMEM((WAYS, pairs, width), F32),
            pltpu.VMEM((WAYS, pairs, width), F32),
            pltpu.VMEM((WAYS, 4, pairs, hidden), F32),
        ],
        compiler_params=pltpu.CompilerParams(vmem_limit_bytes=VMEM_LIMIT),
        cost_estimate=pl.CostEstimate(flops=10**10, bytes_accessed=4 * 10**6, transcendentals=0),
        name="pair_update",
    )(
        place,
        lengths,
        breaks,
        own_sides,
        other_sides,
        pair,
        other_pair,
        outer_proj,
        chain_bias,
        out_ab,
        out_gate,
        out_proj,
        in_ab,
        in_gate,
        in_proj,
    )


def spread_matrix(depth, inner):
    pieces = LANES // inner
    r, c2 = np.divmod(np.arange(depth * inner), inner)
    matrix = np.zeros((depth * inner, depth * inner), np.float32)
    matrix[np.arange(depth * inner), (c2 // pieces) * pieces * depth + (c2 % pieces) * depth + r] = 1.0
    return jnp.asarray(matrix, BF16)


def build_tables(shifts_ref, table, counts, capacity):
    slots, groups = shifts_ref.shape[0], counts.shape[0]
    for v in range(groups):
        counts[v] = 0

    def step(slot, carry):
        v = shifts_ref[slot]
        rank = counts[v]
        table[v * capacity + rank] = slot
        counts[v] = rank + 1
        return carry

    lax.fori_loop(0, slots, step, 0)


def list_large(counts, large, low):
    for k in range(large.shape[0]):
        large[k] = 0
    found = jnp.int32(0)
    for v in range(1, counts.shape[0]):
        many = counts[v] > low

        @pl.when(many)
        def _(found=found, v=v):
            large[found] = v

        found = found + many.astype(jnp.int32)
    return found


def subsets(groups, most):
    return [c for n in range(most + 1) for c in itertools.combinations(range(1, groups), n)]


def pack_kernel(low, capacity, half_ref, shifts_ref, keep, other, *refs):
    branch, table, counts, large = refs[-4:]
    groups = counts.shape[0]
    outs = refs[:-4]
    statics, rests = outs[: groups - 1], outs[groups - 1 :]
    count = keep.shape[0]
    base = half_ref[0] * count
    build_tables(shifts_ref, table, counts, capacity)
    found = list_large(counts, large, low)
    taken = [large[k] for k in range(min(AT_ONCE, large.shape[0]))]
    index = jnp.int32(0)
    for n, subset in enumerate(subsets(groups, AT_ONCE)):
        same = functools.reduce(
            jnp.logical_and, [t == (subset[k] if k < len(subset) else 0) for k, t in enumerate(taken)]
        )
        index = jnp.where(same, n, index)
    branch[0] = index
    branch[1] = found
    for k in range(AT_ONCE, large.shape[0]):
        branch[2 + k - AT_ONCE] = large[k]

    def fetch(v, rank):
        slot = jnp.where(rank < counts[v], table[v * capacity + rank], 0)
        at = slot - base
        mine = (at >= 0) & (at < count)
        near = keep[jnp.clip(at, 0, count - 1)]
        far = other[jnp.clip(slot - (count - base), 0, count - 1)]
        return jnp.where(mine, near, far)

    for v in range(1, groups):
        for rank in range(low):
            statics[v - 1][rank] = fetch(v, rank)
    for k, rest in enumerate(rests):
        @pl.when(k < found)
        def _(k=k, rest=rest):
            v = large[k]
            for rank in range(low, capacity):
                rest[rank - low] = fetch(v, rank)


def unpack_kernel(low, capacity, half_ref, shifts_ref, keep, other, *refs):
    out, table, counts, large, sem = refs[-5:]
    groups = counts.shape[0]
    statics, rests = refs[: groups - 1], refs[groups - 1 : -5]
    count = keep.shape[0]
    base = half_ref[0] * count
    build_tables(shifts_ref, table, counts, capacity)
    found = list_large(counts, large, low)

    def put(source, slot):
        pltpu.make_async_copy(source, out.at[slot], sem).start()

    for v in range(1, groups):
        for rank in range(low):

            @pl.when(rank < counts[v])
            def _(v=v, rank=rank):
                put(statics[v - 1].at[rank], table[v * capacity + rank])

    def step(rank, carry):
        slot = table[rank]
        at = slot - base
        mine = (at >= 0) & (at < count)

        @pl.when(mine)
        def _():
            put(keep.at[jnp.clip(at, 0, count - 1)], slot)

        @pl.when(jnp.logical_not(mine))
        def _():
            put(other.at[jnp.clip(slot - (count - base), 0, count - 1)], slot)

        return carry

    lax.fori_loop(0, counts[0], step, 0)
    for k, rest in enumerate(rests):
        for rank in range(low, capacity):

            @pl.when((k < found) & (rank < counts[large[k]]))
            def _(k=k, rank=rank, rest=rest):
                put(rest.at[rank - low], table[large[k] * capacity + rank])

    pltpu.make_async_copy(out, out, sem).wait()


def exchange(half, shifts, keep, other, group_count, capacity):
    slots = shifts.shape[0]
    low = capacity // 2
    most = min(slots // (low + 1), group_count - 1)
    most = max(most, AT_ONCE)
    block = keep.shape[1:]
    smem = pl.BlockSpec(memory_space=pltpu.SMEM)
    vmem = pl.BlockSpec(memory_space=pltpu.VMEM)
    anywhere = pl.BlockSpec(memory_space=pl.ANY)
    tables = [
        pltpu.SMEM((group_count * capacity,), jnp.int32),
        pltpu.SMEM((group_count,), jnp.int32),
        pltpu.SMEM((most,), jnp.int32),
        pltpu.SemaphoreType.DMA,
    ]
    params = pltpu.CompilerParams(vmem_limit_bytes=VMEM_LIMIT)
    low_shape = jax.ShapeDtypeStruct((low,) + block, BF16)
    high_shape = jax.ShapeDtypeStruct((capacity - low,) + block, BF16)
    packed = pl.pallas_call(
        functools.partial(pack_kernel, low, capacity),
        out_shape=[low_shape] * (group_count - 1)
        + [high_shape] * most
        + [jax.ShapeDtypeStruct((2 + most - AT_ONCE,), jnp.int32)],
        in_specs=[smem, smem, vmem, vmem],
        out_specs=[vmem] * (group_count - 1 + most) + [smem],
        scratch_shapes=tables[:-1],
        compiler_params=params,
        name="pack",
    )(half, shifts, keep, other)
    statics = packed[: group_count - 1]
    rests = packed[group_count - 1 : -1]
    branch = packed[-1]

    def move(block, v):
        return lax.ppermute(block, "pool", [(g, (g + v) % group_count) for g in range(group_count)])

    arrived = {}
    for v in range(1, group_count):
        arrived[v] = move(statics[v - 1], v)
    arrived = [arrived[v] for v in range(1, group_count)]

    def choice(subset):
        def run(*blocks):
            moved = [move(block, v) for block, v in zip(blocks, subset)]
            return tuple(moved) + blocks[len(subset) :]

        return run

    late = list(
        lax.switch(
            branch[0], [choice(subset) for subset in subsets(group_count, AT_ONCE)], *rests[:AT_ONCE]
        )
    )
    if most > AT_ONCE:

        def more(*blocks):
            singles = [choice(subset) for subset in subsets(group_count, 1)]
            return tuple(lax.switch(branch[2 + k], singles, block)[0] for k, block in enumerate(blocks))

        late += lax.cond(branch[1] > AT_ONCE, more, lambda *blocks: blocks, *rests[AT_ONCE:])
    return pl.pallas_call(
        functools.partial(unpack_kernel, low, capacity),
        out_shape=jax.ShapeDtypeStruct((slots,) + block, BF16),
        in_specs=[smem, smem] + [vmem] * (2 + group_count - 1 + most),
        out_specs=anywhere,
        scratch_shapes=tables,
        compiler_params=params,
        name="unpack",
    )(half, shifts, keep, other, *arrived, *late)


def exchange_padded(half, shifts, keep, other, group_count, capacity):
    slots = shifts.shape[0]
    my_group = lax.axis_index("pool")
    blocks = jnp.where(
        half == 0, jnp.concatenate([keep, other], axis=0), jnp.concatenate([other, keep], axis=0)
    )
    slot = jnp.arange(slots, dtype=jnp.int32)
    earlier = (shifts[None, :] == shifts[:, None]) & (slot[None, :] < slot[:, None])
    rank = jnp.sum(earlier.astype(jnp.int32), axis=1)
    send_at = (my_group + shifts) % group_count * capacity + rank
    receive_at = (my_group - shifts) % group_count * capacity + rank
    place = jnp.arange(group_count * capacity, dtype=jnp.int32)
    source = jnp.sum(jnp.where(send_at[None, :] == place[:, None], slot[None, :], 0), axis=1)
    received = lax.all_to_all(
        jnp.take(blocks, source, axis=0), "pool", split_axis=0, concat_axis=0, tiled=True
    )
    return jnp.take(received, receive_at, axis=0)


def body(pair_rep, alignment, lengths, chain_breaks, shifts, *weights):
    group_count = lax.axis_size("pool")
    slot_count = pair_rep.shape[0]
    count = slot_count // 2
    capacity = max(2, (2 * slot_count + group_count - 1) // group_count)
    half = lax.axis_index("dap").astype(jnp.int32)
    swap = [(0, 1), (1, 0)]
    place = jnp.stack([half, (1 - half) * count, half * count, lax.axis_index("pool") * slot_count])
    place = place.astype(jnp.int32)
    alignment_proj, outer_proj = weights[:2]
    inner = alignment_proj.shape[1] // 2
    w_spread = spread_matrix(alignment.shape[1], inner)
    w_outer = (
        outer_proj.reshape(inner, inner, -1).transpose(1, 0, 2).reshape(outer_proj.shape)
    )
    other_pair = lax.ppermute(pair_rep, "dap", swap)
    own_sides, send_sides = project(place, lengths, alignment, alignment_proj.T, w_spread)
    other_sides = lax.ppermute(send_sides, "dap", swap)
    keep, send = update(
        place, lengths, chain_breaks, own_sides, other_sides, pair_rep, other_pair, (w_outer,) + weights[2:]
    )
    other = lax.ppermute(send, "dap", swap)
    move = exchange if group_count <= 8 else exchange_padded
    return move(half.reshape(1), shifts, keep, other, group_count, capacity)


def solution(mesh):
    step = sharded(mesh)
    return step


def sharded(mesh):
    return jax.shard_map(
        body,
        mesh=mesh,
        in_specs=(
            P(("screen", "pool"), "dap", None, None),
            P(("screen", "pool"), None, "dap", None),
            P("screen"),
            P("screen"),
            P("screen"),
        )
        + (P(),) * 9,
        out_specs=P(("screen", "pool"), "dap", None, None),
        check_vma=False,
    )
```

```python
import functools
import itertools

import jax
import jax.numpy as jnp
import numpy as np
from jax import lax
from jax.experimental import pallas as pl
from jax.experimental.pallas import tpu as pltpu
from jax.sharding import PartitionSpec as P

EPSILON = 1e-05
F32 = jnp.float32
BF16 = jnp.bfloat16
LANES = 128
AT_ONCE = 3
VMEM_LIMIT = 24 * 2**20
PROJECT_LIMIT = 64500000
WAYS = 4
PROJECT_WAYS = 3
OUTER_AFTER = 2
BLOCK = 4
OUTER_TILES = 4


def dot(left, right):
    return jnp.dot(left, right, preferred_element_type=F32)


def normalize_steps(values, scale, ones):
    width = values.shape[-1]
    values = values - jnp.sum(values, axis=-1, keepdims=True) * (1.0 / width)
    yield
    spread = dot((values * values).astype(BF16), ones[...])
    yield
    return (values * (lax.rsqrt(spread + width * EPSILON) * scale)).astype(BF16)


def interleave(streams):
    running = list(streams)
    while running:
        for stream in list(running):
            if next(stream, running) is running:
                running.remove(stream)


def lane_groups(inner):
    group = lax.broadcasted_iota(jnp.int32, (1, LANES), 1) // inner
    return [group == q for q in range(LANES // inner)]


def project_kernel(
    lengths_in,
    alignment_in,
    w_align_in,
    w_spread_in,
    own_ref,
    send_ref,
    lengths_ref,
    alignment,
    w_align,
    w_spread,
    side,
    rights,
    sems,
):
    slots, depth, rows, width = alignment.shape
    count = slots // 2
    inner = rights.shape[-1] // depth
    pieces = LANES // inner
    half = lax.axis_index("dap")
    mine, theirs = half * count, (1 - half) * count
    home = lax.axis_index("pool") * slots
    copies = [
        pltpu.make_async_copy(source, target, sems.at[n])
        for n, (source, target) in enumerate(
            ((w_align_in, w_align), (lengths_in, lengths_ref), (alignment_in, alignment), (w_spread_in, w_spread))
        )
    ]
    for copy in copies:
        copy.start()
    groups = lane_groups(inner)
    source = lax.broadcasted_iota(jnp.int32, (2 * inner, 2 * LANES), 0)
    target = lax.broadcasted_iota(jnp.int32, (2 * inner, 2 * LANES), 1)
    repeat = (source == (target // LANES) * inner + target % inner).astype(BF16)
    copies[0].wait()
    w_project = lax.dot_general(
        w_align[...], repeat, (((0,), (0,)), ((), ())), preferred_element_type=F32
    ).astype(BF16)
    residue = lax.broadcasted_iota(jnp.int32, (rows, 1), 0) + half * rows
    copies[1].wait()
    copies[2].wait()

    def one(index, start, which, way, out_ref):
        length = lengths_ref[home + start + index]
        values = alignment[start + index].astype(F32).reshape(depth * rows, width)
        values = values - jnp.sum(values, axis=-1, keepdims=True) * (1.0 / width)
        yield
        spread = jnp.sum(values * values, axis=-1, keepdims=True) * (1.0 / width)
        yield
        values = dot((values * lax.rsqrt(spread + EPSILON)).astype(BF16), w_project)
        yield
        values = values.reshape(depth, rows, 2 * LANES) * jnp.where(residue < length, 1.0, 0.0)
        side[way] = values[:, :, :LANES].reshape(depth * rows, LANES) * (1.0 / depth)
        tiles = []
        for tile in range(rows // pieces):
            piece = side[way, pl.ds(tile * pieces, depth, stride=rows), :]
            for q in range(1, pieces):
                other = side[way, pl.ds(tile * pieces + q, depth, stride=rows), :]
                piece = jnp.where(groups[q], other, piece)
            tiles.append(piece)
        out_ref[index, :depth] = jnp.concatenate(tiles, axis=1).astype(BF16)
        for tile in range(depth // pieces):
            piece = values[tile * pieces, :, LANES:]
            for q in range(1, pieces):
                piece = jnp.where(groups[q], values[tile * pieces + q, :, LANES:], piece)
            rights[which, index, :, LANES * tile : LANES * tile + LANES] = piece

    ways = side.shape[0] // 2

    def step(round_, carry):
        streams = []
        for way in range(ways):
            index = jnp.minimum(round_ * ways + way, count - 1)
            streams.append(one(index, mine, 0, 2 * way, own_ref))
            streams.append(one(index, theirs, 1, 2 * way + 1, send_ref))
        interleave(streams)
        return carry

    lax.fori_loop(0, (count + ways - 1) // ways, step, 0)
    copies[3].wait()
    flat = rights[...].reshape(slots * rows, depth * inner).astype(BF16)
    spread = dot(flat, w_spread[...]).reshape(2, count, rows, depth * inner).astype(BF16)
    parts = own_ref.shape[-1]
    for which, out_ref in enumerate((own_ref, send_ref)):
        for part in range(depth * inner // parts):
            out_ref[:, depth + part * rows : depth + part * rows + rows] = spread[
                which, :, :, part * parts : part * parts + parts
            ]


def project(lengths, alignment, w_align, w_spread):
    slots, depth, rows, _ = alignment.shape
    count = slots // 2
    inner = w_align.shape[0] // 2
    smem = pl.BlockSpec(memory_space=pltpu.SMEM)
    vmem = pl.BlockSpec(memory_space=pltpu.VMEM)
    hbm = pl.BlockSpec(memory_space=pltpu.HBM)
    out_shape = (count, 2 * depth, rows * inner)
    return pl.pallas_call(
        project_kernel,
        out_shape=(pltpu.VMEM(out_shape, BF16), jax.ShapeDtypeStruct(out_shape, BF16)),
        in_specs=[hbm, hbm, hbm, hbm],
        out_specs=(vmem, vmem),
        scratch_shapes=[
            pltpu.SMEM(lengths.shape, jnp.int32),
            pltpu.VMEM(alignment.shape, BF16),
            pltpu.VMEM(w_align.shape, BF16),
            pltpu.VMEM(w_spread.shape, BF16),
            pltpu.VMEM((2 * PROJECT_WAYS, depth * rows, LANES), F32),
            pltpu.VMEM((2, count, rows, depth * inner), F32),
            pltpu.SemaphoreType.DMA((4,)),
        ],
        compiler_params=pltpu.CompilerParams(vmem_limit_bytes=PROJECT_LIMIT),
        cost_estimate=pl.CostEstimate(flops=2 * 10**9, bytes_accessed=4 * 10**6, transcendentals=0),
        name="project",
    )(lengths, alignment, w_align, w_spread)


def update_kernel(
    lengths_ref,
    breaks_ref,
    own_sides,
    other_sides,
    pair,
    other_pair,
    w_outer,
    bias,
    out_ab,
    out_gate,
    out_proj,
    in_ab,
    in_gate,
    in_proj,
    keep_ref,
    send_ref,
    ones,
    updates_refs,
    stream_refs,
    gates_refs,
    sides_refs,
):
    count, rows, full, width = keep_ref.shape
    depth = own_sides.shape[1] // 2
    inner = own_sides.shape[2] // rows
    pieces = LANES // inner
    sets = inner // pieces
    hidden = out_proj.shape[0]
    half = lax.axis_index("dap")
    start = half * count
    home = lax.axis_index("pool") * pair.shape[0] + start
    low_is_own = half == 0
    groups = lane_groups(inner)
    zero = jnp.zeros((), BF16)
    place_j = lax.broadcasted_iota(jnp.int32, (full, 1), 0)
    ones[...] = jnp.ones_like(ones)
    unit = 0.5 * width**0.5
    pairs = full * full
    ways = updates_refs.shape[0]
    within, across = bias[0:1].astype(F32), bias[1:2].astype(F32)

    def clamp(index):
        return jnp.minimum(index, count - 1)

    def outer_update(way, step):
        own, other = own_sides[step], other_sides[step]
        low = jnp.where(low_is_own, own, other)
        high = jnp.where(low_is_own, other, own)
        right = jnp.concatenate(
            [
                jnp.concatenate(
                    [side[depth + rows * part : depth + rows * part + rows] for part in range(depth // rows)],
                    axis=1,
                )
                for side in (low, high)
            ],
            axis=0,
        )
        per = LANES // (pieces * depth)
        tiles = []
        for c2 in range(sets):
            tile = right[:, c2 // per * LANES : c2 // per * LANES + LANES]
            turn = c2 % per * pieces * depth
            tiles.append(pltpu.roll(tile, LANES - turn, 1) if turn else tile)
        right = jnp.concatenate(tiles, axis=0)
        yield
        tail = jnp.zeros((LANES - pieces * depth, 2 * LANES), BF16)
        lefts = rows // pieces
        parts = []
        for tile in range(full // pieces):
            source = low if tile < lefts else high
            at = tile % lefts * LANES
            left = source[:depth, at : at + LANES]
            turned = [left] + [pltpu.roll(left, inner * turn, 1) for turn in range(1, pieces)]
            for first_p in range(0, pieces, 2):
                column = [
                    jnp.concatenate(
                        [jnp.where(groups[q], turned[(q - p) % pieces], zero) for q in range(pieces)], axis=0
                    )
                    for p in (first_p, first_p + 1)
                ]
                stacked = jnp.concatenate([jnp.concatenate(column, axis=1), tail], axis=0)
                product = dot(right, stacked).astype(BF16)
                for k in range(2):
                    parts.append(
                        jnp.concatenate(
                            [
                                product[full * g : full * g + full, LANES * k : LANES * k + LANES]
                                for g in range(sets)
                            ],
                            axis=1,
                        )
                    )
                yield
            if (tile + 1) % OUTER_TILES == 0:
                span = len(parts) * full
                start_row = (tile + 1) * pieces * full - span
                updates_refs[way, start_row : start_row + span] = dot(
                    jnp.concatenate(parts, axis=0), w_outer[...]
                )
                parts = []
                yield

    def row_masks(length):
        column = jnp.where(place_j < length, 1.0, 0.0)
        return jnp.concatenate([jnp.where(i < length, column, 0.0) for i in range(full)], axis=0)

    def sides(values, inside, w_ab, w_gate, way, first):
        x = yield from normalize_steps(values, inside * unit, ones)
        yield
        for n in range(2):
            projected = dot(x, w_ab[:, 2 * hidden * n : 2 * hidden * n + 2 * hidden])
            sides_refs[way, first + n] = (jnp.tanh(projected[:, hidden:]) + 1.0) * projected[:, :hidden]
            yield
        gates_refs[way] = jnp.tanh(dot(x, w_gate[...])) + 1.0

    def contract(row_of, column_of):
        parts = []
        for first in range(0, full, BLOCK):
            totals = [None] * BLOCK
            for k in range(full):
                column = column_of(k)
                for i in range(BLOCK):
                    term = row_of(first + i, k) * column
                    totals[i] = term if totals[i] is None else totals[i] + term
            parts += totals
            yield
        return jnp.concatenate(parts, axis=0)

    def begin(step, way):
        stop = breaks_ref[home + step]
        head = place_j < stop
        terms = (jnp.where(head, within, across), jnp.where(head, across, within))
        chain = jnp.concatenate([jnp.where(i < stop, terms[0], terms[1]) for i in range(full)], axis=0)
        own, other = pair[start + step], other_pair[start + step]
        block = jnp.concatenate(
            [jnp.where(low_is_own, own, other), jnp.where(low_is_own, other, own)], axis=0
        )
        z1 = block.reshape(pairs, width).astype(F32) + updates_refs[way] + chain
        stream_refs[way] = z1
        yield
        yield from sides(z1, row_masks(lengths_ref[home + step]), out_ab, out_gate, way, 0)

    def middle(step, way):
        t = yield from contract(
            lambda i, k: sides_refs[way, 0, pl.ds(full * i + k, 1), :],
            lambda k: sides_refs[way, 1, pl.ds(k, full, stride=full), :],
        )
        u = yield from normalize_steps(t, unit, ones)
        yield
        z2 = stream_refs[way] + gates_refs[way] * dot(u, out_proj[...])
        z2 = z2.astype(BF16).astype(F32)
        stream_refs[way] = z2
        yield
        yield from sides(z2, row_masks(lengths_ref[home + step]), in_ab, in_gate, way, 2)

    def last(step, way):
        t = yield from contract(
            lambda i, k: sides_refs[way, 3, pl.ds(full * k + i, 1), :],
            lambda k: sides_refs[way, 2, full * k : full * k + full],
        )
        u = yield from normalize_steps(t, unit, ones)
        yield
        y3 = stream_refs[way] + gates_refs[way] * dot(u, in_proj[...])
        y3 = (y3 * row_masks(lengths_ref[home + step])).astype(BF16)
        low = y3[: rows * full].reshape(rows, full, width)
        high = y3[rows * full :].reshape(rows, full, width)
        keep_ref[step] = jnp.where(low_is_own, low, high)
        send_ref[step] = jnp.where(low_is_own, high, low)

    def whole(step, way):
        yield from begin(step, way)
        yield
        yield from middle(step, way)
        yield
        yield from last(step, way)

    def later(streams, ticks):
        for _ in range(ticks):
            yield
        for stream in streams:
            yield from stream

    def round_of(steps, ahead):
        streams = [whole(step, way) for way, step in enumerate(steps)]
        outers = [outer_update(way, step) for way, step in enumerate(ahead)]
        interleave(streams + [later(outers, OUTER_AFTER)])

    def both(round_, carry):
        base = round_ * ways
        round_of([base + way for way in range(ways)], [clamp(base + ways + way) for way in range(ways)])
        return carry

    rounds = (count + ways - 1) // ways
    interleave([outer_update(way, clamp(way)) for way in range(ways)])
    lax.fori_loop(0, rounds - 1, both, 0)
    round_of(list(range((rounds - 1) * ways, count)), [])


def update(lengths, breaks, own_sides, other_sides, pair, other_pair, weights):
    outer_proj, chain_bias, out_ab, out_gate, out_proj, in_ab, in_gate, in_proj = weights
    count = own_sides.shape[0]
    _, full, width = pair.shape[1:]
    smem = pl.BlockSpec(memory_space=pltpu.SMEM)
    vmem = pl.BlockSpec(memory_space=pltpu.VMEM)
    shape = jax.ShapeDtypeStruct((count,) + pair.shape[1:], BF16)
    pairs, hidden = full * full, out_proj.shape[0]
    return pl.pallas_call(
        update_kernel,
        out_shape=(shape, shape),
        in_specs=[smem] * 2 + [vmem] * 12,
        out_specs=(vmem, vmem),
        scratch_shapes=[
            pltpu.VMEM((width, width), BF16),
            pltpu.VMEM((WAYS, pairs, width), F32),
            pltpu.VMEM((WAYS, pairs, width), F32),
            pltpu.VMEM((WAYS, pairs, width), F32),
            pltpu.VMEM((WAYS, 4, pairs, hidden), F32),
        ],
        compiler_params=pltpu.CompilerParams(vmem_limit_bytes=VMEM_LIMIT),
        cost_estimate=pl.CostEstimate(flops=10**10, bytes_accessed=4 * 10**6, transcendentals=0),
        name="pair_update",
    )(
        lengths,
        breaks,
        own_sides,
        other_sides,
        pair,
        other_pair,
        outer_proj,
        chain_bias,
        out_ab,
        out_gate,
        out_proj,
        in_ab,
        in_gate,
        in_proj,
    )


def spread_matrix(depth, inner):
    pieces = LANES // inner
    r, c2 = np.divmod(np.arange(depth * inner), inner)
    matrix = np.zeros((depth * inner, depth * inner), np.float32)
    matrix[np.arange(depth * inner), (c2 // pieces) * pieces * depth + (c2 % pieces) * depth + r] = 1.0
    return jnp.asarray(matrix, BF16)


def build_tables(shifts_ref, table, counts, capacity):
    slots, groups = shifts_ref.shape[0], counts.shape[0]
    for v in range(groups):
        counts[v] = 0

    def step(slot, carry):
        v = shifts_ref[slot]
        rank = counts[v]
        table[v * capacity + rank] = slot
        counts[v] = rank + 1
        return carry

    lax.fori_loop(0, slots, step, 0)


def list_large(counts, large, low):
    for k in range(large.shape[0]):
        large[k] = 0
    found = jnp.int32(0)
    for v in range(1, counts.shape[0]):
        many = counts[v] > low

        @pl.when(many)
        def _(found=found, v=v):
            large[found] = v

        found = found + many.astype(jnp.int32)
    return found


def subsets(groups, most):
    return [c for n in range(most + 1) for c in itertools.combinations(range(1, groups), n)]


def plan_kernel(low, capacity, shifts_ref, table, counts, large, branch):
    groups = counts.shape[0]
    build_tables(shifts_ref, table, counts, capacity)
    found = list_large(counts, large, low)
    taken = [large[k] for k in range(min(AT_ONCE, large.shape[0]))]
    index = jnp.int32(0)
    for n, subset in enumerate(subsets(groups, AT_ONCE)):
        same = functools.reduce(
            jnp.logical_and, [t == (subset[k] if k < len(subset) else 0) for k, t in enumerate(taken)]
        )
        index = jnp.where(same, n, index)
    branch[0] = index
    branch[1] = found
    for k in range(AT_ONCE, large.shape[0]):
        branch[2 + k - AT_ONCE] = large[k]


def pack_kernel(low, capacity, table, counts, large, branch, keep, other, *outs):
    groups = counts.shape[0]
    found = branch[1]
    statics, rests = outs[: groups - 1], outs[groups - 1 :]
    count = keep.shape[0]
    base = lax.axis_index("dap") * count

    def fetch(v, rank):
        slot = jnp.where(rank < counts[v], table[v * capacity + rank], 0)
        at = slot - base
        mine = (at >= 0) & (at < count)
        near = keep[jnp.clip(at, 0, count - 1)]
        far = other[jnp.clip(slot - (count - base), 0, count - 1)]
        return jnp.where(mine, near, far)

    for v in range(1, groups):
        for rank in range(low):
            statics[v - 1][rank] = fetch(v, rank)
    for k, rest in enumerate(rests):
        @pl.when(k < found)
        def _(k=k, rest=rest):
            v = large[k]
            for rank in range(low, capacity):
                rest[rank - low] = fetch(v, rank)


def unpack_kernel(low, capacity, table, counts, large, branch, keep, other, *refs):
    groups = counts.shape[0]
    found = branch[1]
    out, sem = refs[-2:]
    statics, rests = refs[: groups - 1], refs[groups - 1 : -2]
    count = keep.shape[0]
    base = lax.axis_index("dap") * count

    def put(source, slot):
        pltpu.make_async_copy(source, out.at[slot], sem).start()

    for v in range(1, groups):
        for rank in range(low):

            @pl.when(rank < counts[v])
            def _(v=v, rank=rank):
                put(statics[v - 1].at[rank], table[v * capacity + rank])

    def step(rank, carry):
        slot = table[rank]
        at = slot - base
        mine = (at >= 0) & (at < count)

        @pl.when(mine)
        def _():
            put(keep.at[jnp.clip(at, 0, count - 1)], slot)

        @pl.when(jnp.logical_not(mine))
        def _():
            put(other.at[jnp.clip(slot - (count - base), 0, count - 1)], slot)

        return carry

    lax.fori_loop(0, counts[0], step, 0)
    for k, rest in enumerate(rests):
        for rank in range(low, capacity):

            @pl.when((k < found) & (rank < counts[large[k]]))
            def _(k=k, rank=rank, rest=rest):
                put(rest.at[rank - low], table[large[k] * capacity + rank])

    pltpu.make_async_copy(out, out, sem).wait()


def sizes(slots, group_count, capacity):
    low = capacity // 2
    return low, max(min(slots // (low + 1), group_count - 1), AT_ONCE)


def plan(shifts, group_count, capacity):
    low, most = sizes(shifts.shape[0], group_count, capacity)
    smem = pl.BlockSpec(memory_space=pltpu.SMEM)
    lengths = (group_count * capacity, group_count, most, 2 + most - AT_ONCE)
    return pl.pallas_call(
        functools.partial(plan_kernel, low, capacity),
        out_shape=[jax.ShapeDtypeStruct((length,), jnp.int32) for length in lengths],
        in_specs=[smem],
        out_specs=[smem] * 4,
        cost_estimate=pl.CostEstimate(flops=10**6, bytes_accessed=10**6, transcendentals=0),
        name="plan",
    )(shifts)


def exchange(tables, keep, other, slots, group_count, capacity):
    low, most = sizes(slots, group_count, capacity)
    branch = tables[-1]
    block = keep.shape[1:]
    smem = pl.BlockSpec(memory_space=pltpu.SMEM)
    vmem = pl.BlockSpec(memory_space=pltpu.VMEM)
    anywhere = pl.BlockSpec(memory_space=pl.ANY)
    params = pltpu.CompilerParams(vmem_limit_bytes=VMEM_LIMIT)
    low_shape = jax.ShapeDtypeStruct((low,) + block, BF16)
    high_shape = jax.ShapeDtypeStruct((capacity - low,) + block, BF16)
    packed = pl.pallas_call(
        functools.partial(pack_kernel, low, capacity),
        out_shape=[low_shape] * (group_count - 1) + [high_shape] * most,
        in_specs=[smem] * 4 + [vmem, vmem],
        out_specs=[vmem] * (group_count - 1 + most),
        compiler_params=params,
        name="pack",
    )(*tables, keep, other)
    statics = packed[: group_count - 1]
    rests = packed[group_count - 1 :]

    def move(block, v):
        return lax.ppermute(block, "pool", [(g, (g + v) % group_count) for g in range(group_count)])

    arrived = {}
    for v in range(1, group_count):
        arrived[v] = move(statics[v - 1], v)
    arrived = [arrived[v] for v in range(1, group_count)]

    def choice(subset):
        def run(*blocks):
            moved = [move(block, v) for block, v in zip(blocks, subset)]
            return tuple(moved) + blocks[len(subset) :]

        return run

    late = list(
        lax.switch(
            branch[0], [choice(subset) for subset in subsets(group_count, AT_ONCE)], *rests[:AT_ONCE]
        )
    )
    if most > AT_ONCE:

        def more(*blocks):
            singles = [choice(subset) for subset in subsets(group_count, 1)]
            return tuple(lax.switch(branch[2 + k], singles, block)[0] for k, block in enumerate(blocks))

        late += lax.cond(branch[1] > AT_ONCE, more, lambda *blocks: blocks, *rests[AT_ONCE:])
    return pl.pallas_call(
        functools.partial(unpack_kernel, low, capacity),
        out_shape=jax.ShapeDtypeStruct((slots,) + block, BF16),
        in_specs=[smem] * 4 + [vmem] * (2 + group_count - 1 + most),
        out_specs=anywhere,
        scratch_shapes=[pltpu.SemaphoreType.DMA],
        compiler_params=params,
        name="unpack",
    )(*tables, keep, other, *arrived, *late)


def exchange_padded(half, shifts, keep, other, group_count, capacity):
    slots = shifts.shape[0]
    my_group = lax.axis_index("pool")
    blocks = jnp.where(
        half == 0, jnp.concatenate([keep, other], axis=0), jnp.concatenate([other, keep], axis=0)
    )
    slot = jnp.arange(slots, dtype=jnp.int32)
    earlier = (shifts[None, :] == shifts[:, None]) & (slot[None, :] < slot[:, None])
    rank = jnp.sum(earlier.astype(jnp.int32), axis=1)
    send_at = (my_group + shifts) % group_count * capacity + rank
    receive_at = (my_group - shifts) % group_count * capacity + rank
    place = jnp.arange(group_count * capacity, dtype=jnp.int32)
    source = jnp.sum(jnp.where(send_at[None, :] == place[:, None], slot[None, :], 0), axis=1)
    received = lax.all_to_all(
        jnp.take(blocks, source, axis=0), "pool", split_axis=0, concat_axis=0, tiled=True
    )
    return jnp.take(received, receive_at, axis=0)


def body(pair_rep, alignment, lengths, chain_breaks, shifts, *weights):
    group_count = lax.axis_size("pool")
    slot_count = pair_rep.shape[0]
    capacity = max(2, (2 * slot_count + group_count - 1) // group_count)
    half = lax.axis_index("dap").astype(jnp.int32)
    swap = [(0, 1), (1, 0)]
    alignment_proj, outer_proj = weights[:2]
    inner = alignment_proj.shape[1] // 2
    w_spread = spread_matrix(alignment.shape[1], inner)
    w_outer = (
        outer_proj.reshape(inner, inner, -1).transpose(1, 0, 2).reshape(outer_proj.shape)
    )
    other_pair = lax.ppermute(pair_rep, "dap", swap)
    own_sides, send_sides = project(lengths, alignment, alignment_proj.T, w_spread)
    other_sides = lax.ppermute(send_sides, "dap", swap)
    keep, send = update(
        lengths, chain_breaks, own_sides, other_sides, pair_rep, other_pair, (w_outer,) + weights[2:]
    )
    if group_count > 8:
        other = lax.ppermute(send, "dap", swap)
        return exchange_padded(half, shifts, keep, other, group_count, capacity)
    tables = plan(shifts, group_count, capacity)
    other = lax.ppermute(send, "dap", swap)
    return exchange(tables, keep, other, slot_count, group_count, capacity)


def solution(mesh):
    step = sharded(mesh)
    return step


def sharded(mesh):
    return jax.shard_map(
        body,
        mesh=mesh,
        in_specs=(
            P(("screen", "pool"), "dap", None, None),
            P(("screen", "pool"), None, "dap", None),
            P("screen"),
            P("screen"),
            P("screen"),
        )
        + (P(),) * 9,
        out_specs=P(("screen", "pool"), "dap", None, None),
        check_vma=False,
    )
```

```python
import functools
import itertools

import jax
import jax.numpy as jnp
import numpy as np
from jax import lax
from jax.experimental import pallas as pl
from jax.experimental.pallas import tpu as pltpu
from jax.sharding import PartitionSpec as P

EPSILON = 1e-05
F32 = jnp.float32
BF16 = jnp.bfloat16
LANES = 128
AT_ONCE = 3
VMEM_LIMIT = 24 * 2**20
PROJECT_LIMIT = 64500000
WAYS = 4
PROJECT_WAYS = 3
OUTER_AFTER = 2
BLOCK = 4
OUTER_TILES = 4


def dot(left, right):
    return jnp.dot(left, right, preferred_element_type=F32)


def normalize_steps(values, scale, ones):
    width = values.shape[-1]
    values = values - jnp.sum(values, axis=-1, keepdims=True) * (1.0 / width)
    yield
    spread = dot((values * values).astype(BF16), ones[...])
    yield
    return (values * (lax.rsqrt(spread + width * EPSILON) * scale)).astype(BF16)


def interleave(streams):
    running = list(streams)
    while running:
        for stream in list(running):
            if next(stream, running) is running:
                running.remove(stream)


def lane_groups(inner):
    group = lax.broadcasted_iota(jnp.int32, (1, LANES), 1) // inner
    return [group == q for q in range(LANES // inner)]


def project_kernel(
    lengths_in,
    alignment_in,
    w_align_in,
    w_spread_in,
    own_ref,
    send_ref,
    lengths_ref,
    alignment,
    w_align,
    w_spread,
    side,
    rights,
    sems,
):
    slots, depth, rows, width = alignment.shape
    count = slots // 2
    inner = rights.shape[-1] // depth
    pieces = LANES // inner
    half = lax.axis_index("dap")
    mine, theirs = half * count, (1 - half) * count
    home = lax.axis_index("pool") * slots
    copies = [
        pltpu.make_async_copy(source, target, sems.at[n])
        for n, (source, target) in enumerate(
            ((w_align_in, w_align), (lengths_in, lengths_ref), (alignment_in, alignment), (w_spread_in, w_spread))
        )
    ]
    for copy in copies:
        copy.start()
    groups = lane_groups(inner)
    source = lax.broadcasted_iota(jnp.int32, (2 * inner, 2 * LANES), 0)
    target = lax.broadcasted_iota(jnp.int32, (2 * inner, 2 * LANES), 1)
    repeat = (source == (target // LANES) * inner + target % inner).astype(BF16)
    copies[0].wait()
    w_project = lax.dot_general(
        w_align[...], repeat, (((0,), (0,)), ((), ())), preferred_element_type=F32
    ).astype(BF16)
    residue = lax.broadcasted_iota(jnp.int32, (rows, 1), 0) + half * rows
    copies[1].wait()
    copies[2].wait()

    def one(index, start, which, way, out_ref):
        length = lengths_ref[home + start + index]
        values = alignment[start + index].astype(F32).reshape(depth * rows, width)
        values = values - jnp.sum(values, axis=-1, keepdims=True) * (1.0 / width)
        yield
        spread = jnp.sum(values * values, axis=-1, keepdims=True) * (1.0 / width)
        yield
        values = dot((values * lax.rsqrt(spread + EPSILON)).astype(BF16), w_project)
        yield
        values = values.reshape(depth, rows, 2 * LANES) * jnp.where(residue < length, 1.0, 0.0)
        side[way] = values[:, :, :LANES].reshape(depth * rows, LANES) * (1.0 / depth)
        tiles = []
        for tile in range(rows // pieces):
            piece = side[way, pl.ds(tile * pieces, depth, stride=rows), :]
            for q in range(1, pieces):
                other = side[way, pl.ds(tile * pieces + q, depth, stride=rows), :]
                piece = jnp.where(groups[q], other, piece)
            tiles.append(piece)
        out_ref[index, :depth] = jnp.concatenate(tiles, axis=1).astype(BF16)
        for tile in range(depth // pieces):
            piece = values[tile * pieces, :, LANES:]
            for q in range(1, pieces):
                piece = jnp.where(groups[q], values[tile * pieces + q, :, LANES:], piece)
            rights[which, index, :, LANES * tile : LANES * tile + LANES] = piece

    ways = side.shape[0] // 2

    def step(round_, carry):
        streams = []
        for way in range(ways):
            index = jnp.minimum(round_ * ways + way, count - 1)
            streams.append(one(index, mine, 0, 2 * way, own_ref))
            streams.append(one(index, theirs, 1, 2 * way + 1, send_ref))
        interleave(streams)
        return carry

    lax.fori_loop(0, (count + ways - 1) // ways, step, 0)
    copies[3].wait()
    flat = rights[...].reshape(slots * rows, depth * inner).astype(BF16)
    spread = dot(flat, w_spread[...]).reshape(2, count, rows, depth * inner).astype(BF16)
    parts = own_ref.shape[-1]
    for which, out_ref in enumerate((own_ref, send_ref)):
        for part in range(depth * inner // parts):
            out_ref[:, depth + part * rows : depth + part * rows + rows] = spread[
                which, :, :, part * parts : part * parts + parts
            ]


def project(lengths, alignment, w_align, w_spread):
    slots, depth, rows, _ = alignment.shape
    count = slots // 2
    inner = w_align.shape[0] // 2
    smem = pl.BlockSpec(memory_space=pltpu.SMEM)
    vmem = pl.BlockSpec(memory_space=pltpu.VMEM)
    hbm = pl.BlockSpec(memory_space=pltpu.HBM)
    out_shape = (count, 2 * depth, rows * inner)
    return pl.pallas_call(
        project_kernel,
        out_shape=(pltpu.VMEM(out_shape, BF16), jax.ShapeDtypeStruct(out_shape, BF16)),
        in_specs=[hbm, hbm, hbm, hbm],
        out_specs=(vmem, vmem),
        scratch_shapes=[
            pltpu.SMEM(lengths.shape, jnp.int32),
            pltpu.VMEM(alignment.shape, BF16),
            pltpu.VMEM(w_align.shape, BF16),
            pltpu.VMEM(w_spread.shape, BF16),
            pltpu.VMEM((2 * PROJECT_WAYS, depth * rows, LANES), F32),
            pltpu.VMEM((2, count, rows, depth * inner), F32),
            pltpu.SemaphoreType.DMA((4,)),
        ],
        compiler_params=pltpu.CompilerParams(vmem_limit_bytes=PROJECT_LIMIT),
        cost_estimate=pl.CostEstimate(flops=2 * 10**9, bytes_accessed=4 * 10**6, transcendentals=0),
        name="project",
    )(lengths, alignment, w_align, w_spread)


def update_kernel(
    lengths_ref,
    breaks_ref,
    own_sides,
    other_sides,
    pair,
    other_pair,
    w_outer,
    bias,
    out_ab,
    out_gate,
    out_proj,
    in_ab,
    in_gate,
    in_proj,
    keep_ref,
    send_ref,
    ones,
    updates_refs,
    stream_refs,
    gates_refs,
    sides_refs,
):
    count, rows, full, width = keep_ref.shape
    depth = own_sides.shape[1] // 2
    inner = own_sides.shape[2] // rows
    pieces = LANES // inner
    sets = inner // pieces
    hidden = out_proj.shape[0]
    half = lax.axis_index("dap")
    start = half * count
    home = lax.axis_index("pool") * pair.shape[0] + start
    low_is_own = half == 0
    groups = lane_groups(inner)
    zero = jnp.zeros((), BF16)
    place_j = lax.broadcasted_iota(jnp.int32, (full, 1), 0)
    ones[...] = jnp.ones_like(ones)
    unit = 0.5 * width**0.5
    pairs = full * full
    ways = updates_refs.shape[0]
    within, across = bias[0:1].astype(F32), bias[1:2].astype(F32)

    def clamp(index):
        return jnp.minimum(index, count - 1)

    def outer_update(way, step):
        own, other = own_sides[step], other_sides[step]
        low = jnp.where(low_is_own, own, other)
        high = jnp.where(low_is_own, other, own)
        right = jnp.concatenate(
            [
                jnp.concatenate(
                    [side[depth + rows * part : depth + rows * part + rows] for part in range(depth // rows)],
                    axis=1,
                )
                for side in (low, high)
            ],
            axis=0,
        )
        per = LANES // (pieces * depth)
        tiles = []
        for c2 in range(sets):
            tile = right[:, c2 // per * LANES : c2 // per * LANES + LANES]
            turn = c2 % per * pieces * depth
            tiles.append(pltpu.roll(tile, LANES - turn, 1) if turn else tile)
        right = jnp.concatenate(tiles, axis=0)
        yield
        tail = jnp.zeros((LANES - pieces * depth, 2 * LANES), BF16)
        lefts = rows // pieces
        parts = []
        for tile in range(full // pieces):
            source = low if tile < lefts else high
            at = tile % lefts * LANES
            left = source[:depth, at : at + LANES]
            turned = [left] + [pltpu.roll(left, inner * turn, 1) for turn in range(1, pieces)]
            for first_p in range(0, pieces, 2):
                column = [
                    jnp.concatenate(
                        [jnp.where(groups[q], turned[(q - p) % pieces], zero) for q in range(pieces)], axis=0
                    )
                    for p in (first_p, first_p + 1)
                ]
                stacked = jnp.concatenate([jnp.concatenate(column, axis=1), tail], axis=0)
                product = dot(right, stacked).astype(BF16)
                for k in range(2):
                    parts.append(
                        jnp.concatenate(
                            [
                                product[full * g : full * g + full, LANES * k : LANES * k + LANES]
                                for g in range(sets)
                            ],
                            axis=1,
                        )
                    )
                yield
            if (tile + 1) % OUTER_TILES == 0:
                span = len(parts) * full
                start_row = (tile + 1) * pieces * full - span
                updates_refs[way, start_row : start_row + span] = dot(
                    jnp.concatenate(parts, axis=0), w_outer[...]
                )
                parts = []
                yield

    def row_masks(length):
        column = jnp.where(place_j < length, 1.0, 0.0)
        return jnp.concatenate([jnp.where(i < length, column, 0.0) for i in range(full)], axis=0)

    def sides(values, inside, w_ab, w_gate, way, first):
        x = yield from normalize_steps(values, inside * unit, ones)
        yield
        for n in range(2):
            projected = dot(x, w_ab[:, 2 * hidden * n : 2 * hidden * n + 2 * hidden])
            sides_refs[way, first + n] = (jnp.tanh(projected[:, hidden:]) + 1.0) * projected[:, :hidden]
            yield
        gates_refs[way] = jnp.tanh(dot(x, w_gate[...])) + 1.0

    def contract(row_of, column_of):
        parts = []
        for first in range(0, full, BLOCK):
            totals = [None] * BLOCK
            for k in range(full):
                column = column_of(k)
                for i in range(BLOCK):
                    term = row_of(first + i, k) * column
                    totals[i] = term if totals[i] is None else totals[i] + term
            parts += totals
            yield
        return jnp.concatenate(parts, axis=0)

    def begin(step, way):
        stop = breaks_ref[home + step]
        head = place_j < stop
        terms = (jnp.where(head, within, across), jnp.where(head, across, within))
        chain = jnp.concatenate([jnp.where(i < stop, terms[0], terms[1]) for i in range(full)], axis=0)
        own, other = pair[start + step], other_pair[start + step]
        block = jnp.concatenate(
            [jnp.where(low_is_own, own, other), jnp.where(low_is_own, other, own)], axis=0
        )
        z1 = block.reshape(pairs, width).astype(F32) + updates_refs[way] + chain
        stream_refs[way] = z1
        yield
        yield from sides(z1, row_masks(lengths_ref[home + step]), out_ab, out_gate, way, 0)

    def middle(step, way):
        t = yield from contract(
            lambda i, k: sides_refs[way, 0, pl.ds(full * i + k, 1), :],
            lambda k: sides_refs[way, 1, pl.ds(k, full, stride=full), :],
        )
        u = yield from normalize_steps(t, unit, ones)
        yield
        z2 = stream_refs[way] + gates_refs[way] * dot(u, out_proj[...])
        z2 = z2.astype(BF16).astype(F32)
        stream_refs[way] = z2
        yield
        yield from sides(z2, row_masks(lengths_ref[home + step]), in_ab, in_gate, way, 2)

    def last(step, way):
        t = yield from contract(
            lambda i, k: sides_refs[way, 3, pl.ds(full * k + i, 1), :],
            lambda k: sides_refs[way, 2, full * k : full * k + full],
        )
        u = yield from normalize_steps(t, unit, ones)
        yield
        y3 = stream_refs[way] + gates_refs[way] * dot(u, in_proj[...])
        y3 = (y3 * row_masks(lengths_ref[home + step])).astype(BF16)
        low = y3[: rows * full].reshape(rows, full, width)
        high = y3[rows * full :].reshape(rows, full, width)
        keep_ref[step] = jnp.where(low_is_own, low, high)
        send_ref[step] = jnp.where(low_is_own, high, low)

    def whole(step, way):
        yield from begin(step, way)
        yield
        yield from middle(step, way)
        yield
        yield from last(step, way)

    def later(streams, ticks):
        for _ in range(ticks):
            yield
        for stream in streams:
            yield from stream

    def round_of(steps, ahead):
        streams = [whole(step, way) for way, step in enumerate(steps)]
        outers = [outer_update(way, step) for way, step in enumerate(ahead)]
        interleave(streams + [later(outers, OUTER_AFTER)])

    def both(round_, carry):
        base = round_ * ways
        round_of([base + way for way in range(ways)], [clamp(base + ways + way) for way in range(ways)])
        return carry

    rounds = (count + ways - 1) // ways
    interleave([outer_update(way, clamp(way)) for way in range(ways)])
    lax.fori_loop(0, rounds - 1, both, 0)
    round_of(list(range((rounds - 1) * ways, count)), [])


def update(lengths, breaks, own_sides, other_sides, pair, other_pair, weights):
    outer_proj, chain_bias, out_ab, out_gate, out_proj, in_ab, in_gate, in_proj = weights
    count = own_sides.shape[0]
    _, full, width = pair.shape[1:]
    smem = pl.BlockSpec(memory_space=pltpu.SMEM)
    vmem = pl.BlockSpec(memory_space=pltpu.VMEM)
    shape = jax.ShapeDtypeStruct((count,) + pair.shape[1:], BF16)
    pairs, hidden = full * full, out_proj.shape[0]
    return pl.pallas_call(
        update_kernel,
        out_shape=(shape, shape),
        in_specs=[smem] * 2 + [vmem] * 12,
        out_specs=(vmem, vmem),
        scratch_shapes=[
            pltpu.VMEM((width, width), BF16),
            pltpu.VMEM((WAYS, pairs, width), F32),
            pltpu.VMEM((WAYS, pairs, width), F32),
            pltpu.VMEM((WAYS, pairs, width), F32),
            pltpu.VMEM((WAYS, 4, pairs, hidden), F32),
        ],
        compiler_params=pltpu.CompilerParams(vmem_limit_bytes=VMEM_LIMIT),
        cost_estimate=pl.CostEstimate(flops=10**10, bytes_accessed=4 * 10**6, transcendentals=0),
        name="pair_update",
    )(
        lengths,
        breaks,
        own_sides,
        other_sides,
        pair,
        other_pair,
        outer_proj,
        chain_bias,
        out_ab,
        out_gate,
        out_proj,
        in_ab,
        in_gate,
        in_proj,
    )


def spread_matrix(depth, inner):
    pieces = LANES // inner
    r, c2 = np.divmod(np.arange(depth * inner), inner)
    matrix = np.zeros((depth * inner, depth * inner), np.float32)
    matrix[np.arange(depth * inner), (c2 // pieces) * pieces * depth + (c2 % pieces) * depth + r] = 1.0
    return jnp.asarray(matrix, BF16)


def build_tables(shifts_ref, table, counts, capacity):
    slots, groups = shifts_ref.shape[0], counts.shape[0]
    for v in range(groups):
        counts[v] = 0

    def step(slot, carry):
        v = shifts_ref[slot]
        rank = counts[v]
        table[v * capacity + rank] = slot
        counts[v] = rank + 1
        return carry

    lax.fori_loop(0, slots, step, 0)


def list_large(counts, large, low):
    for k in range(large.shape[0]):
        large[k] = 0
    found = jnp.int32(0)
    for v in range(1, counts.shape[0]):
        many = counts[v] > low

        @pl.when(many)
        def _(found=found, v=v):
            large[found] = v

        found = found + many.astype(jnp.int32)
    return found


def subsets(groups, most):
    return [c for n in range(most + 1) for c in itertools.combinations(range(1, groups), n)]


def split_plan(plan_ref, groups, capacity, most):
    views, start = [], 0
    for length in plan_lengths(groups, capacity, most):
        views.append(plan_ref.at[pl.ds(start, length)])
        start += length
    return views


def plan_lengths(groups, capacity, most):
    return groups * capacity, groups, most, 2 + most - AT_ONCE


def plan_kernel(low, capacity, groups, most, shifts_ref, plan_ref):
    table, counts, large, branch = split_plan(plan_ref, groups, capacity, most)
    build_tables(shifts_ref, table, counts, capacity)
    found = list_large(counts, large, low)
    taken = [large[k] for k in range(min(AT_ONCE, large.shape[0]))]
    index = jnp.int32(0)
    for n, subset in enumerate(subsets(groups, AT_ONCE)):
        same = functools.reduce(
            jnp.logical_and, [t == (subset[k] if k < len(subset) else 0) for k, t in enumerate(taken)]
        )
        index = jnp.where(same, n, index)
    branch[0] = index
    branch[1] = found
    for k in range(AT_ONCE, large.shape[0]):
        branch[2 + k - AT_ONCE] = large[k]


def pack_kernel(low, capacity, groups, most, plan_ref, keep, other, *outs):
    table, counts, large, branch = split_plan(plan_ref, groups, capacity, most)
    found = branch[1]
    statics, rests = outs[: groups - 1], outs[groups - 1 :]
    count = keep.shape[0]
    base = lax.axis_index("dap") * count

    def fetch(v, rank):
        slot = jnp.where(rank < counts[v], table[v * capacity + rank], 0)
        at = slot - base
        mine = (at >= 0) & (at < count)
        near = keep[jnp.clip(at, 0, count - 1)]
        far = other[jnp.clip(slot - (count - base), 0, count - 1)]
        return jnp.where(mine, near, far)

    for v in range(1, groups):
        for rank in range(low):
            statics[v - 1][rank] = fetch(v, rank)
    for k, rest in enumerate(rests):
        @pl.when(k < found)
        def _(k=k, rest=rest):
            v = large[k]
            for rank in range(low, capacity):
                rest[rank - low] = fetch(v, rank)


def unpack_kernel(low, capacity, groups, most, plan_ref, keep, other, *refs):
    table, counts, large, branch = split_plan(plan_ref, groups, capacity, most)
    found = branch[1]
    out, sem = refs[-2:]
    statics, rests = refs[: groups - 1], refs[groups - 1 : -2]
    count = keep.shape[0]
    base = lax.axis_index("dap") * count

    def put(source, slot):
        pltpu.make_async_copy(source, out.at[slot], sem).start()

    for v in range(1, groups):
        for rank in range(low):

            @pl.when(rank < counts[v])
            def _(v=v, rank=rank):
                put(statics[v - 1].at[rank], table[v * capacity + rank])

    def step(rank, carry):
        slot = table[rank]
        at = slot - base
        mine = (at >= 0) & (at < count)

        @pl.when(mine)
        def _():
            put(keep.at[jnp.clip(at, 0, count - 1)], slot)

        @pl.when(jnp.logical_not(mine))
        def _():
            put(other.at[jnp.clip(slot - (count - base), 0, count - 1)], slot)

        return carry

    lax.fori_loop(0, counts[0], step, 0)
    for k, rest in enumerate(rests):
        for rank in range(low, capacity):

            @pl.when((k < found) & (rank < counts[large[k]]))
            def _(k=k, rank=rank, rest=rest):
                put(rest.at[rank - low], table[large[k] * capacity + rank])

    pltpu.make_async_copy(out, out, sem).wait()


def sizes(slots, group_count, capacity):
    low = capacity // 2
    return low, max(min(slots // (low + 1), group_count - 1), AT_ONCE)


def plan(shifts, group_count, capacity):
    low, most = sizes(shifts.shape[0], group_count, capacity)
    smem = pl.BlockSpec(memory_space=pltpu.SMEM)
    length = sum(plan_lengths(group_count, capacity, most))
    return pl.pallas_call(
        functools.partial(plan_kernel, low, capacity, group_count, most),
        out_shape=jax.ShapeDtypeStruct((length,), jnp.int32),
        in_specs=[smem],
        out_specs=smem,
        cost_estimate=pl.CostEstimate(flops=10**6, bytes_accessed=10**6, transcendentals=0),
        name="plan",
    )(shifts)


def exchange(tables, keep, other, slots, group_count, capacity):
    low, most = sizes(slots, group_count, capacity)
    branch = tables[sum(plan_lengths(group_count, capacity, most)[:-1]) :]
    block = keep.shape[1:]
    smem = pl.BlockSpec(memory_space=pltpu.SMEM)
    vmem = pl.BlockSpec(memory_space=pltpu.VMEM)
    anywhere = pl.BlockSpec(memory_space=pl.ANY)
    params = pltpu.CompilerParams(vmem_limit_bytes=VMEM_LIMIT)
    low_shape = jax.ShapeDtypeStruct((low,) + block, BF16)
    high_shape = jax.ShapeDtypeStruct((capacity - low,) + block, BF16)
    packed = pl.pallas_call(
        functools.partial(pack_kernel, low, capacity, group_count, most),
        out_shape=[low_shape] * (group_count - 1) + [high_shape] * most,
        in_specs=[smem, vmem, vmem],
        out_specs=[vmem] * (group_count - 1 + most),
        compiler_params=params,
        name="pack",
    )(tables, keep, other)
    statics = packed[: group_count - 1]
    rests = packed[group_count - 1 :]

    def move(block, v):
        return lax.ppermute(block, "pool", [(g, (g + v) % group_count) for g in range(group_count)])

    arrived = {}
    for v in range(1, group_count):
        arrived[v] = move(statics[v - 1], v)
    arrived = [arrived[v] for v in range(1, group_count)]

    def choice(subset):
        def run(*blocks):
            moved = [move(block, v) for block, v in zip(blocks, subset)]
            return tuple(moved) + blocks[len(subset) :]

        return run

    late = list(
        lax.switch(
            branch[0], [choice(subset) for subset in subsets(group_count, AT_ONCE)], *rests[:AT_ONCE]
        )
    )
    if most > AT_ONCE:

        def more(*blocks):
            singles = [choice(subset) for subset in subsets(group_count, 1)]
            return tuple(lax.switch(branch[2 + k], singles, block)[0] for k, block in enumerate(blocks))

        late += lax.cond(branch[1] > AT_ONCE, more, lambda *blocks: blocks, *rests[AT_ONCE:])
    return pl.pallas_call(
        functools.partial(unpack_kernel, low, capacity, group_count, most),
        out_shape=jax.ShapeDtypeStruct((slots,) + block, BF16),
        in_specs=[smem] + [vmem] * (2 + group_count - 1 + most),
        out_specs=anywhere,
        scratch_shapes=[pltpu.SemaphoreType.DMA],
        compiler_params=params,
        name="unpack",
    )(tables, keep, other, *arrived, *late)


def exchange_padded(half, shifts, keep, other, group_count, capacity):
    slots = shifts.shape[0]
    my_group = lax.axis_index("pool")
    blocks = jnp.where(
        half == 0, jnp.concatenate([keep, other], axis=0), jnp.concatenate([other, keep], axis=0)
    )
    slot = jnp.arange(slots, dtype=jnp.int32)
    earlier = (shifts[None, :] == shifts[:, None]) & (slot[None, :] < slot[:, None])
    rank = jnp.sum(earlier.astype(jnp.int32), axis=1)
    send_at = (my_group + shifts) % group_count * capacity + rank
    receive_at = (my_group - shifts) % group_count * capacity + rank
    place = jnp.arange(group_count * capacity, dtype=jnp.int32)
    source = jnp.sum(jnp.where(send_at[None, :] == place[:, None], slot[None, :], 0), axis=1)
    received = lax.all_to_all(
        jnp.take(blocks, source, axis=0), "pool", split_axis=0, concat_axis=0, tiled=True
    )
    return jnp.take(received, receive_at, axis=0)


def body(pair_rep, alignment, lengths, chain_breaks, shifts, *weights):
    group_count = lax.axis_size("pool")
    slot_count = pair_rep.shape[0]
    capacity = max(2, (2 * slot_count + group_count - 1) // group_count)
    half = lax.axis_index("dap").astype(jnp.int32)
    swap = [(0, 1), (1, 0)]
    alignment_proj, outer_proj = weights[:2]
    inner = alignment_proj.shape[1] // 2
    w_spread = spread_matrix(alignment.shape[1], inner)
    w_outer = (
        outer_proj.reshape(inner, inner, -1).transpose(1, 0, 2).reshape(outer_proj.shape)
    )
    other_pair = lax.ppermute(pair_rep, "dap", swap)
    own_sides, send_sides = project(lengths, alignment, alignment_proj.T, w_spread)
    tables = plan(shifts, group_count, capacity) if group_count <= 8 else None
    other_sides = lax.ppermute(send_sides, "dap", swap)
    keep, send = update(
        lengths, chain_breaks, own_sides, other_sides, pair_rep, other_pair, (w_outer,) + weights[2:]
    )
    if group_count > 8:
        other = lax.ppermute(send, "dap", swap)
        return exchange_padded(half, shifts, keep, other, group_count, capacity)
    other = lax.ppermute(send, "dap", swap)
    return exchange(tables, keep, other, slot_count, group_count, capacity)


def solution(mesh):
    step = sharded(mesh)
    return step


def sharded(mesh):
    return jax.shard_map(
        body,
        mesh=mesh,
        in_specs=(
            P(("screen", "pool"), "dap", None, None),
            P(("screen", "pool"), None, "dap", None),
            P("screen"),
            P("screen"),
            P("screen"),
        )
        + (P(),) * 9,
        out_specs=P(("screen", "pool"), "dap", None, None),
        check_vma=False,
    )
```

```python
import functools
import itertools

import jax
import jax.numpy as jnp
import numpy as np
from jax import lax
from jax.experimental import pallas as pl
from jax.experimental.pallas import tpu as pltpu
from jax.sharding import PartitionSpec as P

EPSILON = 1e-05
F32 = jnp.float32
BF16 = jnp.bfloat16
LANES = 128
AT_ONCE = 3
VMEM_LIMIT = 24 * 2**20
PROJECT_LIMIT = 64500000
WAYS = 4
PROJECT_WAYS = 6
OUTER_AFTER = 2
BLOCK = 4
OUTER_TILES = 4


def dot(left, right):
    return jnp.dot(left, right, preferred_element_type=F32)


def normalize_steps(values, scale, ones):
    width = values.shape[-1]
    values = values - jnp.sum(values, axis=-1, keepdims=True) * (1.0 / width)
    yield
    spread = dot((values * values).astype(BF16), ones[...])
    yield
    return (values * (lax.rsqrt(spread + width * EPSILON) * scale)).astype(BF16)


def interleave(streams):
    running = list(streams)
    while running:
        for stream in list(running):
            if next(stream, running) is running:
                running.remove(stream)


def lane_groups(inner):
    group = lax.broadcasted_iota(jnp.int32, (1, LANES), 1) // inner
    return [group == q for q in range(LANES // inner)]


def project_kernel(
    lengths_in,
    alignment_in,
    w_align_in,
    w_spread_in,
    own_ref,
    send_ref,
    lengths_ref,
    alignment,
    w_align,
    w_spread,
    side,
    rights,
    sems,
):
    slots, depth, rows, width = alignment.shape
    count = slots // 2
    inner = rights.shape[-1] // depth
    pieces = LANES // inner
    half = lax.axis_index("dap")
    mine, theirs = half * count, (1 - half) * count
    home = lax.axis_index("pool") * slots
    copies = [
        pltpu.make_async_copy(source, target, sems.at[n])
        for n, (source, target) in enumerate(
            ((w_align_in, w_align), (lengths_in, lengths_ref), (alignment_in, alignment), (w_spread_in, w_spread))
        )
    ]
    for copy in copies:
        copy.start()
    groups = lane_groups(inner)
    source = lax.broadcasted_iota(jnp.int32, (2 * inner, 2 * LANES), 0)
    target = lax.broadcasted_iota(jnp.int32, (2 * inner, 2 * LANES), 1)
    repeat = (source == (target // LANES) * inner + target % inner).astype(BF16)
    copies[0].wait()
    w_project = lax.dot_general(
        w_align[...], repeat, (((0,), (0,)), ((), ())), preferred_element_type=F32
    ).astype(BF16)
    residue = lax.broadcasted_iota(jnp.int32, (rows, 1), 0) + half * rows
    copies[1].wait()
    copies[2].wait()

    def one(index, start, which, way, out_ref):
        length = lengths_ref[home + start + index]
        values = alignment[start + index].astype(F32).reshape(depth * rows, width)
        values = values - jnp.sum(values, axis=-1, keepdims=True) * (1.0 / width)
        yield
        spread = jnp.sum(values * values, axis=-1, keepdims=True) * (1.0 / width)
        yield
        values = dot((values * lax.rsqrt(spread + EPSILON)).astype(BF16), w_project)
        yield
        values = values.reshape(depth, rows, 2 * LANES) * jnp.where(residue < length, 1.0, 0.0)
        side[way] = values[:, :, :LANES].reshape(depth * rows, LANES) * (1.0 / depth)
        tiles = []
        for tile in range(rows // pieces):
            piece = side[way, pl.ds(tile * pieces, depth, stride=rows), :]
            for q in range(1, pieces):
                other = side[way, pl.ds(tile * pieces + q, depth, stride=rows), :]
                piece = jnp.where(groups[q], other, piece)
            tiles.append(piece)
        out_ref[index, :depth] = jnp.concatenate(tiles, axis=1).astype(BF16)
        for tile in range(depth // pieces):
            piece = values[tile * pieces, :, LANES:]
            for q in range(1, pieces):
                piece = jnp.where(groups[q], values[tile * pieces + q, :, LANES:], piece)
            rights[which, index, :, LANES * tile : LANES * tile + LANES] = piece

    ways = side.shape[0] // 2

    def step(round_, carry):
        streams = []
        for way in range(ways):
            index = jnp.minimum(round_ * ways + way, count - 1)
            streams.append(one(index, mine, 0, 2 * way, own_ref))
            streams.append(one(index, theirs, 1, 2 * way + 1, send_ref))
        interleave(streams)
        return carry

    lax.fori_loop(0, (count + ways - 1) // ways, step, 0)
    copies[3].wait()
    flat = rights[...].reshape(slots * rows, depth * inner).astype(BF16)
    spread = dot(flat, w_spread[...]).reshape(2, count, rows, depth * inner).astype(BF16)
    parts = own_ref.shape[-1]
    for which, out_ref in enumerate((own_ref, send_ref)):
        for part in range(depth * inner // parts):
            out_ref[:, depth + part * rows : depth + part * rows + rows] = spread[
                which, :, :, part * parts : part * parts + parts
            ]


def project(lengths, alignment, w_align, w_spread):
    slots, depth, rows, _ = alignment.shape
    count = slots // 2
    inner = w_align.shape[0] // 2
    smem = pl.BlockSpec(memory_space=pltpu.SMEM)
    vmem = pl.BlockSpec(memory_space=pltpu.VMEM)
    hbm = pl.BlockSpec(memory_space=pltpu.HBM)
    out_shape = (count, 2 * depth, rows * inner)
    return pl.pallas_call(
        project_kernel,
        out_shape=(pltpu.VMEM(out_shape, BF16), jax.ShapeDtypeStruct(out_shape, BF16)),
        in_specs=[hbm, hbm, hbm, hbm],
        out_specs=(vmem, vmem),
        scratch_shapes=[
            pltpu.SMEM(lengths.shape, jnp.int32),
            pltpu.VMEM(alignment.shape, BF16),
            pltpu.VMEM(w_align.shape, BF16),
            pltpu.VMEM(w_spread.shape, BF16),
            pltpu.VMEM((2 * PROJECT_WAYS, depth * rows, LANES), F32),
            pltpu.VMEM((2, count, rows, depth * inner), F32),
            pltpu.SemaphoreType.DMA((4,)),
        ],
        compiler_params=pltpu.CompilerParams(vmem_limit_bytes=PROJECT_LIMIT),
        cost_estimate=pl.CostEstimate(flops=2 * 10**9, bytes_accessed=4 * 10**6, transcendentals=0),
        name="project",
    )(lengths, alignment, w_align, w_spread)


def update_kernel(
    lengths_ref,
    breaks_ref,
    own_sides,
    other_sides,
    pair,
    other_pair,
    w_outer,
    bias,
    out_ab,
    out_gate,
    out_proj,
    in_ab,
    in_gate,
    in_proj,
    keep_ref,
    send_ref,
    ones,
    updates_refs,
    stream_refs,
    gates_refs,
    sides_refs,
):
    count, rows, full, width = keep_ref.shape
    depth = own_sides.shape[1] // 2
    inner = own_sides.shape[2] // rows
    pieces = LANES // inner
    sets = inner // pieces
    hidden = out_proj.shape[0]
    half = lax.axis_index("dap")
    start = half * count
    home = lax.axis_index("pool") * pair.shape[0] + start
    low_is_own = half == 0
    groups = lane_groups(inner)
    zero = jnp.zeros((), BF16)
    place_j = lax.broadcasted_iota(jnp.int32, (full, 1), 0)
    ones[...] = jnp.ones_like(ones)
    unit = 0.5 * width**0.5
    pairs = full * full
    ways = updates_refs.shape[0]
    within, across = bias[0:1].astype(F32), bias[1:2].astype(F32)

    def clamp(index):
        return jnp.minimum(index, count - 1)

    def outer_update(way, step):
        own, other = own_sides[step], other_sides[step]
        low = jnp.where(low_is_own, own, other)
        high = jnp.where(low_is_own, other, own)
        right = jnp.concatenate(
            [
                jnp.concatenate(
                    [side[depth + rows * part : depth + rows * part + rows] for part in range(depth // rows)],
                    axis=1,
                )
                for side in (low, high)
            ],
            axis=0,
        )
        per = LANES // (pieces * depth)
        tiles = []
        for c2 in range(sets):
            tile = right[:, c2 // per * LANES : c2 // per * LANES + LANES]
            turn = c2 % per * pieces * depth
            tiles.append(pltpu.roll(tile, LANES - turn, 1) if turn else tile)
        right = jnp.concatenate(tiles, axis=0)
        yield
        tail = jnp.zeros((LANES - pieces * depth, 2 * LANES), BF16)
        lefts = rows // pieces
        parts = []
        for tile in range(full // pieces):
            source = low if tile < lefts else high
            at = tile % lefts * LANES
            left = source[:depth, at : at + LANES]
            turned = [left] + [pltpu.roll(left, inner * turn, 1) for turn in range(1, pieces)]
            for first_p in range(0, pieces, 2):
                column = [
                    jnp.concatenate(
                        [jnp.where(groups[q], turned[(q - p) % pieces], zero) for q in range(pieces)], axis=0
                    )
                    for p in (first_p, first_p + 1)
                ]
                stacked = jnp.concatenate([jnp.concatenate(column, axis=1), tail], axis=0)
                product = dot(right, stacked).astype(BF16)
                for k in range(2):
                    parts.append(
                        jnp.concatenate(
                            [
                                product[full * g : full * g + full, LANES * k : LANES * k + LANES]
                                for g in range(sets)
                            ],
                            axis=1,
                        )
                    )
                yield
            if (tile + 1) % OUTER_TILES == 0:
                span = len(parts) * full
                start_row = (tile + 1) * pieces * full - span
                updates_refs[way, start_row : start_row + span] = dot(
                    jnp.concatenate(parts, axis=0), w_outer[...]
                )
                parts = []
                yield

    def row_masks(length):
        column = jnp.where(place_j < length, 1.0, 0.0)
        return jnp.concatenate([jnp.where(i < length, column, 0.0) for i in range(full)], axis=0)

    def sides(values, inside, w_ab, w_gate, way, first):
        x = yield from normalize_steps(values, inside * unit, ones)
        yield
        for n in range(2):
            projected = dot(x, w_ab[:, 2 * hidden * n : 2 * hidden * n + 2 * hidden])
            sides_refs[way, first + n] = (jnp.tanh(projected[:, hidden:]) + 1.0) * projected[:, :hidden]
            yield
        gates_refs[way] = jnp.tanh(dot(x, w_gate[...])) + 1.0

    def contract(row_of, column_of):
        parts = []
        for first in range(0, full, BLOCK):
            totals = [None] * BLOCK
            for k in range(full):
                column = column_of(k)
                for i in range(BLOCK):
                    term = row_of(first + i, k) * column
                    totals[i] = term if totals[i] is None else totals[i] + term
            parts += totals
            yield
        return jnp.concatenate(parts, axis=0)

    def begin(step, way):
        stop = breaks_ref[home + step]
        head = place_j < stop
        terms = (jnp.where(head, within, across), jnp.where(head, across, within))
        chain = jnp.concatenate([jnp.where(i < stop, terms[0], terms[1]) for i in range(full)], axis=0)
        own, other = pair[start + step], other_pair[start + step]
        block = jnp.concatenate(
            [jnp.where(low_is_own, own, other), jnp.where(low_is_own, other, own)], axis=0
        )
        z1 = block.reshape(pairs, width).astype(F32) + updates_refs[way] + chain
        stream_refs[way] = z1
        yield
        yield from sides(z1, row_masks(lengths_ref[home + step]), out_ab, out_gate, way, 0)

    def middle(step, way):
        t = yield from contract(
            lambda i, k: sides_refs[way, 0, pl.ds(full * i + k, 1), :],
            lambda k: sides_refs[way, 1, pl.ds(k, full, stride=full), :],
        )
        u = yield from normalize_steps(t, unit, ones)
        yield
        z2 = stream_refs[way] + gates_refs[way] * dot(u, out_proj[...])
        z2 = z2.astype(BF16).astype(F32)
        stream_refs[way] = z2
        yield
        yield from sides(z2, row_masks(lengths_ref[home + step]), in_ab, in_gate, way, 2)

    def last(step, way):
        t = yield from contract(
            lambda i, k: sides_refs[way, 3, pl.ds(full * k + i, 1), :],
            lambda k: sides_refs[way, 2, full * k : full * k + full],
        )
        u = yield from normalize_steps(t, unit, ones)
        yield
        y3 = stream_refs[way] + gates_refs[way] * dot(u, in_proj[...])
        y3 = (y3 * row_masks(lengths_ref[home + step])).astype(BF16)
        low = y3[: rows * full].reshape(rows, full, width)
        high = y3[rows * full :].reshape(rows, full, width)
        keep_ref[step] = jnp.where(low_is_own, low, high)
        send_ref[step] = jnp.where(low_is_own, high, low)

    def whole(step, way):
        yield from begin(step, way)
        yield
        yield from middle(step, way)
        yield
        yield from last(step, way)

    def later(streams, ticks):
        for _ in range(ticks):
            yield
        for stream in streams:
            yield from stream

    def round_of(steps, ahead):
        streams = [whole(step, way) for way, step in enumerate(steps)]
        outers = [outer_update(way, step) for way, step in enumerate(ahead)]
        interleave([later(outers, OUTER_AFTER)] + streams)

    def both(round_, carry):
        base = round_ * ways
        round_of([base + way for way in range(ways)], [clamp(base + ways + way) for way in range(ways)])
        return carry

    rounds = (count + ways - 1) // ways
    interleave([outer_update(way, clamp(way)) for way in range(ways)])
    lax.fori_loop(0, rounds - 1, both, 0)
    round_of(list(range((rounds - 1) * ways, count)), [])


def update(lengths, breaks, own_sides, other_sides, pair, other_pair, weights):
    outer_proj, chain_bias, out_ab, out_gate, out_proj, in_ab, in_gate, in_proj = weights
    count = own_sides.shape[0]
    _, full, width = pair.shape[1:]
    smem = pl.BlockSpec(memory_space=pltpu.SMEM)
    vmem = pl.BlockSpec(memory_space=pltpu.VMEM)
    shape = jax.ShapeDtypeStruct((count,) + pair.shape[1:], BF16)
    pairs, hidden = full * full, out_proj.shape[0]
    return pl.pallas_call(
        update_kernel,
        out_shape=(shape, shape),
        in_specs=[smem] * 2 + [vmem] * 12,
        out_specs=(vmem, vmem),
        scratch_shapes=[
            pltpu.VMEM((width, width), BF16),
            pltpu.VMEM((WAYS, pairs, width), F32),
            pltpu.VMEM((WAYS, pairs, width), F32),
            pltpu.VMEM((WAYS, pairs, width), F32),
            pltpu.VMEM((WAYS, 4, pairs, hidden), F32),
        ],
        compiler_params=pltpu.CompilerParams(vmem_limit_bytes=VMEM_LIMIT),
        cost_estimate=pl.CostEstimate(flops=10**10, bytes_accessed=4 * 10**6, transcendentals=0),
        name="pair_update",
    )(
        lengths,
        breaks,
        own_sides,
        other_sides,
        pair,
        other_pair,
        outer_proj,
        chain_bias,
        out_ab,
        out_gate,
        out_proj,
        in_ab,
        in_gate,
        in_proj,
    )


def spread_matrix(depth, inner):
    pieces = LANES // inner
    r, c2 = np.divmod(np.arange(depth * inner), inner)
    matrix = np.zeros((depth * inner, depth * inner), np.float32)
    matrix[np.arange(depth * inner), (c2 // pieces) * pieces * depth + (c2 % pieces) * depth + r] = 1.0
    return jnp.asarray(matrix, BF16)


def build_tables(shifts_ref, table, counts, capacity):
    slots, groups = shifts_ref.shape[0], counts.shape[0]
    for v in range(groups):
        counts[v] = 0

    def step(slot, carry):
        v = shifts_ref[slot]
        rank = counts[v]
        table[v * capacity + rank] = slot
        counts[v] = rank + 1
        return carry

    lax.fori_loop(0, slots, step, 0)


def list_large(counts, large, low):
    for k in range(large.shape[0]):
        large[k] = 0
    found = jnp.int32(0)
    for v in range(1, counts.shape[0]):
        many = counts[v] > low

        @pl.when(many)
        def _(found=found, v=v):
            large[found] = v

        found = found + many.astype(jnp.int32)
    return found


def subsets(groups, most):
    return [c for n in range(most + 1) for c in itertools.combinations(range(1, groups), n)]


def split_plan(plan_ref, groups, capacity, most):
    views, start = [], 0
    for length in plan_lengths(groups, capacity, most):
        views.append(plan_ref.at[pl.ds(start, length)])
        start += length
    return views


def plan_lengths(groups, capacity, most):
    return groups * capacity, groups, most, 2 + most - AT_ONCE


def plan_kernel(low, capacity, groups, most, shifts_ref, plan_ref):
    table, counts, large, branch = split_plan(plan_ref, groups, capacity, most)
    build_tables(shifts_ref, table, counts, capacity)
    found = list_large(counts, large, low)
    taken = [large[k] for k in range(min(AT_ONCE, large.shape[0]))]
    index = jnp.int32(0)
    for n, subset in enumerate(subsets(groups, AT_ONCE)):
        same = functools.reduce(
            jnp.logical_and, [t == (subset[k] if k < len(subset) else 0) for k, t in enumerate(taken)]
        )
        index = jnp.where(same, n, index)
    branch[0] = index
    branch[1] = found
    for k in range(AT_ONCE, large.shape[0]):
        branch[2 + k - AT_ONCE] = large[k]


def pack_kernel(low, capacity, groups, most, plan_ref, keep, other, *outs):
    table, counts, large, branch = split_plan(plan_ref, groups, capacity, most)
    found = branch[1]
    statics, rests = outs[: groups - 1], outs[groups - 1 :]
    count = keep.shape[0]
    base = lax.axis_index("dap") * count

    def fetch(v, rank):
        slot = jnp.where(rank < counts[v], table[v * capacity + rank], 0)
        at = slot - base
        mine = (at >= 0) & (at < count)
        near = keep[jnp.clip(at, 0, count - 1)]
        far = other[jnp.clip(slot - (count - base), 0, count - 1)]
        return jnp.where(mine, near, far)

    for v in range(1, groups):
        for rank in range(low):
            statics[v - 1][rank] = fetch(v, rank)
    for k, rest in enumerate(rests):
        @pl.when(k < found)
        def _(k=k, rest=rest):
            v = large[k]
            for rank in range(low, capacity):
                rest[rank - low] = fetch(v, rank)


def unpack_kernel(low, capacity, groups, most, plan_ref, keep, other, *refs):
    table, counts, large, branch = split_plan(plan_ref, groups, capacity, most)
    found = branch[1]
    out, sem = refs[-2:]
    statics, rests = refs[: groups - 1], refs[groups - 1 : -2]
    count = keep.shape[0]
    base = lax.axis_index("dap") * count

    def put(source, slot):
        pltpu.make_async_copy(source, out.at[slot], sem).start()

    for v in range(1, groups):
        for rank in range(low):

            @pl.when(rank < counts[v])
            def _(v=v, rank=rank):
                put(statics[v - 1].at[rank], table[v * capacity + rank])

    def step(rank, carry):
        slot = table[rank]
        at = slot - base
        mine = (at >= 0) & (at < count)

        @pl.when(mine)
        def _():
            put(keep.at[jnp.clip(at, 0, count - 1)], slot)

        @pl.when(jnp.logical_not(mine))
        def _():
            put(other.at[jnp.clip(slot - (count - base), 0, count - 1)], slot)

        return carry

    lax.fori_loop(0, counts[0], step, 0)
    for k, rest in enumerate(rests):
        for rank in range(low, capacity):

            @pl.when((k < found) & (rank < counts[large[k]]))
            def _(k=k, rank=rank, rest=rest):
                put(rest.at[rank - low], table[large[k] * capacity + rank])

    pltpu.make_async_copy(out, out, sem).wait()


def sizes(slots, group_count, capacity):
    low = capacity // 2
    return low, max(min(slots // (low + 1), group_count - 1), AT_ONCE)


def plan(shifts, group_count, capacity):
    low, most = sizes(shifts.shape[0], group_count, capacity)
    smem = pl.BlockSpec(memory_space=pltpu.SMEM)
    length = sum(plan_lengths(group_count, capacity, most))
    return pl.pallas_call(
        functools.partial(plan_kernel, low, capacity, group_count, most),
        out_shape=jax.ShapeDtypeStruct((length,), jnp.int32),
        in_specs=[smem],
        out_specs=smem,
        cost_estimate=pl.CostEstimate(flops=10**6, bytes_accessed=10**6, transcendentals=0),
        name="plan",
    )(shifts)


def exchange(picks, tables, keep, other, slots, group_count, capacity):
    low, most = sizes(slots, group_count, capacity)
    block = keep.shape[1:]
    smem = pl.BlockSpec(memory_space=pltpu.SMEM)
    vmem = pl.BlockSpec(memory_space=pltpu.VMEM)
    anywhere = pl.BlockSpec(memory_space=pl.ANY)
    params = pltpu.CompilerParams(vmem_limit_bytes=VMEM_LIMIT)
    low_shape = jax.ShapeDtypeStruct((low,) + block, BF16)
    high_shape = jax.ShapeDtypeStruct((capacity - low,) + block, BF16)
    packed = pl.pallas_call(
        functools.partial(pack_kernel, low, capacity, group_count, most),
        out_shape=[low_shape] * (group_count - 1) + [high_shape] * most,
        in_specs=[smem, vmem, vmem],
        out_specs=[vmem] * (group_count - 1 + most),
        compiler_params=params,
        name="pack",
    )(tables, keep, other)
    statics = packed[: group_count - 1]
    rests = packed[group_count - 1 :]

    def move(block, v):
        return lax.ppermute(block, "pool", [(g, (g + v) % group_count) for g in range(group_count)])

    arrived = {}
    for v in range(1, group_count):
        arrived[v] = move(statics[v - 1], v)
    arrived = [arrived[v] for v in range(1, group_count)]

    def choice(subset):
        def run(*blocks):
            moved = [move(block, v) for block, v in zip(blocks, subset)]
            return tuple(moved) + blocks[len(subset) :]

        return run

    late = list(
        lax.switch(
            picks[0], [choice(subset) for subset in subsets(group_count, AT_ONCE)], *rests[:AT_ONCE]
        )
    )
    if most > AT_ONCE:

        def more(*blocks):
            singles = [choice(subset) for subset in subsets(group_count, 1)]
            return tuple(lax.switch(picks[2 + k], singles, block)[0] for k, block in enumerate(blocks))

        late += lax.switch(picks[1], [lambda *blocks: blocks, more], *rests[AT_ONCE:])
    return pl.pallas_call(
        functools.partial(unpack_kernel, low, capacity, group_count, most),
        out_shape=jax.ShapeDtypeStruct((slots,) + block, BF16),
        in_specs=[smem] + [vmem] * (2 + group_count - 1 + most),
        out_specs=anywhere,
        scratch_shapes=[pltpu.SemaphoreType.DMA],
        compiler_params=params,
        name="unpack",
    )(tables, keep, other, *arrived, *late)


def exchange_padded(half, shifts, keep, other, group_count, capacity):
    slots = shifts.shape[0]
    my_group = lax.axis_index("pool")
    blocks = jnp.where(
        half == 0, jnp.concatenate([keep, other], axis=0), jnp.concatenate([other, keep], axis=0)
    )
    slot = jnp.arange(slots, dtype=jnp.int32)
    earlier = (shifts[None, :] == shifts[:, None]) & (slot[None, :] < slot[:, None])
    rank = jnp.sum(earlier.astype(jnp.int32), axis=1)
    send_at = (my_group + shifts) % group_count * capacity + rank
    receive_at = (my_group - shifts) % group_count * capacity + rank
    place = jnp.arange(group_count * capacity, dtype=jnp.int32)
    source = jnp.sum(jnp.where(send_at[None, :] == place[:, None], slot[None, :], 0), axis=1)
    received = lax.all_to_all(
        jnp.take(blocks, source, axis=0), "pool", split_axis=0, concat_axis=0, tiled=True
    )
    return jnp.take(received, receive_at, axis=0)


def body(pair_rep, alignment, lengths, chain_breaks, shifts, *weights):
    group_count = lax.axis_size("pool")
    slot_count = pair_rep.shape[0]
    capacity = max(2, (2 * slot_count + group_count - 1) // group_count)
    half = lax.axis_index("dap").astype(jnp.int32)
    swap = [(0, 1), (1, 0)]
    alignment_proj, outer_proj = weights[:2]
    inner = alignment_proj.shape[1] // 2
    w_spread = spread_matrix(alignment.shape[1], inner)
    w_outer = (
        outer_proj.reshape(inner, inner, -1).transpose(1, 0, 2).reshape(outer_proj.shape)
    )
    other_pair = lax.ppermute(pair_rep, "dap", swap)
    own_sides, send_sides = project(lengths, alignment, alignment_proj.T, w_spread)
    tables = plan(shifts, group_count, capacity) if group_count <= 8 else None
    other_sides = lax.ppermute(send_sides, "dap", swap)
    keep, send = update(
        lengths, chain_breaks, own_sides, other_sides, pair_rep, other_pair, (w_outer,) + weights[2:]
    )
    if group_count > 8:
        other = lax.ppermute(send, "dap", swap)
        return exchange_padded(half, shifts, keep, other, group_count, capacity)
    other = lax.ppermute(send, "dap", swap)
    _, most = sizes(slot_count, group_count, capacity)
    choices = tables[sum(plan_lengths(group_count, capacity, most)[:-1]) :]
    picks = [choices[0], (choices[1] > AT_ONCE).astype(jnp.int32)]
    picks += [choices[2 + k] for k in range(most - AT_ONCE)]
    other, picks = lax.optimization_barrier((other, picks))
    return exchange(picks, tables, keep, other, slot_count, group_count, capacity)


def solution(mesh):
    step = sharded(mesh)
    return step


def sharded(mesh):
    return jax.shard_map(
        body,
        mesh=mesh,
        in_specs=(
            P(("screen", "pool"), "dap", None, None),
            P(("screen", "pool"), None, "dap", None),
            P("screen"),
            P("screen"),
            P("screen"),
        )
        + (P(),) * 9,
        out_specs=P(("screen", "pool"), "dap", None, None),
        check_vma=False,
    )
```

```python
import functools
import itertools

import jax
import jax.numpy as jnp
import numpy as np
from jax import lax
from jax.experimental import pallas as pl
from jax.experimental.pallas import tpu as pltpu
from jax.sharding import PartitionSpec as P

EPSILON = 1e-05
F32 = jnp.float32
BF16 = jnp.bfloat16
LANES = 128
AT_ONCE = 3
VMEM_LIMIT = 24 * 2**20
PROJECT_LIMIT = 64500000
WAYS = 4
PROJECT_WAYS = 6
OUTER_AFTER = 2
BLOCK = 4
OUTER_TILES = 4


def dot(left, right):
    return jnp.dot(left, right, preferred_element_type=F32)


def normalize_steps(values, scale, ones):
    width = values.shape[-1]
    values = values - jnp.sum(values, axis=-1, keepdims=True) * (1.0 / width)
    yield
    spread = dot((values * values).astype(BF16), ones[...])
    yield
    return (values * (lax.rsqrt(spread + width * EPSILON) * scale)).astype(BF16)


def interleave(streams):
    running = list(streams)
    while running:
        for stream in list(running):
            if next(stream, running) is running:
                running.remove(stream)


def lane_groups(inner):
    group = lax.broadcasted_iota(jnp.int32, (1, LANES), 1) // inner
    return [group == q for q in range(LANES // inner)]


def project_kernel(
    lengths_in,
    alignment_in,
    w_align_in,
    w_spread_in,
    own_ref,
    send_ref,
    lengths_ref,
    alignment,
    w_align,
    w_spread,
    side,
    rights,
    sems,
):
    slots, depth, rows, width = alignment.shape
    count = slots // 2
    inner = rights.shape[-1] // depth
    pieces = LANES // inner
    half = lax.axis_index("dap")
    mine, theirs = half * count, (1 - half) * count
    home = lax.axis_index("pool") * slots
    ways = side.shape[0] // 2
    pieces_in = [
        (alignment_in.at[pl.ds(start + first, size)], alignment.at[pl.ds(start + first, size)])
        for first, size in ((0, ways), (ways, count - ways))
        for start in (mine, theirs)
        if size > 0
    ]
    copies = [
        pltpu.make_async_copy(source, target, sems.at[n])
        for n, (source, target) in enumerate(
            [(w_align_in, w_align), (lengths_in, lengths_ref)] + pieces_in + [(w_spread_in, w_spread)]
        )
    ]
    for copy in copies:
        copy.start()
    groups = lane_groups(inner)
    source = lax.broadcasted_iota(jnp.int32, (2 * inner, 2 * LANES), 0)
    target = lax.broadcasted_iota(jnp.int32, (2 * inner, 2 * LANES), 1)
    repeat = (source == (target // LANES) * inner + target % inner).astype(BF16)
    copies[0].wait()
    w_project = lax.dot_general(
        w_align[...], repeat, (((0,), (0,)), ((), ())), preferred_element_type=F32
    ).astype(BF16)
    residue = lax.broadcasted_iota(jnp.int32, (rows, 1), 0) + half * rows
    for copy in copies[1:4]:
        copy.wait()

    def one(index, start, which, way, out_ref):
        length = lengths_ref[home + start + index]
        values = alignment[start + index].astype(F32).reshape(depth * rows, width)
        values = values - jnp.sum(values, axis=-1, keepdims=True) * (1.0 / width)
        yield
        spread = jnp.sum(values * values, axis=-1, keepdims=True) * (1.0 / width)
        yield
        values = dot((values * lax.rsqrt(spread + EPSILON)).astype(BF16), w_project)
        yield
        values = values.reshape(depth, rows, 2 * LANES) * jnp.where(residue < length, 1.0, 0.0)
        side[way, : depth * rows] = values[:, :, :LANES].reshape(depth * rows, LANES) * (1.0 / depth)
        tiles = []
        for tile in range(rows // pieces):
            piece = side[way, pl.ds(tile * pieces, depth, stride=rows), :]
            for q in range(1, pieces):
                other = side[way, pl.ds(tile * pieces + q, depth, stride=rows), :]
                piece = jnp.where(groups[q], other, piece)
            tiles.append(piece)
        out_ref[index, :depth] = jnp.concatenate(tiles, axis=1).astype(BF16)
        for tile in range(depth // pieces):
            piece = values[tile * pieces, :, LANES:]
            for q in range(1, pieces):
                piece = jnp.where(groups[q], values[tile * pieces + q, :, LANES:], piece)
            rights[which, index, :, LANES * tile : LANES * tile + LANES] = piece

    def step(round_, carry):
        @pl.when(round_ == 1)
        def _():
            for copy in copies[4:-1]:
                copy.wait()

        streams = []
        for way in range(ways):
            index = jnp.minimum(round_ * ways + way, count - 1)
            streams.append(one(index, mine, 0, 2 * way, own_ref))
            streams.append(one(index, theirs, 1, 2 * way + 1, send_ref))
        interleave(streams)
        return carry

    lax.fori_loop(0, (count + ways - 1) // ways, step, 0)
    copies[-1].wait()
    flat = rights[...].reshape(slots * rows, depth * inner).astype(BF16)
    spread = dot(flat, w_spread[...]).reshape(2, count, rows, depth * inner).astype(BF16)
    parts = own_ref.shape[-1]
    for which, out_ref in enumerate((own_ref, send_ref)):
        for part in range(depth * inner // parts):
            out_ref[:, depth + part * rows : depth + part * rows + rows] = spread[
                which, :, :, part * parts : part * parts + parts
            ]


def project(lengths, alignment, w_align, w_spread):
    slots, depth, rows, _ = alignment.shape
    count = slots // 2
    inner = w_align.shape[0] // 2
    smem = pl.BlockSpec(memory_space=pltpu.SMEM)
    vmem = pl.BlockSpec(memory_space=pltpu.VMEM)
    hbm = pl.BlockSpec(memory_space=pltpu.HBM)
    out_shape = (count, 2 * depth, rows * inner)
    return pl.pallas_call(
        project_kernel,
        out_shape=(pltpu.VMEM(out_shape, BF16), jax.ShapeDtypeStruct(out_shape, BF16)),
        in_specs=[hbm, hbm, hbm, hbm],
        out_specs=(vmem, vmem),
        scratch_shapes=[
            pltpu.SMEM(lengths.shape, jnp.int32),
            pltpu.VMEM(alignment.shape, BF16),
            pltpu.VMEM(w_align.shape, BF16),
            pltpu.VMEM(w_spread.shape, BF16),
            pltpu.VMEM((2 * PROJECT_WAYS, depth * rows + rows, LANES), F32),
            pltpu.VMEM((2, count, rows, depth * inner), F32),
            pltpu.SemaphoreType.DMA((7,)),
        ],
        compiler_params=pltpu.CompilerParams(vmem_limit_bytes=PROJECT_LIMIT),
        cost_estimate=pl.CostEstimate(flops=2 * 10**9, bytes_accessed=4 * 10**6, transcendentals=0),
        name="project",
    )(lengths, alignment, w_align, w_spread)


def update_kernel(
    lengths_ref,
    breaks_ref,
    own_sides,
    other_sides,
    pair,
    other_pair,
    w_outer,
    bias,
    out_ab,
    out_gate,
    out_proj,
    in_ab,
    in_gate,
    in_proj,
    keep_ref,
    send_ref,
    ones,
    updates_refs,
    stream_refs,
    gates_refs,
    sides_refs,
):
    count, rows, full, width = keep_ref.shape
    depth = own_sides.shape[1] // 2
    inner = own_sides.shape[2] // rows
    pieces = LANES // inner
    sets = inner // pieces
    hidden = out_proj.shape[0]
    half = lax.axis_index("dap")
    start = half * count
    home = lax.axis_index("pool") * pair.shape[0] + start
    low_is_own = half == 0
    groups = lane_groups(inner)
    zero = jnp.zeros((), BF16)
    place_j = lax.broadcasted_iota(jnp.int32, (full, 1), 0)
    ones[...] = jnp.ones_like(ones)
    unit = 0.5 * width**0.5
    pairs = full * full
    ways = updates_refs.shape[0]
    within, across = bias[0:1].astype(F32), bias[1:2].astype(F32)

    def clamp(index):
        return jnp.minimum(index, count - 1)

    def outer_update(way, step):
        own, other = own_sides[step], other_sides[step]
        low = jnp.where(low_is_own, own, other)
        high = jnp.where(low_is_own, other, own)
        right = jnp.concatenate(
            [
                jnp.concatenate(
                    [side[depth + rows * part : depth + rows * part + rows] for part in range(depth // rows)],
                    axis=1,
                )
                for side in (low, high)
            ],
            axis=0,
        )
        per = LANES // (pieces * depth)
        tiles = []
        for c2 in range(sets):
            tile = right[:, c2 // per * LANES : c2 // per * LANES + LANES]
            turn = c2 % per * pieces * depth
            tiles.append(pltpu.roll(tile, LANES - turn, 1) if turn else tile)
        right = jnp.concatenate(tiles, axis=0)
        yield
        tail = jnp.zeros((LANES - pieces * depth, 2 * LANES), BF16)
        lefts = rows // pieces
        parts = []
        for tile in range(full // pieces):
            source = low if tile < lefts else high
            at = tile % lefts * LANES
            left = source[:depth, at : at + LANES]
            turned = [left] + [pltpu.roll(left, inner * turn, 1) for turn in range(1, pieces)]
            for first_p in range(0, pieces, 2):
                column = [
                    jnp.concatenate(
                        [jnp.where(groups[q], turned[(q - p) % pieces], zero) for q in range(pieces)], axis=0
                    )
                    for p in (first_p, first_p + 1)
                ]
                stacked = jnp.concatenate([jnp.concatenate(column, axis=1), tail], axis=0)
                product = dot(right, stacked).astype(BF16)
                for k in range(2):
                    parts.append(
                        jnp.concatenate(
                            [
                                product[full * g : full * g + full, LANES * k : LANES * k + LANES]
                                for g in range(sets)
                            ],
                            axis=1,
                        )
                    )
                yield
            if (tile + 1) % OUTER_TILES == 0:
                span = len(parts) * full
                start_row = (tile + 1) * pieces * full - span
                updates_refs[way, start_row : start_row + span] = dot(
                    jnp.concatenate(parts, axis=0), w_outer[...]
                )
                parts = []
                yield

    def row_masks(length):
        column = jnp.where(place_j < length, 1.0, 0.0)
        return jnp.concatenate([jnp.where(i < length, column, 0.0) for i in range(full)], axis=0)

    def sides(values, inside, w_ab, w_gate, way, first):
        x = yield from normalize_steps(values, inside * unit, ones)
        yield
        for n in range(2):
            projected = dot(x, w_ab[:, 2 * hidden * n : 2 * hidden * n + 2 * hidden])
            sides_refs[way, first + n, :pairs] = (jnp.tanh(projected[:, hidden:]) + 1.0) * projected[:, :hidden]
            yield
        gates_refs[way] = jnp.tanh(dot(x, w_gate[...])) + 1.0

    def contract(row_of, column_of):
        parts = []
        for first in range(0, full, BLOCK):
            totals = [None] * BLOCK
            for k in range(full):
                column = column_of(k)
                for i in range(BLOCK):
                    term = row_of(first + i, k) * column
                    totals[i] = term if totals[i] is None else totals[i] + term
            parts += totals
            yield
        return jnp.concatenate(parts, axis=0)

    def begin(step, way):
        stop = breaks_ref[home + step]
        head = place_j < stop
        terms = (jnp.where(head, within, across), jnp.where(head, across, within))
        chain = jnp.concatenate([jnp.where(i < stop, terms[0], terms[1]) for i in range(full)], axis=0)
        own, other = pair[start + step], other_pair[start + step]
        block = jnp.concatenate(
            [jnp.where(low_is_own, own, other), jnp.where(low_is_own, other, own)], axis=0
        )
        z1 = block.reshape(pairs, width).astype(F32) + updates_refs[way] + chain
        stream_refs[way] = z1
        yield
        yield from sides(z1, row_masks(lengths_ref[home + step]), out_ab, out_gate, way, 0)

    def middle(step, way):
        t = yield from contract(
            lambda i, k: sides_refs[way, 0, pl.ds(full * i + k, 1), :],
            lambda k: sides_refs[way, 1, pl.ds(k, full, stride=full), :],
        )
        u = yield from normalize_steps(t, unit, ones)
        yield
        z2 = stream_refs[way] + gates_refs[way] * dot(u, out_proj[...])
        z2 = z2.astype(BF16).astype(F32)
        stream_refs[way] = z2
        yield
        yield from sides(z2, row_masks(lengths_ref[home + step]), in_ab, in_gate, way, 2)

    def last(step, way):
        t = yield from contract(
            lambda i, k: sides_refs[way, 3, pl.ds(full * k + i, 1), :],
            lambda k: sides_refs[way, 2, full * k : full * k + full],
        )
        u = yield from normalize_steps(t, unit, ones)
        yield
        y3 = stream_refs[way] + gates_refs[way] * dot(u, in_proj[...])
        y3 = (y3 * row_masks(lengths_ref[home + step])).astype(BF16)
        low = y3[: rows * full].reshape(rows, full, width)
        high = y3[rows * full :].reshape(rows, full, width)
        keep_ref[step] = jnp.where(low_is_own, low, high)
        send_ref[step] = jnp.where(low_is_own, high, low)

    def whole(step, way):
        yield from begin(step, way)
        yield
        yield from middle(step, way)
        yield
        yield from last(step, way)

    def later(streams, ticks):
        for _ in range(ticks):
            yield
        for stream in streams:
            yield from stream

    def round_of(steps, ahead):
        streams = [whole(step, way) for way, step in enumerate(steps)]
        outers = [outer_update(way, step) for way, step in enumerate(ahead)]
        interleave([later(outers, OUTER_AFTER)] + streams)

    def both(round_, carry):
        base = round_ * ways
        round_of([base + way for way in range(ways)], [clamp(base + ways + way) for way in range(ways)])
        return carry

    rounds = (count + ways - 1) // ways
    interleave([outer_update(way, clamp(way)) for way in range(ways)])
    lax.fori_loop(0, rounds - 1, both, 0)
    round_of(list(range((rounds - 1) * ways, count)), [])


def update(lengths, breaks, own_sides, other_sides, pair, other_pair, weights):
    outer_proj, chain_bias, out_ab, out_gate, out_proj, in_ab, in_gate, in_proj = weights
    count = own_sides.shape[0]
    _, full, width = pair.shape[1:]
    smem = pl.BlockSpec(memory_space=pltpu.SMEM)
    vmem = pl.BlockSpec(memory_space=pltpu.VMEM)
    shape = jax.ShapeDtypeStruct((count,) + pair.shape[1:], BF16)
    pairs, hidden = full * full, out_proj.shape[0]
    return pl.pallas_call(
        update_kernel,
        out_shape=(shape, shape),
        in_specs=[smem] * 2 + [vmem] * 12,
        out_specs=(vmem, vmem),
        scratch_shapes=[
            pltpu.VMEM((width, width), BF16),
            pltpu.VMEM((WAYS, pairs, width), F32),
            pltpu.VMEM((WAYS, pairs, width), F32),
            pltpu.VMEM((WAYS, pairs, width), F32),
            pltpu.VMEM((WAYS, 4, pairs + full, hidden), F32),
        ],
        compiler_params=pltpu.CompilerParams(vmem_limit_bytes=VMEM_LIMIT),
        cost_estimate=pl.CostEstimate(flops=10**10, bytes_accessed=4 * 10**6, transcendentals=0),
        name="pair_update",
    )(
        lengths,
        breaks,
        own_sides,
        other_sides,
        pair,
        other_pair,
        outer_proj,
        chain_bias,
        out_ab,
        out_gate,
        out_proj,
        in_ab,
        in_gate,
        in_proj,
    )


def spread_matrix(depth, inner):
    pieces = LANES // inner
    r, c2 = np.divmod(np.arange(depth * inner), inner)
    matrix = np.zeros((depth * inner, depth * inner), np.float32)
    matrix[np.arange(depth * inner), (c2 // pieces) * pieces * depth + (c2 % pieces) * depth + r] = 1.0
    return jnp.asarray(matrix, BF16)


def build_tables(shifts_ref, table, counts, capacity):
    slots, groups = shifts_ref.shape[0], counts.shape[0]
    for v in range(groups):
        counts[v] = 0

    def step(slot, carry):
        v = shifts_ref[slot]
        rank = counts[v]
        table[v * capacity + rank] = slot
        counts[v] = rank + 1
        return carry

    lax.fori_loop(0, slots, step, 0)


def list_large(counts, large, low):
    for k in range(large.shape[0]):
        large[k] = 0
    found = jnp.int32(0)
    for v in range(1, counts.shape[0]):
        many = counts[v] > low

        @pl.when(many)
        def _(found=found, v=v):
            large[found] = v

        found = found + many.astype(jnp.int32)
    return found


def subsets(groups, most):
    return [c for n in range(most + 1) for c in itertools.combinations(range(1, groups), n)]


def split_plan(plan_ref, groups, capacity, most):
    views, start = [], 0
    for length in plan_lengths(groups, capacity, most):
        views.append(plan_ref.at[pl.ds(start, length)])
        start += length
    return views


def plan_lengths(groups, capacity, most):
    return groups * capacity, groups, most, 2 + most - AT_ONCE


def plan_kernel(low, capacity, groups, most, shifts_ref, plan_ref):
    table, counts, large, branch = split_plan(plan_ref, groups, capacity, most)
    build_tables(shifts_ref, table, counts, capacity)
    found = list_large(counts, large, low)
    taken = [large[k] for k in range(min(AT_ONCE, large.shape[0]))]
    index = jnp.int32(0)
    for n, subset in enumerate(subsets(groups, AT_ONCE)):
        same = functools.reduce(
            jnp.logical_and, [t == (subset[k] if k < len(subset) else 0) for k, t in enumerate(taken)]
        )
        index = jnp.where(same, n, index)
    branch[0] = index
    branch[1] = found
    for k in range(AT_ONCE, large.shape[0]):
        branch[2 + k - AT_ONCE] = large[k]


def pack_kernel(low, capacity, groups, most, plan_ref, keep, other, *outs):
    table, counts, large, branch = split_plan(plan_ref, groups, capacity, most)
    found = branch[1]
    statics, rests = outs[: groups - 1], outs[groups - 1 :]
    count = keep.shape[0]
    base = lax.axis_index("dap") * count

    def fetch(v, rank):
        slot = jnp.where(rank < counts[v], table[v * capacity + rank], 0)
        at = slot - base
        mine = (at >= 0) & (at < count)
        near = keep[jnp.clip(at, 0, count - 1)]
        far = other[jnp.clip(slot - (count - base), 0, count - 1)]
        return jnp.where(mine, near, far)

    for v in range(1, groups):
        for rank in range(low):
            statics[v - 1][rank] = fetch(v, rank)
    for k, rest in enumerate(rests):
        @pl.when(k < found)
        def _(k=k, rest=rest):
            v = large[k]
            for rank in range(low, capacity):
                rest[rank - low] = fetch(v, rank)


def unpack_kernel(low, capacity, groups, most, plan_ref, keep, other, *refs):
    table, counts, large, branch = split_plan(plan_ref, groups, capacity, most)
    found = branch[1]
    out, sem = refs[-2:]
    statics, rests = refs[: groups - 1], refs[groups - 1 : -2]
    count = keep.shape[0]
    base = lax.axis_index("dap") * count

    def put(source, slot):
        pltpu.make_async_copy(source, out.at[slot], sem).start()

    for v in range(1, groups):
        for rank in range(low):

            @pl.when(rank < counts[v])
            def _(v=v, rank=rank):
                put(statics[v - 1].at[rank], table[v * capacity + rank])

    def step(rank, carry):
        slot = table[rank]
        at = slot - base
        mine = (at >= 0) & (at < count)

        @pl.when(mine)
        def _():
            put(keep.at[jnp.clip(at, 0, count - 1)], slot)

        @pl.when(jnp.logical_not(mine))
        def _():
            put(other.at[jnp.clip(slot - (count - base), 0, count - 1)], slot)

        return carry

    lax.fori_loop(0, counts[0], step, 0)
    for k, rest in enumerate(rests):
        for rank in range(low, capacity):

            @pl.when((k < found) & (rank < counts[large[k]]))
            def _(k=k, rank=rank, rest=rest):
                put(rest.at[rank - low], table[large[k] * capacity + rank])

    pltpu.make_async_copy(out, out, sem).wait()


def sizes(slots, group_count, capacity):
    low = capacity // 2
    return low, max(min(slots // (low + 1), group_count - 1), AT_ONCE)


def plan(shifts, group_count, capacity):
    low, most = sizes(shifts.shape[0], group_count, capacity)
    smem = pl.BlockSpec(memory_space=pltpu.SMEM)
    length = sum(plan_lengths(group_count, capacity, most))
    return pl.pallas_call(
        functools.partial(plan_kernel, low, capacity, group_count, most),
        out_shape=jax.ShapeDtypeStruct((length,), jnp.int32),
        in_specs=[smem],
        out_specs=smem,
        cost_estimate=pl.CostEstimate(flops=10**6, bytes_accessed=10**6, transcendentals=0),
        name="plan",
    )(shifts)


def exchange(picks, tables, keep, other, slots, group_count, capacity):
    low, most = sizes(slots, group_count, capacity)
    block = keep.shape[1:]
    smem = pl.BlockSpec(memory_space=pltpu.SMEM)
    vmem = pl.BlockSpec(memory_space=pltpu.VMEM)
    anywhere = pl.BlockSpec(memory_space=pl.ANY)
    params = pltpu.CompilerParams(vmem_limit_bytes=VMEM_LIMIT)
    low_shape = jax.ShapeDtypeStruct((low,) + block, BF16)
    high_shape = jax.ShapeDtypeStruct((capacity - low,) + block, BF16)
    packed = pl.pallas_call(
        functools.partial(pack_kernel, low, capacity, group_count, most),
        out_shape=[low_shape] * (group_count - 1) + [high_shape] * most,
        in_specs=[smem, vmem, vmem],
        out_specs=[vmem] * (group_count - 1 + most),
        compiler_params=params,
        name="pack",
    )(tables, keep, other)
    statics = packed[: group_count - 1]
    rests = packed[group_count - 1 :]

    def move(block, v):
        return lax.ppermute(block, "pool", [(g, (g + v) % group_count) for g in range(group_count)])

    arrived = {}
    for v in range(1, group_count):
        arrived[v] = move(statics[v - 1], v)
    arrived = [arrived[v] for v in range(1, group_count)]

    def choice(subset):
        def run(*blocks):
            moved = [move(block, v) for block, v in zip(blocks, subset)]
            return tuple(moved) + blocks[len(subset) :]

        return run

    late = list(
        lax.switch(
            picks[0], [choice(subset) for subset in subsets(group_count, AT_ONCE)], *rests[:AT_ONCE]
        )
    )
    if most > AT_ONCE:

        def more(*blocks):
            singles = [choice(subset) for subset in subsets(group_count, 1)]
            return tuple(lax.switch(picks[2 + k], singles, block)[0] for k, block in enumerate(blocks))

        late += lax.switch(picks[1], [lambda *blocks: blocks, more], *rests[AT_ONCE:])
    return pl.pallas_call(
        functools.partial(unpack_kernel, low, capacity, group_count, most),
        out_shape=jax.ShapeDtypeStruct((slots,) + block, BF16),
        in_specs=[smem] + [vmem] * (2 + group_count - 1 + most),
        out_specs=anywhere,
        scratch_shapes=[pltpu.SemaphoreType.DMA],
        compiler_params=params,
        name="unpack",
    )(tables, keep, other, *arrived, *late)


def exchange_padded(half, shifts, keep, other, group_count, capacity):
    slots = shifts.shape[0]
    my_group = lax.axis_index("pool")
    blocks = jnp.where(
        half == 0, jnp.concatenate([keep, other], axis=0), jnp.concatenate([other, keep], axis=0)
    )
    slot = jnp.arange(slots, dtype=jnp.int32)
    earlier = (shifts[None, :] == shifts[:, None]) & (slot[None, :] < slot[:, None])
    rank = jnp.sum(earlier.astype(jnp.int32), axis=1)
    send_at = (my_group + shifts) % group_count * capacity + rank
    receive_at = (my_group - shifts) % group_count * capacity + rank
    place = jnp.arange(group_count * capacity, dtype=jnp.int32)
    source = jnp.sum(jnp.where(send_at[None, :] == place[:, None], slot[None, :], 0), axis=1)
    received = lax.all_to_all(
        jnp.take(blocks, source, axis=0), "pool", split_axis=0, concat_axis=0, tiled=True
    )
    return jnp.take(received, receive_at, axis=0)


def body(pair_rep, alignment, lengths, chain_breaks, shifts, *weights):
    group_count = lax.axis_size("pool")
    slot_count = pair_rep.shape[0]
    capacity = max(2, (2 * slot_count + group_count - 1) // group_count)
    half = lax.axis_index("dap").astype(jnp.int32)
    swap = [(0, 1), (1, 0)]
    alignment_proj, outer_proj = weights[:2]
    inner = alignment_proj.shape[1] // 2
    w_spread = spread_matrix(alignment.shape[1], inner)
    w_outer = (
        outer_proj.reshape(inner, inner, -1).transpose(1, 0, 2).reshape(outer_proj.shape)
    )
    other_pair = lax.ppermute(pair_rep, "dap", swap)
    own_sides, send_sides = project(lengths, alignment, alignment_proj.T, w_spread)
    tables = plan(shifts, group_count, capacity) if group_count <= 8 else None
    other_sides = lax.ppermute(send_sides, "dap", swap)
    keep, send = update(
        lengths, chain_breaks, own_sides, other_sides, pair_rep, other_pair, (w_outer,) + weights[2:]
    )
    if group_count > 8:
        other = lax.ppermute(send, "dap", swap)
        return exchange_padded(half, shifts, keep, other, group_count, capacity)
    other = lax.ppermute(send, "dap", swap)
    _, most = sizes(slot_count, group_count, capacity)
    choices = tables[sum(plan_lengths(group_count, capacity, most)[:-1]) :]
    picks = [choices[0], (choices[1] > AT_ONCE).astype(jnp.int32)]
    picks += [choices[2 + k] for k in range(most - AT_ONCE)]
    other, picks = lax.optimization_barrier((other, picks))
    return exchange(picks, tables, keep, other, slot_count, group_count, capacity)


def solution(mesh):
    step = sharded(mesh)
    return step


def sharded(mesh):
    return jax.shard_map(
        body,
        mesh=mesh,
        in_specs=(
            P(("screen", "pool"), "dap", None, None),
            P(("screen", "pool"), None, "dap", None),
            P("screen"),
            P("screen"),
            P("screen"),
        )
        + (P(),) * 9,
        out_specs=P(("screen", "pool"), "dap", None, None),
        check_vma=False,
    )
```
